256 devices in a mesh: head: 4 (over y), ctx: 64 (over x, z, core).
Axes of the slice: x: 4, y: 4, z: 8, core: 2. Of those that a mesh axis runs over, the one named last changes fastest.
Arguments:
- ssm_x: float32 [16384, 2048], P('ctx', 'head'), may hold values from -18 to 18
- ssm_z: float32 [16384, 2048], P('ctx', 'head'), may hold values from -6 to 6
- ssm_b: float32 [16384, 256], P('ctx'), may hold values from -6 to 6
- ssm_c: float32 [16384, 256], P('ctx'), may hold values from -6 to 6
- step_sizes: float32 [16384, 32], P('ctx', 'head'), may hold values from 0.2 to 9830.4
- a_log: float32 [32], P('head'), may hold values from -16 to -3
- conv_x: float32 [4, 2048], P(None, 'head'), may hold values from -3 to 3
- conv_b: float32 [4, 256], replicated, may hold values from -3 to 3
- conv_c: float32 [4, 256], replicated, may hold values from -3 to 3
- norm_gain: float32 [2048], P('head'), may hold values from 0.1 to 1.9
- queries: float32 [16384, 1024], P('ctx', 'head'), may hold values from -6 to 6
- keys: float32 [16384, 128], P('ctx'), may hold values from -6 to 6
- values: float32 [16384, 128], P('ctx'), may hold values from -6 to 6
Outputs:
- mixer_out: float32 [16384, 2048], P('ctx', 'head')
- attention_out: float32 [16384, 1024], P('ctx', 'head')
The draws below stay inside these ranges and needn't reach their ends.
All inputs are finite; a program needn't handle non-finite values.
Results may differ from the reference program's by a relative error of at most 0.0003.
Values sent between devices are 32-bit elements; how exact they have to be, the bound alone decides.
A program may use at most 128 MiB of HBM per device.

```python
import math
import jax
import jax.numpy as jnp
from jax import lax

P_SIZE = 64
N = 256
E = 128
KCONV = 4
QHEADS = 8
SSM_HEADS = 32
TOK_DEV = 256
SEQUENCE_TOKENS = 16384


def head_kinds(key):
    marks = jax.random.uniform(jax.random.fold_in(key, 31), (SSM_HEADS,))
    return marks < 0.5


def draw_a_log(key, part):
    fast_heads = head_kinds(key)
    spread = jax.random.uniform(jax.random.fold_in(key, 32), (SSM_HEADS,))
    slow_rate = (0.3 + 0.5 * spread) / SEQUENCE_TOKENS
    fast_rate = jnp.exp(math.log(1.0 / 50.0) + spread * math.log(50.0 / 30.0))
    return jnp.log(jnp.where(fast_heads, fast_rate, slow_rate)).astype(jnp.float32)


def draw_step_sizes(key, part):
    rough = jax.random.uniform(jax.random.fold_in(key, 41), (SEQUENCE_TOKENS, SSM_HEADS), minval=0.5, maxval=1.5)
    level = jnp.exp(jax.random.uniform(jax.random.fold_in(key, 42), (SEQUENCE_TOKENS // TOK_DEV, 1, 1), minval=-0.7, maxval=0.7))
    advanced_state = (rough.reshape(SEQUENCE_TOKENS // TOK_DEV, TOK_DEV, SSM_HEADS) * level).reshape(SEQUENCE_TOKENS, SSM_HEADS)
    token_groups = jax.random.randint(jax.random.fold_in(key, 43), (3,), 0, SEQUENCE_TOKENS)
    advanced_state = advanced_state.at[token_groups].set(0.6 * SEQUENCE_TOKENS)
    return advanced_state.astype(jnp.float32)


def draw_ssm_x(key, part):
    columns = SSM_HEADS * P_SIZE
    rising = jnp.exp(math.log(3.0) * jnp.arange(columns, dtype=jnp.float32) / columns)
    inner = jax.random.fold_in(key, 71)
    entries = jnp.clip(jax.random.normal(inner, (SEQUENCE_TOKENS, columns)), -6.0, 6.0)
    return (entries * rising[None, :]).astype(jnp.float32)


def draw_queries(key, part):
    inner = jax.random.fold_in(key, 61)
    entries = jnp.clip(jax.random.normal(inner, (SEQUENCE_TOKENS, QHEADS * E)), -6.0, 6.0)
    return entries.astype(jnp.float32)


def draw_keys(key, part):
    inner = jax.random.fold_in(key, 62)
    entries = jnp.clip(jax.random.normal(inner, (SEQUENCE_TOKENS, E)), -6.0, 6.0)
    return entries.astype(jnp.float32)


def block_levels(stream_key, shape, cuts, smallest, largest):
    def one(dim, blocks):
        steps = jax.random.uniform(jax.random.fold_in(jax.random.fold_in(stream_key, 6), dim), (blocks,), jnp.float32, smallest / len(cuts), largest / len(cuts))
        return jnp.repeat(jnp.exp(steps), shape[dim] // blocks).reshape((-1,) + (1,) * (len(shape) - dim - 1))

    factor_of = one(*cuts[0])
    for cut in cuts[1:]:
        factor_of = factor_of * one(*cut)
    return factor_of


def gaussian(stream_key, extent, scale, reach, split=(), kind=jnp.bfloat16):
    result = scale * jax.random.normal(stream_key, extent, jnp.float32)
    if split:
        result = result * block_levels(stream_key, extent, split, -0.22, 0.18)
    return jnp.clip(result, -reach, reach).astype(kind)


def setup_inputs(seed: int = 0) -> dict:
    arg_keys = jax.random.split(jax.random.key(seed), 14)
    ssm_x = draw_ssm_x(jax.random.fold_in(arg_keys[13], 71), 0)
    ssm_z = gaussian(arg_keys[1], (SEQUENCE_TOKENS, SSM_HEADS * P_SIZE), 1.0, 6.0, ((0, 64), (1, 4)), jnp.float32)
    ssm_b = gaussian(arg_keys[2], (SEQUENCE_TOKENS, N), 1.0, 6.0, ((0, 64),), jnp.float32)
    ssm_c = gaussian(arg_keys[3], (SEQUENCE_TOKENS, N), 1.0, 6.0, ((0, 64),), jnp.float32)
    step_sizes = draw_step_sizes(jax.random.fold_in(arg_keys[13], 71), 0)
    a_log = draw_a_log(jax.random.fold_in(arg_keys[13], 71), 0)
    conv_x = gaussian(arg_keys[6], (KCONV, SSM_HEADS * P_SIZE), KCONV ** -0.5, 3.0, ((1, 4),), jnp.float32)
    conv_b = gaussian(arg_keys[7], (KCONV, N), KCONV ** -0.5, 3.0, (), jnp.float32)
    conv_c = gaussian(arg_keys[8], (KCONV, N), KCONV ** -0.5, 3.0, (), jnp.float32)
    norm_gain = jnp.clip(1.0 + 0.18 * jax.random.normal(arg_keys[9], (SSM_HEADS * P_SIZE,), jnp.float32), 0.1, 1.9)
    queries = draw_queries(jax.random.fold_in(arg_keys[13], 71), 0)
    keys = draw_keys(jax.random.fold_in(arg_keys[13], 71), 0)
    values = gaussian(arg_keys[12], (SEQUENCE_TOKENS, E), 1.0, 6.0, ((0, 64),), jnp.float32)
    return dict(ssm_x=ssm_x, ssm_z=ssm_z, ssm_b=ssm_b, ssm_c=ssm_c, step_sizes=step_sizes, a_log=a_log, conv_x=conv_x, conv_b=conv_b, conv_c=conv_c, norm_gain=norm_gain, queries=queries, keys=keys, values=values)


HIGHEST = lax.Precision.HIGHEST

def causal_conv(signal, weights):
    rim_width = weights.shape[0] - 1
    padded = jnp.concatenate([jnp.zeros((rim_width, signal.shape[1]), jnp.float32), signal], axis=0)
    summed = jnp.zeros_like(signal)
    for offset in range(rim_width + 1):
        summed = summed + weights[offset] * padded[offset:offset + signal.shape[0]]
    return summed

def ssd_block(state, block_item):
    block_x, block_b, block_c, block_log, block_dt = block_item
    block_rows = block_x.shape[0]
    causal_mask = jnp.tril(jnp.ones((block_rows, block_rows), dtype=bool))
    running = jnp.cumsum(block_log, axis=0)
    spread = running[:, None, :] - running[None, :, :]
    decays = jnp.where(causal_mask[:, :, None], jnp.exp(jnp.minimum(spread, 0.0)), 0.0)
    intersections = jnp.dot(block_c, block_b.T, precision=HIGHEST)
    mixing = intersections[:, :, None] * decays * block_dt[None, :, :]
    inside = jnp.einsum('tsh,shp->thp', mixing, block_x, precision=HIGHEST)
    carried = jnp.exp(running)[:, :, None] * jnp.einsum('tn,hpn->thp', block_c, state, precision=HIGHEST)
    towards = jnp.exp(running[-1][None, :] - running) * block_dt
    update = jnp.einsum('sh,shp,sn->hpn', towards, block_x, block_b, precision=HIGHEST)
    new_state = jnp.exp(running[-1])[:, None, None] * state + update
    return (new_state, inside + carried)

def mixer(ssm_x, ssm_z, ssm_b, ssm_c, step_sizes, a_log, conv_x, conv_b, conv_c, norm_gain):
    blocks = SEQUENCE_TOKENS // TOK_DEV
    layer_input_rows = jax.nn.silu(causal_conv(ssm_x, conv_x)).reshape(blocks, TOK_DEV, SSM_HEADS, P_SIZE)
    key_side = jax.nn.silu(causal_conv(ssm_b, conv_b)).reshape(blocks, TOK_DEV, N)
    read_side = jax.nn.silu(causal_conv(ssm_c, conv_c)).reshape(blocks, TOK_DEV, N)
    log_decay = (step_sizes * (-jnp.exp(a_log))[None, :]).reshape(blocks, TOK_DEV, SSM_HEADS)
    block_steps = step_sizes.reshape(blocks, TOK_DEV, SSM_HEADS)
    initial = jnp.zeros((SSM_HEADS, P_SIZE, N), jnp.float32)
    _, mixed_out = lax.scan(ssd_block, initial, (layer_input_rows, key_side, read_side, log_decay, block_steps))
    mixed_out = mixed_out.reshape(SEQUENCE_TOKENS, SSM_HEADS * P_SIZE)
    gated_out = mixed_out * jax.nn.silu(ssm_z)
    strength = lax.optimization_barrier(jnp.sum(gated_out * gated_out, axis=1)) / (SSM_HEADS * P_SIZE)
    return gated_out * lax.rsqrt(strength + 1e-05)[:, None] * norm_gain[None, :]

def attention(queries, keys, values):
    head_dim = keys.shape[1]
    block_span = math.gcd(SEQUENCE_TOKENS, 512)
    token_block_grid = queries.reshape(SEQUENCE_TOKENS // block_span, block_span, QHEADS, head_dim)
    key_pos = jnp.arange(SEQUENCE_TOKENS, dtype=jnp.int32)
    starts = (jnp.arange(SEQUENCE_TOKENS // block_span, dtype=jnp.int32) * block_span).astype(jnp.int32)

    def one_block(block_item):
        query_block, first_row = block_item
        query_pos = first_row + jnp.arange(block_span, dtype=jnp.int32)
        scores = jnp.einsum('qhe,ke->qhk', query_block, keys, precision=HIGHEST) / math.sqrt(head_dim)
        allowed = key_pos[None, None, :] <= query_pos[:, None, None]
        weights = jax.nn.softmax(jnp.where(allowed, scores, -jnp.inf), axis=2)
        return jnp.einsum('qhk,ke->qhe', weights, values, precision=HIGHEST)
    return lax.map(one_block, (token_block_grid, starts)).reshape(SEQUENCE_TOKENS, QHEADS * head_dim)

def reference(ssm_x, ssm_z, ssm_b, ssm_c, step_sizes, a_log, conv_x, conv_b, conv_c, norm_gain, queries, keys, values):
    mixer_out = mixer(ssm_x, ssm_z, ssm_b, ssm_c, step_sizes, a_log, conv_x, conv_b, conv_c, norm_gain)
    attention_out = attention(queries, keys, values)
    return (mixer_out, attention_out)
```

```python
import math

import jax
import jax.numpy as jnp
from jax import lax
from jax.experimental import pallas as pl
from jax.experimental.pallas import tpu as pltpu
from jax.sharding import PartitionSpec as P

HIGHEST = lax.Precision.HIGHEST
F32 = jnp.float32
BF16 = jnp.bfloat16
FLOOR = -1e30
MESH = pl.DeviceIdType.MESH
NY, NX, NZ, NC = 4, 4, 8, 2
TOK = 256
SHARD = TOK // NY
E = 128
PD = 64
ND = 256
HEADS = 8
XW = HEADS * PD


def fdot(a, b, ca, cb):
    return lax.dot_general(
        a, b, (((ca,), (cb,)), ((), ())), precision=HIGHEST, preferred_element_type=F32
    )


def split2(v):
    hi = v.astype(BF16)
    lo = (v - hi.astype(F32)).astype(BF16)
    return hi, lo


def silu(v):
    return v / (1.0 + jnp.exp(-v))


def body(
    x_ref, z_ref, b_ref, c_ref, dt_ref, alog_ref, wx_ref, wb_ref, wc_ref, gain_ref,
    q_ref, k_ref, v_ref,
    mix_ref, att_ref,
    qbuf, qs, kvbuf, kcat, vcat, acc, mrow, lrow, mlsend, mlrecv, crecv, crelay,
    halo_x, halo_b, halo_c, xp, bp, cp, xc, bc, cc, ybuf, ecum, sst, part, merged,
    rin, pre, tot, xtot, fin, iin, dsend, inc, ss_own, ss_in,
    q_send, q_recv, halo_send, halo_recv, kv_sem, zp_send, zp_recv, zm_send, zm_recv,
    part_send, part_recv, x_recv, r_send, l_send, fr_send, fl_send,
    sp_send, sp_recv, a2a_send, a2a_recv, xt_send, xt_recv, f_send, f_recv, d_send, d_recv,
    ml_send, ml_rsem, c_send, c_rsem, cr_send, cr_recv, cf_send, ss_send, ss_recv,
):
    h = lax.axis_index("head")
    i = lax.axis_index("ctx")
    c = lax.rem(i, NC)
    z = lax.rem(i // NC, NZ)
    x = i // (NC * NZ)

    def at(xx, zz, c_):
        return (xx * NZ + zz) * NC + c_

    def yid(d):
        return (lax.rem(h + d + NY, NY), i)

    def zid(d):
        return (h, at(x, lax.rem(z + d + NZ, NZ), c))

    def xid(d):
        return (h, at(lax.rem(x + d + NX, NX), z, c))

    mate = (h, i + 1 - 2 * c)

    def rcopy(src, dst, ssem, rsem, dev):
        return pltpu.make_async_remote_copy(
            src_ref=src, dst_ref=dst, send_sem=ssem, recv_sem=rsem,
            device_id=dev, device_id_type=MESH,
        )

    barrier = pltpu.get_barrier_semaphore()

    def hello(dev):
        pl.semaphore_signal(barrier, inc=1, device_id=dev, device_id_type=MESH)

    for d in range(1, NY):
        hello(yid(d))
    for d in range(1, NZ):
        hello(zid(d))
    for d in range(1, NX):
        hello(xid(d))
    hello(mate)

    @pl.when(i > 0)
    def _():
        hello((h, i - 1))

    @pl.when(i < NX * NZ * NC - 1)
    def _():
        hello((h, i + 1))

    own_a = 2 * x
    mine = pl.ds(c * 256, 256)

    def slot(n):
        return kvbuf.at[2 * x + n // 4, pl.ds(c * 256 + (n % 4) * SHARD, SHARD), :]

    def local_kv():
        ours = pl.ds(h * SHARD, SHARD)
        rows = pl.ds(c * 256, SHARD)
        return (
            pltpu.make_async_copy(k_ref.at[ours, :], kvbuf.at[own_a, rows, pl.ds(0, E)], kv_sem.at[0]),
            pltpu.make_async_copy(v_ref.at[ours, :], kvbuf.at[own_a, rows, pl.ds(E, E)], kv_sem.at[1]),
        )

    for cpy in local_kv():
        cpy.start()
    for cpy in local_kv():
        cpy.wait()

    pl.semaphore_wait(
        barrier,
        (NY - 1) + (NZ - 1) + (NX - 1) + 1
        + jnp.where(i > 0, 1, 0) + jnp.where(i < NX * NZ * NC - 1, 1, 0),
    )

    def halo(k, src, dst):
        return rcopy(
            src.at[pl.ds(TOK - 8, 8), :], dst, halo_send.at[k], halo_recv.at[k], (h, i + 1)
        )

    def halos():
        return (halo(0, x_ref, halo_x), halo(1, b_ref, halo_b), halo(2, c_ref, halo_c))

    @pl.when(i < NX * NZ * NC - 1)
    def _():
        for cpy in halos():
            cpy.start()

    def zplus(s):
        return rcopy(slot(0 if s == 1 else 2 * s - 3), slot(2 * s - 1), zp_send.at[s - 1], zp_recv.at[s - 1], zid(1))

    def zminus(s):
        return rcopy(slot(0 if s == 1 else 2 * s - 2), slot(2 * s), zm_send.at[s - 1], zm_recv.at[s - 1], zid(-1))

    zplus(1).start()
    zminus(1).start()

    def qhalf(ref, k):
        return ref.at[pl.ds(k * 128, 128), :]

    def q_up(k):
        return rcopy(qhalf(q_ref, k), qbuf.at[0, pl.ds(k * 128, 128), :], q_send.at[k], q_recv.at[0, k], yid(1))

    def q_down(k):
        return rcopy(qhalf(q_ref, k), qbuf.at[1, pl.ds(k * 128, 128), :], q_send.at[2 + k], q_recv.at[1, k], yid(-1))

    def q_relay_up():
        return rcopy(qbuf.at[0, pl.ds(0, 128), :], qbuf.at[2, pl.ds(0, 128), :], q_send.at[4], q_recv.at[2, 0], yid(1))

    def q_relay_down():
        return rcopy(qbuf.at[1, pl.ds(128, 128), :], qbuf.at[2, pl.ds(128, 128), :], q_send.at[5], q_recv.at[2, 1], yid(-1))

    q_up(0).start()
    q_down(1).start()
    q_up(1).start()
    q_down(0).start()

    acc[...] = jnp.zeros_like(acc)
    lrow[...] = jnp.zeros_like(lrow)
    mrow[...] = jnp.full(mrow.shape, FLOOR, F32)

    qscale = math.log2(math.e) / math.sqrt(E)

    def load_q(g, src):
        for a in range(2):
            hi, lo = split2(src[:, a * E : (a + 1) * E] * qscale)
            qs[g, pl.ds(a * 256, 256), 0:128] = hi
            qs[g, pl.ds(a * 256, 256), 128:256] = lo
            qs[g, pl.ds(a * 256, 256), 256:384] = hi

    load_q(0, q_ref[...])

    xp[pl.ds(8, TOK), :] = x_ref[...]
    bp[pl.ds(8, TOK), :] = b_ref[...]
    cp[pl.ds(8, TOK), :] = c_ref[...]

    @pl.when(i > 0)
    def _():
        for cpy in halos():
            cpy.wait_recv()
        xp[0:8, :] = halo_x[...]
        bp[0:8, :] = halo_b[...]
        cp[0:8, :] = halo_c[...]

    @pl.when(i == 0)
    def _():
        xp[0:8, :] = jnp.zeros((8, XW), F32)
        bp[0:8, :] = jnp.zeros((8, ND), F32)
        cp[0:8, :] = jnp.zeros((8, ND), F32)

    def conv(pad, w_ref):
        total = w_ref[0:1, :] * pad[pl.ds(5, TOK), :]
        for k in range(1, 4):
            total = total + w_ref[k : k + 1, :] * pad[pl.ds(5 + k, TOK), :]
        return silu(total)

    bc[...] = conv(bp, wb_ref)
    xc[...] = conv(xp, wx_ref)

    zplus(1).wait_recv()
    zplus(2).start()
    zminus(1).wait_recv()
    zminus(2).start()

    row_t = lax.broadcasted_iota(jnp.int32, (TOK, TOK), 0)
    col_t = lax.broadcasted_iota(jnp.int32, (TOK, TOK), 1)
    lower = jnp.where(col_t <= row_t, 1.0, 0.0).astype(F32)
    eye = jnp.where(col_t == row_t, 1.0, 0.0).astype(F32)
    spread_h = lax.broadcasted_iota(jnp.int32, (HEADS, XW), 0)
    spread_c = lax.broadcasted_iota(jnp.int32, (HEADS, XW), 1)
    expand = jnp.where(spread_c // PD == spread_h, 1.0, 0.0).astype(F32)
    dt = dt_ref[...]
    la = dt * (-jnp.exp(alog_ref[...]))
    cum = fdot(lower, la, 1, 0)
    cum_t = fdot(cum, eye, 0, 0)
    last = cum[TOK - 1 : TOK, :]
    towards = jnp.exp(last - cum) * dt
    tow_x = fdot(towards, expand, 1, 0)
    own = fdot(xc[...] * tow_x, bc[...], 0, 0)
    sst[:, 0:4, :, :] = own.reshape(16, 4, 8, ND)
    growth = jnp.broadcast_to(jnp.exp(cum_t[:, TOK - 1 : TOK]), (HEADS, ND))
    for hh in range(HEADS):
        g8 = jnp.broadcast_to(growth[hh : hh + 1, :], (8, ND))
        sst[2 * hh, 4, :, :] = g8
        sst[2 * hh + 1, 4, :, :] = g8

    def to_mate():
        return rcopy(sst.at[pl.ds(8 * (1 - c), 8)], part, sp_send.at[0], sp_recv.at[0], mate)

    to_mate().start()

    q_up(0).wait_recv()
    q_relay_up().start()
    q_down(1).wait_recv()
    q_relay_down().start()

    def kvrows(blk):
        return kvbuf.at[blk, mine, :]

    def share(blk):
        return rcopy(kvrows(blk), kvrows(blk), part_send.at[blk], part_recv.at[blk], mate)

    def right(hb, blk, sem):
        return rcopy(kvrows(blk), kvrows(blk), sem.at[hb], x_recv.at[blk], xid(1))

    def left(hb, blk, sem):
        return rcopy(kvrows(blk), kvrows(blk), sem.at[hb], x_recv.at[blk], xid(-1))

    goes_left = jnp.logical_or(x == 0, jnp.logical_and(x == 1, c == 1))

    def ready(hb):
        blk = 2 * x + hb
        share(blk).start()

        @pl.when(x < NX - 1)
        def _():
            right(hb, blk, r_send).start()

        @pl.when(goes_left)
        def _():
            left(hb, blk, l_send).start()

    zplus(2).wait_recv()
    zplus(3).start()
    ready(0)
    zminus(2).wait_recv()
    zminus(3).start()

    cc[...] = conv(cp, wc_ref)
    inter = fdot(cc[...], bc[...], 1, 1)
    dt_x = fdot(dt, expand, 1, 0)
    ecum[...] = fdot(jnp.exp(cum), expand, 1, 0)
    causal = col_t <= row_t
    first = lax.broadcasted_iota(jnp.int32, (TOK, 128), 1) < PD
    for pair in range(HEADS // 2):
        lanes = pl.ds(pair * 128, 128)
        xd = xc[:, pair * 128 : (pair + 1) * 128] * dt_x[:, pair * 128 : (pair + 1) * 128]
        outs = []
        for k in range(2):
            hh = 2 * pair + k
            gap = cum[:, hh : hh + 1] - cum_t[hh : hh + 1, :]
            mixing = inter * jnp.where(causal, jnp.exp(jnp.minimum(gap, 0.0)), 0.0)
            outs.append(fdot(mixing, xd, 1, 0))
        ybuf[:, lanes] = jnp.where(first, outs[0], outs[1])

    zplus(3).wait_recv()
    zplus(4).start()
    zminus(3).wait_recv()

    to_mate().wait_recv()
    whole = pl.ds(8 * c, 8)
    mine_s = sst[whole]
    theirs = part[...]
    g_mine, g_theirs = mine_s[:, 4:5], theirs[:, 4:5]
    chip = jnp.where(
        c == 0, g_theirs * mine_s[:, 0:4] + theirs[:, 0:4], g_mine * theirs[:, 0:4] + mine_s[:, 0:4]
    )
    merged[:, 0:4] = chip
    merged[:, 4:5] = g_mine * g_theirs

    def to_owner(d):
        k = lax.rem(z + d, NZ)
        return rcopy(merged.at[k], rin.at[z], a2a_send.at[d - 1], a2a_recv.at[d - 1], zid(d))

    def from_peer(d):
        return rcopy(merged.at[z], rin.at[lax.rem(z + NZ - d, NZ)], a2a_send.at[d - 1], a2a_recv.at[d - 1], zid(d))

    for d in (4, 3, 5, 2, 6, 1, 7):
        to_owner(d).start()
    rin[z] = merged[z]

    zplus(4).wait_recv()
    ready(1)

    def convert(blk):
        kv = kvbuf[blk]
        hi, lo = split2(kv[:, 0:E])
        kcat[blk, :, 0:128] = hi
        kcat[blk, :, 128:256] = hi
        kcat[blk, :, 256:384] = lo
        hi, lo = split2(kv[:, E : 2 * E])
        vcat[blk, :, 0:128] = hi
        vcat[blk, :, 128:256] = lo

    def attend(g, blk, masked):
        allowed = None
        if masked:
            kidx = lax.broadcasted_iota(jnp.int32, (256, 512), 1)
            kc = kidx // 256
            n = (blk - 2 * x) * 4 + lax.rem(kidx // SHARD, 4)
            rho = jnp.where(lax.rem(n, 2) == 1, -((n + 1) // 2), n // 2)
            kz = lax.rem(z + rho + NZ, NZ)
            kpos = at(x, kz, kc) * TOK + h * SHARD + lax.rem(kidx, SHARD)
            qpos = i * TOK + lax.broadcasted_iota(jnp.int32, (256, 512), 0)
            allowed = kpos <= qpos
        for r in range(2):
            rows = pl.ds(r * 256, 256)
            s = lax.dot_general(
                qs[g, rows, :], kcat[blk], (((1,), (1,)), ((), ())), preferred_element_type=F32
            )
            if masked:
                s = jnp.where(allowed, s, FLOOR)
            m_old = mrow[g, rows, :]
            m_new = jnp.maximum(m_old, jnp.max(s, axis=1, keepdims=True))
            alpha = jnp.exp2(m_old - m_new)
            p = jnp.exp2(s - jnp.concatenate([m_new] * 4, axis=1))
            if masked:
                p = jnp.where(allowed, p, 0.0)
            lrow[g, rows, :] = lrow[g, rows, :] * alpha + (
                (p[:, 0:128] + p[:, 128:256]) + (p[:, 256:384] + p[:, 384:512])
            )
            p_hi, p_lo = split2(p)
            vv = vcat[blk]
            o = jnp.dot(p_hi, vv, preferred_element_type=F32) + jnp.dot(p_lo, vv, preferred_element_type=F32)
            acc[g, rows, :] = acc[g, rows, :] * alpha + (o[:, 0:128] + o[:, 128:256])
            mrow[g, rows, :] = m_new

    for hb in range(2):
        share(2 * x + hb).wait_recv()
        convert(2 * x + hb)

    def own_blocks(g):
        def step(hb, carry):
            attend(g, 2 * x + hb, True)
            return carry

        lax.fori_loop(0, 2, step, 0)

    own_blocks(0)
    q_up(1).wait_recv()
    load_q(1, qbuf[0])
    own_blocks(1)
    q_down(0).wait_recv()
    load_q(2, qbuf[1])
    own_blocks(2)
    q_relay_up().wait_recv()
    q_relay_down().wait_recv()
    load_q(3, qbuf[2])
    own_blocks(3)

    def got(blk):
        return right(0, blk, fr_send)

    @pl.when(jnp.logical_and(x == 0, c == 1))
    def _():
        for hb in range(2):
            got(2 + hb).wait_recv()
            left(hb, 2 + hb, fl_send).start()

    for d in range(1, NZ):
        from_peer(d).wait_recv()
    run = jnp.zeros((4, 8, ND), F32)
    gprod = jnp.ones((1, 8, ND), F32)
    for zz in range(NZ):
        pre[zz, 0:4] = run
        pre[zz, 4:5] = gprod
        gz = rin[zz, 4:5]
        run = gz * run + rin[zz, 0:4]
        gprod = gprod * gz
    tot[0:4] = run
    tot[4:5] = gprod

    def to_x(d):
        return rcopy(tot, xtot.at[x], xt_send.at[d - 1], xt_recv.at[d - 1], (h, at(x + d, z, c)))

    def from_x(d):
        return rcopy(tot, xtot.at[x - d], xt_send.at[d - 1], xt_recv.at[d - 1], (h, at(x - d, z, c)))

    for d in range(1, NX):

        @pl.when(x + d < NX)
        def _():
            to_x(d).start()

    def arrive(u, hb):
        blk = 2 * u + hb
        got(blk).wait_recv()
        share(blk).start()

        @pl.when(jnp.logical_and(x == 3, u == 0))
        def _():
            left(hb, blk, fl_send).start()

        @pl.when(jnp.logical_and(jnp.logical_and(x == 2, u == 1), c == 0))
        def _():
            right(hb, blk, fr_send).start()

    def unit(j):
        return jnp.where(x == 3, lax.rem(2 * j, 3), x - 1 - j)

    def middle_unit(j):
        u = unit(j)
        for hb in range(2):
            arrive(u, hb)
        for hb in range(2):
            blk = 2 * u + hb
            share(blk).wait_recv()
            convert(blk)

            def step(g, carry):
                attend(g, blk, False)
                return carry

            lax.fori_loop(0, 4, step, 0)

    @pl.when(x >= 2)
    def _():
        middle_unit(0)

    for d in range(1, NX):

        @pl.when(x >= d)
        def _():
            from_x(d).wait_recv()

    before = jnp.zeros((4, 8, ND), F32)
    for xs in range(NX - 1):
        before = jnp.where(xs < x, xtot[xs, 4:5] * before + xtot[xs, 0:4], before)
    for zz in range(NZ):
        fin[zz] = pre[zz, 0:4] + pre[zz, 4:5] * before

    def to_block(d):
        k = lax.rem(z + d, NZ)
        return rcopy(fin.at[k], iin.at[z], f_send.at[d - 1], f_recv.at[d - 1], zid(d))

    def from_owner(d):
        return rcopy(fin.at[z], iin.at[lax.rem(z + NZ - d, NZ)], f_send.at[d - 1], f_recv.at[d - 1], zid(d))

    for d in (4, 3, 5, 2, 6, 1, 7):
        to_block(d).start()
    iin[z] = fin[z]

    @pl.when(x >= 3)
    def _():
        middle_unit(1)

    for d in range(1, NZ):
        from_owner(d).wait_recv()
    chip_in = iin[...]
    mine_s = sst[whole]
    theirs = part[...]
    second = jnp.where(c == 0, mine_s[:, 4:5], theirs[:, 4:5]) * chip_in + jnp.where(
        c == 0, mine_s[:, 0:4], theirs[:, 0:4]
    )
    dsend[...] = jnp.where(c == 0, second, chip_in)
    inc[whole] = jnp.where(c == 0, chip_in, second)

    def to_mate_in():
        return rcopy(dsend, inc.at[whole], d_send.at[0], d_recv.at[0], mate)

    to_mate_in().start()

    @pl.when(x >= 1)
    def _():
        u = unit(x - 1)
        for hb in range(2):
            arrive(u, hb)
        for hb in range(2):
            blk = 2 * u + hb
            share(blk).wait_recv()
            convert(blk)

    def last_unit(g):
        @pl.when(x >= 1)
        def _():
            u = unit(x - 1)

            def step(hb, carry):
                attend(g, 2 * u + hb, False)
                return carry

            lax.fori_loop(0, 2, step, 0)

    lane = lax.broadcasted_iota(jnp.int32, (512, 128), 1)
    pick = jnp.where(
        lax.broadcasted_iota(jnp.int32, (8, 128), 0) == lax.broadcasted_iota(jnp.int32, (8, 128), 1), 1.0, 0.0
    ).astype(F32)

    def sums(g):
        return jnp.sum(lrow[g], axis=1, keepdims=True)

    def pack_ml(g):
        ml = jnp.where(lane == 0, mrow[g], jnp.where(lane == 1, sums(g), 0.0))
        mlsend[g - 1] = fdot(pick, ml, 1, 1)

    def ml_copy(g):
        k = g - 1
        return rcopy(mlsend.at[k], mlrecv.at[k], ml_send.at[k], ml_rsem.at[k], yid((-1, 1, 2)[k]))

    def acc_copy(g):
        k = g - 1
        return rcopy(acc.at[g], crecv.at[k], c_send.at[k], c_rsem.at[k], yid((-1, 1)[k]))

    def acc_far(k):
        return rcopy(acc.at[3, pl.ds(k * 256, 256), :], crelay.at[k], cr_send.at[k], cr_recv.at[k], yid((1, -1)[k]))

    def acc_far_on(k):
        return rcopy(crelay.at[k], crecv.at[2, pl.ds(k * 256, 256), :], cf_send.at[k], c_rsem.at[2 + k], yid((1, -1)[k]))

    last_unit(3)
    pack_ml(3)
    acc_far(0).start()
    acc_far(1).start()
    ml_copy(3).start()
    last_unit(1)
    pack_ml(1)
    acc_copy(1).start()
    ml_copy(1).start()
    last_unit(2)
    pack_ml(2)
    acc_copy(2).start()
    ml_copy(2).start()
    for k in range(2):
        acc_far(k).wait_recv()
        acc_far_on(k).start()
    last_unit(0)

    to_mate_in().wait_recv()
    carried = fdot(cc[...], inc[...].reshape(XW, ND), 1, 1)
    gated = (ybuf[...] + ecum[...] * carried) * silu(z_ref[...])
    ybuf[...] = gated
    ss_own[...] = fdot(jnp.ones((8, XW), F32), gated * gated, 1, 1)

    def ss_copy(d):
        return rcopy(ss_own, ss_in.at[d - 1], ss_send.at[d - 1], ss_recv.at[d - 1], yid(d))

    for d in range(1, NY):
        ss_copy(d).start()

    for k in range(3):
        ml_copy(k + 1).wait_recv()
    ms = [mrow[0][:, 0:1]]
    ls = [sums(0)]
    for k in range(3):
        col = fdot(mlrecv[k], pick, 0, 0)
        ms.append(col[:, 0:1])
        ls.append(col[:, 1:2])
    top = jnp.maximum(jnp.maximum(ms[0], ms[1]), jnp.maximum(ms[2], ms[3]))
    ws = [jnp.exp2(m - top) for m in ms]
    den = ws[0] * ls[0] + ws[1] * ls[1] + ws[2] * ls[2] + ws[3] * ls[3]
    inv = 1.0 / den
    acc_copy(1).wait_recv()
    acc_copy(2).wait_recv()
    for k in range(2):
        acc_far_on(k).wait_recv()
    joined = acc[0] * (ws[0] * inv)
    for k in range(3):
        joined = joined + crecv[k] * (ws[k + 1] * inv)
    att_ref[:, 0:128] = joined[0:256]
    att_ref[:, 128:256] = joined[256:512]

    for d in range(1, NY):
        ss_copy(d).wait_recv()
    ss = ss_own[...] + ss_in[0] + ss_in[1] + ss_in[2]
    col = fdot(ss, pick, 0, 0)[:, 0:1]
    mix_ref[...] = ybuf[...] * lax.rsqrt(col / (XW * NY) + 1e-05) * gain_ref[...]

    @pl.when(i < NX * NZ * NC - 1)
    def _():
        for cpy in halos():
            cpy.wait_send()

    for s in range(1, 5):
        zplus(s).wait_send()
    for s in range(1, 4):
        zminus(s).wait_send()
    for k in range(2):
        q_up(k).wait_send()
        q_down(k).wait_send()
    q_relay_up().wait_send()
    q_relay_down().wait_send()
    to_mate().wait_send()
    for hb in range(2):
        share(2 * x + hb).wait_send()

        @pl.when(x < NX - 1)
        def _():
            right(hb, 2 * x + hb, r_send).wait_send()

        @pl.when(goes_left)
        def _():
            left(hb, 2 * x + hb, l_send).wait_send()

        for u in range(NX - 1):

            @pl.when(u < x)
            def _():
                share(2 * u + hb).wait_send()

        @pl.when(jnp.logical_or(x == 3, jnp.logical_and(x == 0, c == 1)))
        def _():
            left(hb, 2 + hb, fl_send).wait_send()

        @pl.when(jnp.logical_and(x == 2, c == 0))
        def _():
            right(hb, 2 + hb, fr_send).wait_send()

    for d in range(1, NZ):
        to_owner(d).wait_send()
        to_block(d).wait_send()
    for d in range(1, NX):

        @pl.when(x + d < NX)
        def _():
            to_x(d).wait_send()

    to_mate_in().wait_send()
    for g in range(1, 4):
        ml_copy(g).wait_send()
    for k in range(2):
        acc_copy(k + 1).wait_send()
        acc_far(k).wait_send()
        acc_far_on(k).wait_send()
    for d in range(1, NY):
        ss_copy(d).wait_send()


def vm(*shape, dtype=F32):
    return pltpu.VMEM(shape, dtype)


def dma(*shape):
    return pltpu.SemaphoreType.DMA(shape)


SCRATCH = [
    vm(3, 256, 256), vm(4, 512, 384, dtype=BF16), vm(8, 512, 256),
    vm(8, 512, 384, dtype=BF16), vm(8, 512, 256, dtype=BF16),
    vm(4, 512, 128), vm(4, 512, 128), vm(4, 512, 128),
    vm(3, 8, 512), vm(3, 8, 512), vm(3, 512, 128), vm(2, 256, 128),
    vm(8, XW), vm(8, ND), vm(8, ND), vm(TOK + 8, XW), vm(TOK + 8, ND), vm(TOK + 8, ND),
    vm(TOK, XW), vm(TOK, ND), vm(TOK, ND), vm(TOK, XW), vm(TOK, XW),
    vm(16, 5, 8, ND), vm(8, 5, 8, ND), vm(8, 5, 8, ND),
    vm(8, 5, 8, ND), vm(8, 5, 8, ND), vm(5, 8, ND), vm(4, 5, 8, ND),
    vm(8, 4, 8, ND), vm(8, 4, 8, ND), vm(8, 4, 8, ND), vm(16, 4, 8, ND),
    vm(8, TOK), vm(3, 8, TOK),
    dma(6), dma(3, 2), dma(3), dma(3), dma(2), dma(4), dma(4), dma(3), dma(3),
    dma(8), dma(8), dma(8), dma(2), dma(2), dma(2), dma(2),
    dma(1), dma(1), dma(7), dma(7), dma(3), dma(3), dma(7), dma(7), dma(1), dma(1),
    dma(3), dma(3), dma(2), dma(4), dma(2), dma(2), dma(2), dma(3), dma(3),
]


def on_device(
    ssm_x, ssm_z, ssm_b, ssm_c, step_sizes, a_log, conv_x, conv_b, conv_c, norm_gain,
    queries, keys, values,
):
    spec = pl.BlockSpec(memory_space=pltpu.VMEM)
    return pl.pallas_call(
        body,
        out_shape=(
            jax.ShapeDtypeStruct((TOK, XW), F32),
            jax.ShapeDtypeStruct((TOK, 256), F32),
        ),
        in_specs=[spec] * 13,
        out_specs=(spec, spec),
        scratch_shapes=SCRATCH,
        compiler_params=pltpu.CompilerParams(
            collective_id=0, has_side_effects=True, vmem_limit_bytes=60 * 1024 * 1024
        ),
        name="layer",
    )(
        ssm_x, ssm_z, ssm_b, ssm_c, step_sizes, a_log.reshape(1, HEADS), conv_x, conv_b, conv_c,
        norm_gain.reshape(1, XW), queries, keys, values,
    )


def solution(mesh):
    placed = (
        P("ctx", "head"),
        P("ctx", "head"),
        P("ctx", None),
        P("ctx", None),
        P("ctx", "head"),
        P("head"),
        P(None, "head"),
        P(),
        P(),
        P("head"),
        P("ctx", "head"),
        P("ctx", None),
        P("ctx", None),
    )
    return jax.shard_map(
        on_device,
        mesh=mesh,
        in_specs=placed,
        out_specs=(P("ctx", "head"), P("ctx", "head")),
        check_vma=False,
    )
```

```python
import math

import jax
import jax.numpy as jnp
from jax import lax
from jax.experimental import pallas as pl
from jax.experimental.pallas import tpu as pltpu
from jax.sharding import PartitionSpec as P

F32 = jnp.float32
BF16 = jnp.bfloat16
FLOOR = -1e30
MESH = pl.DeviceIdType.MESH
NY, NX, NZ, NC = 4, 4, 8, 2
TOK = 256
SHARD = TOK // NY
E = 128
PD = 64
ND = 256
HEADS = 8
XW = HEADS * PD


def split2(v):
    hi = v.astype(BF16)
    lo = (v - hi.astype(F32)).astype(BF16)
    return hi, lo


def bdot(a, b, ca, cb):
    return lax.dot_general(a, b, (((ca,), (cb,)), ((), ())), preferred_element_type=F32)


def dot3(a, b, ca, cb):
    ah, al = split2(a)
    bh, bl = split2(b)
    return bdot(ah, bh, ca, cb) + (bdot(ah, bl, ca, cb) + bdot(al, bh, ca, cb))


def parts3(v):
    hi = v.astype(BF16).astype(F32)
    mid = (v - hi).astype(BF16).astype(F32)
    low = (v - hi) - mid
    return hi, mid, low


def stack3(v):
    hi, mid, low = parts3(v)
    return jnp.concatenate([hi, mid, low, jnp.zeros_like(v)], axis=0).astype(BF16)


def silu(v):
    return v / (1.0 + jnp.exp(-v))


def body(
    x_ref, z_ref, b_ref, c_ref, dt_ref, alog_ref, wx_ref, wb_ref, wc_ref, gain_ref,
    q_ref, k_ref, v_ref,
    mix_ref, att_ref,
    qbuf, qs, kvbuf, kcat, vcat, acc, mrow, lrow, mlsend, mlrecv, crecv, crelay,
    bias_ref, halo_x, halo_b, halo_c, xp, bp, cp, xc, bc, cc, ybuf, ecum, sst, part, merged,
    rin, pre, tot, xtot, fin, iin, dsend, inc, ss_own, ss_in,
    q_send, q_recv, halo_send, halo_recv, kv_sem, zp_send, zp_recv, zm_send, zm_recv,
    part_send, part_recv, x_recv, r_send, l_send, fr_send, fl_send,
    sp_send, sp_recv, a2a_send, a2a_recv, xt_send, xt_recv, f_send, f_recv, d_send, d_recv,
    ml_send, ml_rsem, c_send, c_rsem, cr_send, cr_recv, cf_send, ss_send, ss_recv,
):
    h = lax.axis_index("head")
    i = lax.axis_index("ctx")
    c = lax.rem(i, NC)
    z = lax.rem(i // NC, NZ)
    x = i // (NC * NZ)

    def at(xx, zz, c_):
        return (xx * NZ + zz) * NC + c_

    def yid(d):
        return (lax.rem(h + d + NY, NY), i)

    def zid(d):
        return (h, at(x, lax.rem(z + d + NZ, NZ), c))

    def xid(d):
        return (h, at(lax.rem(x + d + NX, NX), z, c))

    mate = (h, i + 1 - 2 * c)

    def rcopy(src, dst, ssem, rsem, dev):
        return pltpu.make_async_remote_copy(
            src_ref=src, dst_ref=dst, send_sem=ssem, recv_sem=rsem,
            device_id=dev, device_id_type=MESH,
        )

    barrier = pltpu.get_barrier_semaphore()

    def hello(dev):
        pl.semaphore_signal(barrier, inc=1, device_id=dev, device_id_type=MESH)

    for d in range(1, NY):
        hello(yid(d))
    for d in range(1, NZ):
        hello(zid(d))
    for d in range(1, NX):
        hello(xid(d))
    hello(mate)

    @pl.when(i > 0)
    def _():
        hello((h, i - 1))

    @pl.when(i < NX * NZ * NC - 1)
    def _():
        hello((h, i + 1))

    own_a = 2 * x
    mine = pl.ds(c * 256, 256)

    def slot(n):
        return kvbuf.at[2 * x + n // 4, pl.ds(c * 256 + (n % 4) * SHARD, SHARD), :]

    def local_kv():
        ours = pl.ds(h * SHARD, SHARD)
        rows = pl.ds(c * 256, SHARD)
        return (
            pltpu.make_async_copy(k_ref.at[ours, :], kvbuf.at[own_a, rows, pl.ds(0, E)], kv_sem.at[0]),
            pltpu.make_async_copy(v_ref.at[ours, :], kvbuf.at[own_a, rows, pl.ds(E, E)], kv_sem.at[1]),
        )

    for cpy in local_kv():
        cpy.start()
    for cpy in local_kv():
        cpy.wait()

    pl.semaphore_wait(
        barrier,
        (NY - 1) + (NZ - 1) + (NX - 1) + 1
        + jnp.where(i > 0, 1, 0) + jnp.where(i < NX * NZ * NC - 1, 1, 0),
    )

    def halo(k, src, dst):
        return rcopy(
            src.at[pl.ds(TOK - 8, 8), :], dst, halo_send.at[k], halo_recv.at[k], (h, i + 1)
        )

    def halos():
        return (halo(0, x_ref, halo_x), halo(1, b_ref, halo_b), halo(2, c_ref, halo_c))

    @pl.when(i < NX * NZ * NC - 1)
    def _():
        for cpy in halos():
            cpy.start()

    def zplus(s):
        return rcopy(slot(0 if s == 1 else 2 * s - 3), slot(2 * s - 1), zp_send.at[s - 1], zp_recv.at[s - 1], zid(1))

    def zminus(s):
        return rcopy(slot(0 if s == 1 else 2 * s - 2), slot(2 * s), zm_send.at[s - 1], zm_recv.at[s - 1], zid(-1))

    zplus(1).start()
    zminus(1).start()

    def qhalf(ref, k):
        return ref.at[pl.ds(k * 128, 128), :]

    def q_up(k):
        return rcopy(qhalf(q_ref, k), qbuf.at[0, pl.ds(k * 128, 128), :], q_send.at[k], q_recv.at[0, k], yid(1))

    def q_down(k):
        return rcopy(qhalf(q_ref, k), qbuf.at[1, pl.ds(k * 128, 128), :], q_send.at[2 + k], q_recv.at[1, k], yid(-1))

    def q_relay_up():
        return rcopy(qbuf.at[0, pl.ds(0, 128), :], qbuf.at[2, pl.ds(0, 128), :], q_send.at[4], q_recv.at[2, 0], yid(1))

    def q_relay_down():
        return rcopy(qbuf.at[1, pl.ds(128, 128), :], qbuf.at[2, pl.ds(128, 128), :], q_send.at[5], q_recv.at[2, 1], yid(-1))

    q_up(0).start()
    q_down(1).start()
    q_up(1).start()
    q_down(0).start()

    acc[...] = jnp.zeros_like(acc)
    lrow[...] = jnp.zeros_like(lrow)
    mrow[...] = jnp.full(mrow.shape, FLOOR, F32)

    qscale = math.log2(math.e) / math.sqrt(E)

    def load_q(g, src):
        for a in range(2):
            hi, lo = split2(src[:, a * E : (a + 1) * E] * qscale)
            qs[g, pl.ds(a * 256, 256), 0:128] = hi
            qs[g, pl.ds(a * 256, 256), 128:256] = lo
            qs[g, pl.ds(a * 256, 256), 256:384] = hi

    load_q(0, q_ref[...])

    xp[pl.ds(8, TOK), :] = x_ref[...]
    bp[pl.ds(8, TOK), :] = b_ref[...]
    cp[pl.ds(8, TOK), :] = c_ref[...]

    @pl.when(i > 0)
    def _():
        for cpy in halos():
            cpy.wait_recv()
        xp[0:8, :] = halo_x[...]
        bp[0:8, :] = halo_b[...]
        cp[0:8, :] = halo_c[...]

    @pl.when(i == 0)
    def _():
        xp[0:8, :] = jnp.zeros((8, XW), F32)
        bp[0:8, :] = jnp.zeros((8, ND), F32)
        cp[0:8, :] = jnp.zeros((8, ND), F32)

    def conv(pad, w_ref):
        total = w_ref[0:1, :] * pad[pl.ds(5, TOK), :]
        for k in range(1, 4):
            total = total + w_ref[k : k + 1, :] * pad[pl.ds(5 + k, TOK), :]
        return silu(total)

    bc[...] = conv(bp, wb_ref)
    xc[...] = conv(xp, wx_ref)

    zplus(1).wait_recv()
    zplus(2).start()
    zminus(1).wait_recv()
    zminus(2).start()

    row_t = lax.broadcasted_iota(jnp.int32, (TOK, TOK), 0)
    col_t = lax.broadcasted_iota(jnp.int32, (TOK, TOK), 1)
    upper = jnp.where(row_t <= col_t, 1.0, 0.0).astype(BF16)
    eye = jnp.where(col_t == row_t, 1.0, 0.0).astype(BF16)
    spread_h = lax.broadcasted_iota(jnp.int32, (32, XW), 0)
    spread_c = lax.broadcasted_iota(jnp.int32, (32, XW), 1)
    expand = jnp.where(
        jnp.logical_and(spread_c // PD == spread_h % HEADS, spread_h < 3 * HEADS), 1.0, 0.0
    ).astype(BF16)

    def widen(rows):
        return bdot(stack3(rows), expand, 0, 0)

    head_r = lax.broadcasted_iota(jnp.int32, (HEADS, HEADS), 0)
    head_c = lax.broadcasted_iota(jnp.int32, (HEADS, HEADS), 1)
    rate = -jnp.exp(alog_ref[...])
    rate = jnp.sum(jnp.where(head_r == head_c, rate, 0.0), axis=1, keepdims=True)
    dt = dt_ref[...]
    c3 = bdot(stack3(dt * rate), upper, 1, 0)
    cum_t = c3[0:8] + c3[8:16] + c3[16:24]
    c3 = bdot(eye, stack3(cum_t), 1, 1)
    cum = c3[:, 0:8] + c3[:, 8:16] + c3[:, 16:24]
    towards = jnp.exp(cum_t[:, TOK - 1 : TOK] - cum_t) * dt
    own = dot3(xc[...] * widen(towards), bc[...], 0, 0)
    sst[:, 0:4, :, :] = own.reshape(16, 4, 8, ND)
    growth = jnp.broadcast_to(jnp.exp(cum_t[:, TOK - 1 : TOK]), (HEADS, ND))
    for hh in range(HEADS):
        g8 = jnp.broadcast_to(growth[hh : hh + 1, :], (8, ND))
        sst[2 * hh, 4, :, :] = g8
        sst[2 * hh + 1, 4, :, :] = g8

    def to_mate():
        return rcopy(sst.at[pl.ds(8 * (1 - c), 8)], part, sp_send.at[0], sp_recv.at[0], mate)

    to_mate().start()

    q_up(0).wait_recv()
    q_relay_up().start()
    q_down(1).wait_recv()
    q_relay_down().start()

    def kvrows(blk):
        return kvbuf.at[blk, mine, :]

    def share(blk):
        return rcopy(kvrows(blk), kvrows(blk), part_send.at[blk], part_recv.at[blk], mate)

    def right(hb, blk, sem):
        return rcopy(kvrows(blk), kvrows(blk), sem.at[hb], x_recv.at[blk], xid(1))

    def left(hb, blk, sem):
        return rcopy(kvrows(blk), kvrows(blk), sem.at[hb], x_recv.at[blk], xid(-1))

    goes_left = jnp.logical_or(x == 0, jnp.logical_and(x == 1, c == 1))

    def ready(hb):
        blk = 2 * x + hb
        share(blk).start()

        @pl.when(x < NX - 1)
        def _():
            right(hb, blk, r_send).start()

        @pl.when(goes_left)
        def _():
            left(hb, blk, l_send).start()

    zplus(2).wait_recv()
    zplus(3).start()
    ready(0)
    zminus(2).wait_recv()
    zminus(3).start()

    cc[...] = conv(cp, wc_ref)
    inter = dot3(cc[...], bc[...], 1, 1)
    dt_x = widen(dt)
    ecum[...] = widen(jnp.exp(cum_t))
    causal = col_t <= row_t
    first = lax.broadcasted_iota(jnp.int32, (TOK, 128), 1) < PD
    for pair in range(HEADS // 2):
        lanes = pl.ds(pair * 128, 128)
        xd = xc[:, pair * 128 : (pair + 1) * 128] * dt_x[:, pair * 128 : (pair + 1) * 128]
        xd = jnp.concatenate(split2(xd), axis=1)
        outs = []
        for k in range(2):
            hh = 2 * pair + k
            gap = cum[:, hh : hh + 1] - cum_t[hh : hh + 1, :]
            mixing = inter * jnp.where(causal, jnp.exp(jnp.minimum(gap, 0.0)), 0.0)
            both = bdot(jnp.concatenate(split2(mixing), axis=0), xd, 1, 0)
            both = both[0:TOK] + both[TOK : 2 * TOK]
            outs.append(both[:, 0:128] + both[:, 128:256])
        ybuf[:, lanes] = jnp.where(first, outs[0], outs[1])

    zplus(3).wait_recv()
    zplus(4).start()
    zminus(3).wait_recv()

    to_mate().wait_recv()
    whole = pl.ds(8 * c, 8)
    mine_s = sst[whole]
    theirs = part[...]
    g_mine, g_theirs = mine_s[:, 4:5], theirs[:, 4:5]
    chip = jnp.where(
        c == 0, g_theirs * mine_s[:, 0:4] + theirs[:, 0:4], g_mine * theirs[:, 0:4] + mine_s[:, 0:4]
    )
    merged[:, 0:4] = chip
    merged[:, 4:5] = g_mine * g_theirs

    def to_owner(d):
        k = lax.rem(z + d, NZ)
        return rcopy(merged.at[k], rin.at[z], a2a_send.at[d - 1], a2a_recv.at[d - 1], zid(d))

    def from_peer(d):
        return rcopy(merged.at[z], rin.at[lax.rem(z + NZ - d, NZ)], a2a_send.at[d - 1], a2a_recv.at[d - 1], zid(d))

    for d in (4, 3, 5, 2, 6, 1, 7):
        to_owner(d).start()
    rin[z] = merged[z]

    zplus(4).wait_recv()
    ready(1)

    def convert(blk):
        kv = kvbuf[blk]
        hi, lo = split2(kv[:, 0:E])
        kcat[blk, :, 0:128] = hi
        kcat[blk, :, 128:256] = hi
        kcat[blk, :, 256:384] = lo
        hi, lo = split2(kv[:, E : 2 * E])
        vcat[blk, :, 0:128] = hi
        vcat[blk, :, 128:256] = lo

    def attend(g, blk, hb):
        s = bdot(qs[g], kcat[blk], 1, 1)
        if hb is not None:
            bias = bias_ref[hb]
            s = s + jnp.concatenate([bias, bias], axis=0)
        m_old = mrow[g]
        m_new = jnp.maximum(m_old, jnp.max(s, axis=1, keepdims=True))
        alpha = jnp.exp2(m_old - m_new)
        p = jnp.exp2(s - jnp.concatenate([m_new] * 4, axis=1))
        lrow[g] = lrow[g] * alpha + ((p[:, 0:128] + p[:, 128:256]) + (p[:, 256:384] + p[:, 384:512]))
        o = bdot(jnp.concatenate(split2(p), axis=0), vcat[blk], 1, 0)
        o = o[0:512] + o[512:1024]
        acc[g] = acc[g] * alpha + (o[:, 0:128] + o[:, 128:256])
        mrow[g] = m_new

    for hb in range(2):
        kidx = lax.broadcasted_iota(jnp.int32, (1, 512), 1)
        n = hb * 4 + lax.rem(kidx // SHARD, 4)
        rho = jnp.where(lax.rem(n, 2) == 1, -((n + 1) // 2), n // 2)
        kz = lax.rem(z + rho + NZ, NZ)
        kpos = at(x, kz, kidx // 256) * TOK + h * SHARD + lax.rem(kidx, SHARD)
        qpos = i * TOK + lax.broadcasted_iota(jnp.int32, (TOK, 512), 0)
        bias_ref[hb] = jnp.where(kpos <= qpos, 0.0, FLOOR)

    for hb in range(2):
        share(2 * x + hb).wait_recv()
        convert(2 * x + hb)

    def own_blocks(g):
        def step(hb, carry):
            attend(g, 2 * x + hb, hb)
            return carry

        lax.fori_loop(0, 2, step, 0)

    own_blocks(0)
    q_up(1).wait_recv()
    load_q(1, qbuf[0])
    own_blocks(1)
    q_down(0).wait_recv()
    load_q(2, qbuf[1])
    own_blocks(2)
    q_relay_up().wait_recv()
    q_relay_down().wait_recv()
    load_q(3, qbuf[2])
    own_blocks(3)

    def got(blk):
        return right(0, blk, fr_send)

    @pl.when(jnp.logical_and(x == 0, c == 1))
    def _():
        for hb in range(2):
            got(2 + hb).wait_recv()
            left(hb, 2 + hb, fl_send).start()

    for d in range(1, NZ):
        from_peer(d).wait_recv()
    run = jnp.zeros((4, 8, ND), F32)
    gprod = jnp.ones((1, 8, ND), F32)
    for zz in range(NZ):
        pre[zz, 0:4] = run
        pre[zz, 4:5] = gprod
        gz = rin[zz, 4:5]
        run = gz * run + rin[zz, 0:4]
        gprod = gprod * gz
    tot[0:4] = run
    tot[4:5] = gprod

    def to_x(d):
        return rcopy(tot, xtot.at[x], xt_send.at[d - 1], xt_recv.at[d - 1], (h, at(x + d, z, c)))

    def from_x(d):
        return rcopy(tot, xtot.at[x - d], xt_send.at[d - 1], xt_recv.at[d - 1], (h, at(x - d, z, c)))

    for d in range(1, NX):

        @pl.when(x + d < NX)
        def _():
            to_x(d).start()

    def arrive(u, hb):
        blk = 2 * u + hb
        got(blk).wait_recv()
        share(blk).start()

        @pl.when(jnp.logical_and(x == 3, u == 0))
        def _():
            left(hb, blk, fl_send).start()

        @pl.when(jnp.logical_and(jnp.logical_and(x == 2, u == 1), c == 0))
        def _():
            right(hb, blk, fr_send).start()

    def unit(j):
        return jnp.where(x == 3, lax.rem(2 * j, 3), x - 1 - j)

    def middle_unit(j):
        u = unit(j)
        for hb in range(2):
            arrive(u, hb)
        for hb in range(2):
            blk = 2 * u + hb
            share(blk).wait_recv()
            convert(blk)

            def step(g, carry):
                attend(g, blk, None)
                return carry

            lax.fori_loop(0, 4, step, 0)

    @pl.when(x >= 2)
    def _():
        middle_unit(0)

    for d in range(1, NX):

        @pl.when(x >= d)
        def _():
            from_x(d).wait_recv()

    before = jnp.zeros((4, 8, ND), F32)
    for xs in range(NX - 1):
        before = jnp.where(xs < x, xtot[xs, 4:5] * before + xtot[xs, 0:4], before)
    for zz in range(NZ):
        fin[zz] = pre[zz, 0:4] + pre[zz, 4:5] * before

    def to_block(d):
        k = lax.rem(z + d, NZ)
        return rcopy(fin.at[k], iin.at[z], f_send.at[d - 1], f_recv.at[d - 1], zid(d))

    def from_owner(d):
        return rcopy(fin.at[z], iin.at[lax.rem(z + NZ - d, NZ)], f_send.at[d - 1], f_recv.at[d - 1], zid(d))

    for d in (4, 3, 5, 2, 6, 1, 7):
        to_block(d).start()
    iin[z] = fin[z]

    @pl.when(x >= 3)
    def _():
        middle_unit(1)

    for d in range(1, NZ):
        from_owner(d).wait_recv()
    chip_in = iin[...]
    mine_s = sst[whole]
    theirs = part[...]
    second = jnp.where(c == 0, mine_s[:, 4:5], theirs[:, 4:5]) * chip_in + jnp.where(
        c == 0, mine_s[:, 0:4], theirs[:, 0:4]
    )
    dsend[...] = jnp.where(c == 0, second, chip_in)
    inc[whole] = jnp.where(c == 0, chip_in, second)

    def to_mate_in():
        return rcopy(dsend, inc.at[whole], d_send.at[0], d_recv.at[0], mate)

    to_mate_in().start()

    @pl.when(x >= 1)
    def _():
        u = unit(x - 1)
        for hb in range(2):
            arrive(u, hb)
        for hb in range(2):
            blk = 2 * u + hb
            share(blk).wait_recv()
            convert(blk)

    def last_unit(g):
        @pl.when(x >= 1)
        def _():
            u = unit(x - 1)

            def step(hb, carry):
                attend(g, 2 * u + hb, None)
                return carry

            lax.fori_loop(0, 2, step, 0)

    pick_r = lax.broadcasted_iota(jnp.int32, (8, 128), 0)
    pick = jnp.where(pick_r == lax.broadcasted_iota(jnp.int32, (8, 128), 1), 1.0, 0.0).astype(BF16)

    def sums(g):
        return jnp.sum(lrow[g], axis=1, keepdims=True)

    def turn(cols):
        rows = cols[0].shape[0]
        lane = lax.broadcasted_iota(jnp.int32, (rows, 128), 1)
        laid = jnp.zeros((rows, 128), F32)
        for k, col in enumerate(cols):
            for n, part_ in enumerate(parts3(col)):
                laid = jnp.where(lane == 3 * k + n, part_, laid)
        return bdot(pick, laid.astype(BF16), 1, 1)

    def pack_ml(g):
        mlsend[g - 1] = turn([mrow[g], jnp.broadcast_to(sums(g), (512, 128))])

    def ml_copy(g):
        k = g - 1
        return rcopy(mlsend.at[k], mlrecv.at[k], ml_send.at[k], ml_rsem.at[k], yid((-1, 1, 2)[k]))

    def acc_copy(g):
        k = g - 1
        return rcopy(acc.at[g], crecv.at[k], c_send.at[k], c_rsem.at[k], yid((-1, 1)[k]))

    def acc_far(k):
        return rcopy(acc.at[3, pl.ds(k * 256, 256), :], crelay.at[k], cr_send.at[k], cr_recv.at[k], yid((1, -1)[k]))

    def acc_far_on(k):
        return rcopy(crelay.at[k], crecv.at[2, pl.ds(k * 256, 256), :], cf_send.at[k], c_rsem.at[2 + k], yid((1, -1)[k]))

    last_unit(3)
    pack_ml(3)
    acc_far(0).start()
    acc_far(1).start()
    ml_copy(3).start()
    last_unit(1)
    pack_ml(1)
    acc_copy(1).start()
    ml_copy(1).start()
    last_unit(2)
    pack_ml(2)
    acc_copy(2).start()
    ml_copy(2).start()
    for k in range(2):
        acc_far(k).wait_recv()
        acc_far_on(k).start()
    last_unit(0)

    to_mate_in().wait_recv()
    carried = dot3(cc[...], inc[...].reshape(XW, ND), 1, 1)
    gated = (ybuf[...] + ecum[...] * carried) * silu(z_ref[...])
    ybuf[...] = gated
    sq = gated * gated
    sq = (sq[:, 0:128] + sq[:, 128:256]) + (sq[:, 256:384] + sq[:, 384:512])
    ss_own[...] = turn([jnp.broadcast_to(jnp.sum(sq, axis=1, keepdims=True), (TOK, 128))])

    def ss_copy(d):
        return rcopy(ss_own, ss_in.at[d - 1], ss_send.at[d - 1], ss_recv.at[d - 1], yid(d))

    for d in range(1, NY):
        ss_copy(d).start()

    for k in range(3):
        ml_copy(k + 1).wait_recv()
    ms = [mrow[0]]
    ls = [jnp.broadcast_to(sums(0), (512, 128))]
    back_r = lax.broadcasted_iota(jnp.int32, (8, 256), 0)
    back_c = lax.broadcasted_iota(jnp.int32, (8, 256), 1)
    back = jnp.where(back_r // 3 == back_c // 128, 1.0, 0.0).astype(BF16)
    for k in range(3):
        col = bdot(mlrecv[k].astype(BF16), back, 0, 0)
        ms.append(col[:, 0:128])
        ls.append(col[:, 128:256])
    top = jnp.maximum(jnp.maximum(ms[0], ms[1]), jnp.maximum(ms[2], ms[3]))
    ws = [jnp.exp2(m - top) for m in ms]
    den = ws[0] * ls[0] + ws[1] * ls[1] + ws[2] * ls[2] + ws[3] * ls[3]
    inv = 1.0 / den
    acc_copy(1).wait_recv()
    acc_copy(2).wait_recv()
    for k in range(2):
        acc_far_on(k).wait_recv()
    joined = acc[0] * (ws[0] * inv)
    for k in range(3):
        joined = joined + crecv[k] * (ws[k + 1] * inv)
    att_ref[:, 0:128] = joined[0:256]
    att_ref[:, 128:256] = joined[256:512]

    for d in range(1, NY):
        ss_copy(d).wait_recv()
    ss = jnp.concatenate([ss_own[...], ss_in[0], ss_in[1], ss_in[2]], axis=0).astype(BF16)
    every = jnp.where(lax.rem(lax.broadcasted_iota(jnp.int32, (32, 128), 0), 8) < 3, 1.0, 0.0).astype(BF16)
    strength = bdot(ss, every, 0, 0) / (XW * NY)
    strength = lax.rsqrt(strength + 1e-05)
    mix_ref[...] = ybuf[...] * jnp.concatenate([strength] * 4, axis=1) * gain_ref[...]

    @pl.when(i < NX * NZ * NC - 1)
    def _():
        for cpy in halos():
            cpy.wait_send()

    for s in range(1, 5):
        zplus(s).wait_send()
    for s in range(1, 4):
        zminus(s).wait_send()
    for k in range(2):
        q_up(k).wait_send()
        q_down(k).wait_send()
    q_relay_up().wait_send()
    q_relay_down().wait_send()
    to_mate().wait_send()
    for hb in range(2):
        share(2 * x + hb).wait_send()

        @pl.when(x < NX - 1)
        def _():
            right(hb, 2 * x + hb, r_send).wait_send()

        @pl.when(goes_left)
        def _():
            left(hb, 2 * x + hb, l_send).wait_send()

        for u in range(NX - 1):

            @pl.when(u < x)
            def _():
                share(2 * u + hb).wait_send()

        @pl.when(jnp.logical_or(x == 3, jnp.logical_and(x == 0, c == 1)))
        def _():
            left(hb, 2 + hb, fl_send).wait_send()

        @pl.when(jnp.logical_and(x == 2, c == 0))
        def _():
            right(hb, 2 + hb, fr_send).wait_send()

    for d in range(1, NZ):
        to_owner(d).wait_send()
        to_block(d).wait_send()
    for d in range(1, NX):

        @pl.when(x + d < NX)
        def _():
            to_x(d).wait_send()

    to_mate_in().wait_send()
    for g in range(1, 4):
        ml_copy(g).wait_send()
    for k in range(2):
        acc_copy(k + 1).wait_send()
        acc_far(k).wait_send()
        acc_far_on(k).wait_send()
    for d in range(1, NY):
        ss_copy(d).wait_send()


def vm(*shape, dtype=F32):
    return pltpu.VMEM(shape, dtype)


def dma(*shape):
    return pltpu.SemaphoreType.DMA(shape)


SCRATCH = [
    vm(3, 256, 256), vm(4, 512, 384, dtype=BF16), vm(8, 512, 256),
    vm(8, 512, 384, dtype=BF16), vm(8, 512, 256, dtype=BF16),
    vm(4, 512, 128), vm(4, 512, 128), vm(4, 512, 128),
    vm(3, 8, 512), vm(3, 8, 512), vm(3, 512, 128), vm(2, 256, 128),
    vm(2, TOK, 512), vm(8, XW), vm(8, ND), vm(8, ND), vm(TOK + 8, XW), vm(TOK + 8, ND), vm(TOK + 8, ND),
    vm(TOK, XW), vm(TOK, ND), vm(TOK, ND), vm(TOK, XW), vm(TOK, XW),
    vm(16, 5, 8, ND), vm(8, 5, 8, ND), vm(8, 5, 8, ND),
    vm(8, 5, 8, ND), vm(8, 5, 8, ND), vm(5, 8, ND), vm(4, 5, 8, ND),
    vm(8, 4, 8, ND), vm(8, 4, 8, ND), vm(8, 4, 8, ND), vm(16, 4, 8, ND),
    vm(8, TOK), vm(3, 8, TOK),
    dma(6), dma(3, 2), dma(3), dma(3), dma(2), dma(4), dma(4), dma(3), dma(3),
    dma(8), dma(8), dma(8), dma(2), dma(2), dma(2), dma(2),
    dma(1), dma(1), dma(7), dma(7), dma(3), dma(3), dma(7), dma(7), dma(1), dma(1),
    dma(3), dma(3), dma(2), dma(4), dma(2), dma(2), dma(2), dma(3), dma(3),
]


def on_device(
    ssm_x, ssm_z, ssm_b, ssm_c, step_sizes, a_log, conv_x, conv_b, conv_c, norm_gain,
    queries, keys, values,
):
    spec = pl.BlockSpec(memory_space=pltpu.VMEM)
    return pl.pallas_call(
        body,
        out_shape=(
            jax.ShapeDtypeStruct((TOK, XW), F32),
            jax.ShapeDtypeStruct((TOK, 256), F32),
        ),
        in_specs=[spec] * 13,
        out_specs=(spec, spec),
        scratch_shapes=SCRATCH,
        compiler_params=pltpu.CompilerParams(
            collective_id=0, has_side_effects=True, vmem_limit_bytes=60 * 1024 * 1024
        ),
        name="layer",
    )(
        ssm_x, ssm_z, ssm_b, ssm_c, step_sizes.T, a_log.reshape(1, HEADS), conv_x, conv_b, conv_c,
        norm_gain.reshape(1, XW), queries, keys, values,
    )


def solution(mesh):
    placed = (
        P("ctx", "head"),
        P("ctx", "head"),
        P("ctx", None),
        P("ctx", None),
        P("ctx", "head"),
        P("head"),
        P(None, "head"),
        P(),
        P(),
        P("head"),
        P("ctx", "head"),
        P("ctx", None),
        P("ctx", None),
    )
    return jax.shard_map(
        on_device,
        mesh=mesh,
        in_specs=placed,
        out_specs=(P("ctx", "head"), P("ctx", "head")),
        check_vma=False,
    )
```

```python
import math

import jax
import jax.numpy as jnp
from jax import lax
from jax.experimental import pallas as pl
from jax.experimental.pallas import tpu as pltpu
from jax.sharding import PartitionSpec as P

F32 = jnp.float32
BF16 = jnp.bfloat16
FLOOR = -1e30
MESH = pl.DeviceIdType.MESH
NY, NX, NZ, NC = 4, 4, 8, 2
TOK = 256
SHARD = TOK // NY
E = 128
PD = 64
ND = 256
HEADS = 8
XW = HEADS * PD


def split2(v):
    hi = v.astype(BF16)
    lo = (v - hi.astype(F32)).astype(BF16)
    return hi, lo


def bdot(a, b, ca, cb):
    return lax.dot_general(a, b, (((ca,), (cb,)), ((), ())), preferred_element_type=F32)


def dot3(a, b, ca, cb):
    ah, al = split2(a)
    bh, bl = split2(b)
    return bdot(ah, bh, ca, cb) + (bdot(ah, bl, ca, cb) + bdot(al, bh, ca, cb))


def parts3(v):
    hi = v.astype(BF16).astype(F32)
    mid = (v - hi).astype(BF16).astype(F32)
    low = (v - hi) - mid
    return hi, mid, low


def stack3(v):
    hi, mid, low = parts3(v)
    return jnp.concatenate([hi, mid, low, jnp.zeros_like(v)], axis=0).astype(BF16)


def silu(v):
    return v / (1.0 + jnp.exp(-v))


def body(
    x_ref, z_ref, b_ref, c_ref, dt_ref, alog_ref, wx_ref, wb_ref, wc_ref, gain_ref,
    q_ref, k_ref, v_ref,
    mix_ref, att_ref,
    qown, zv, qbuf, qs, kvbuf, kcat, vcat, acc, mrow, lrow, mlsend, mlrecv, crecv, crelay,
    bias_ref, halo_x, halo_b, halo_c, xp, bp, cp, xc, bc, cc, ybuf, ecum, sst, part, merged,
    rin, pre, tot, xtot, fin, iin, dsend, inc, ss_own, ss_in,
    in_sem, q_send, q_recv, halo_send, halo_recv, kv_sem, zp_send, zp_recv, zm_send, zm_recv,
    part_send, part_recv, x_recv, r_send, l_send, fr_send, fl_send,
    sp_send, sp_recv, a2a_send, a2a_recv, xt_send, xt_recv, f_send, f_recv, d_send, d_recv,
    ml_send, ml_rsem, c_send, c_rsem, cr_send, cr_recv, cf_send, ss_send, ss_recv,
):
    h = lax.axis_index("head")
    i = lax.axis_index("ctx")
    c = lax.rem(i, NC)
    z = lax.rem(i // NC, NZ)
    x = i // (NC * NZ)

    def at(xx, zz, c_):
        return (xx * NZ + zz) * NC + c_

    def yid(d):
        return (lax.rem(h + d + NY, NY), i)

    def zid(d):
        return (h, at(x, lax.rem(z + d + NZ, NZ), c))

    def xid(d):
        return (h, at(lax.rem(x + d + NX, NX), z, c))

    mate = (h, i + 1 - 2 * c)

    def rcopy(src, dst, ssem, rsem, dev):
        return pltpu.make_async_remote_copy(
            src_ref=src, dst_ref=dst, send_sem=ssem, recv_sem=rsem,
            device_id=dev, device_id_type=MESH,
        )

    body_rows = pl.ds(8, TOK)

    def load(n):
        src = (q_ref, b_ref, x_ref, c_ref, z_ref)[n]
        dst = (qown, bp.at[body_rows, :], xp.at[body_rows, :], cp.at[body_rows, :], zv)[n]
        return pltpu.make_async_copy(src, dst, in_sem.at[n])

    barrier = pltpu.get_barrier_semaphore()

    def hello(dev):
        pl.semaphore_signal(barrier, inc=1, device_id=dev, device_id_type=MESH)

    for d in range(1, NY):
        hello(yid(d))
    for d in range(1, NZ):
        hello(zid(d))
    for d in range(1, NX):
        hello(xid(d))
    hello(mate)

    @pl.when(i > 0)
    def _():
        hello((h, i - 1))

    @pl.when(i < NX * NZ * NC - 1)
    def _():
        hello((h, i + 1))

    own_a = 2 * x
    mine = pl.ds(c * 256, 256)

    def slot(n):
        return kvbuf.at[2 * x + n // 4, pl.ds(c * 256 + (n % 4) * SHARD, SHARD), :]

    def local_kv():
        ours = pl.ds(h * SHARD, SHARD)
        rows = pl.ds(c * 256, SHARD)
        return (
            pltpu.make_async_copy(k_ref.at[ours, :], kvbuf.at[own_a, rows, pl.ds(0, E)], kv_sem.at[0]),
            pltpu.make_async_copy(v_ref.at[ours, :], kvbuf.at[own_a, rows, pl.ds(E, E)], kv_sem.at[1]),
        )

    for cpy in local_kv():
        cpy.start()
    for n in range(5):
        load(n).start()
    for cpy in local_kv():
        cpy.wait()

    pl.semaphore_wait(
        barrier,
        (NY - 1) + (NZ - 1) + (NX - 1) + 1
        + jnp.where(i > 0, 1, 0) + jnp.where(i < NX * NZ * NC - 1, 1, 0),
    )

    def halo(k, src, dst):
        return rcopy(
            src.at[pl.ds(TOK - 8, 8), :], dst, halo_send.at[k], halo_recv.at[k], (h, i + 1)
        )

    def halos():
        return (halo(0, x_ref, halo_x), halo(1, b_ref, halo_b), halo(2, c_ref, halo_c))

    @pl.when(i < NX * NZ * NC - 1)
    def _():
        for cpy in halos():
            cpy.start()

    def zplus(s):
        return rcopy(slot(0 if s == 1 else 2 * s - 3), slot(2 * s - 1), zp_send.at[s - 1], zp_recv.at[s - 1], zid(1))

    def zminus(s):
        return rcopy(slot(0 if s == 1 else 2 * s - 2), slot(2 * s), zm_send.at[s - 1], zm_recv.at[s - 1], zid(-1))

    zplus(1).start()
    zminus(1).start()

    def qhalf(ref, k):
        return ref.at[pl.ds(k * 128, 128), :]

    def q_up(k):
        return rcopy(qhalf(q_ref, k), qbuf.at[0, pl.ds(k * 128, 128), :], q_send.at[k], q_recv.at[0, k], yid(1))

    def q_down(k):
        return rcopy(qhalf(q_ref, k), qbuf.at[1, pl.ds(k * 128, 128), :], q_send.at[2 + k], q_recv.at[1, k], yid(-1))

    def q_relay_up():
        return rcopy(qbuf.at[0, pl.ds(0, 128), :], qbuf.at[2, pl.ds(0, 128), :], q_send.at[4], q_recv.at[2, 0], yid(1))

    def q_relay_down():
        return rcopy(qbuf.at[1, pl.ds(128, 128), :], qbuf.at[2, pl.ds(128, 128), :], q_send.at[5], q_recv.at[2, 1], yid(-1))

    q_up(0).start()
    q_down(1).start()
    q_up(1).start()
    q_down(0).start()

    acc[...] = jnp.zeros_like(acc)
    lrow[...] = jnp.zeros_like(lrow)
    mrow[...] = jnp.full(mrow.shape, FLOOR, F32)

    qscale = math.log2(math.e) / math.sqrt(E)

    def load_q(g, src):
        for a in range(2):
            hi, lo = split2(src[:, a * E : (a + 1) * E] * qscale)
            qs[g, pl.ds(a * 256, 256), 0:128] = hi
            qs[g, pl.ds(a * 256, 256), 128:256] = lo
            qs[g, pl.ds(a * 256, 256), 256:384] = hi

    load(0).wait()
    load_q(0, qown[...])

    for hb in range(2):
        kidx = lax.broadcasted_iota(jnp.int32, (1, 512), 1)
        n = hb * 4 + lax.rem(kidx // SHARD, 4)
        rho = jnp.where(lax.rem(n, 2) == 1, -((n + 1) // 2), n // 2)
        kz = lax.rem(z + rho + NZ, NZ)
        kpos = at(x, kz, kidx // 256) * TOK + h * SHARD + lax.rem(kidx, SHARD)
        qpos = i * TOK + lax.broadcasted_iota(jnp.int32, (TOK, 512), 0)
        bias_ref[hb] = jnp.where(kpos <= qpos, 0.0, FLOOR)

    for n in range(1, 5):
        load(n).wait()

    @pl.when(i > 0)
    def _():
        for cpy in halos():
            cpy.wait_recv()
        xp[0:8, :] = halo_x[...]
        bp[0:8, :] = halo_b[...]
        cp[0:8, :] = halo_c[...]

    @pl.when(i == 0)
    def _():
        xp[0:8, :] = jnp.zeros((8, XW), F32)
        bp[0:8, :] = jnp.zeros((8, ND), F32)
        cp[0:8, :] = jnp.zeros((8, ND), F32)

    def conv(pad, w_ref):
        total = w_ref[0:1, :] * pad[pl.ds(5, TOK), :]
        for k in range(1, 4):
            total = total + w_ref[k : k + 1, :] * pad[pl.ds(5 + k, TOK), :]
        return silu(total)

    bc[...] = conv(bp, wb_ref)
    xc[...] = conv(xp, wx_ref)

    zplus(1).wait_recv()
    zplus(2).start()
    zminus(1).wait_recv()
    zminus(2).start()

    row_t = lax.broadcasted_iota(jnp.int32, (TOK, TOK), 0)
    col_t = lax.broadcasted_iota(jnp.int32, (TOK, TOK), 1)
    upper = jnp.where(row_t <= col_t, 1.0, 0.0).astype(BF16)
    eye = jnp.where(col_t == row_t, 1.0, 0.0).astype(BF16)
    spread_h = lax.broadcasted_iota(jnp.int32, (32, XW), 0)
    spread_c = lax.broadcasted_iota(jnp.int32, (32, XW), 1)
    expand = jnp.where(
        jnp.logical_and(spread_c // PD == spread_h % HEADS, spread_h < 3 * HEADS), 1.0, 0.0
    ).astype(BF16)

    def widen(rows):
        return bdot(stack3(rows), expand, 0, 0)

    head_r = lax.broadcasted_iota(jnp.int32, (HEADS, HEADS), 0)
    head_c = lax.broadcasted_iota(jnp.int32, (HEADS, HEADS), 1)
    rate = -jnp.exp(alog_ref[...])
    rate = jnp.sum(jnp.where(head_r == head_c, rate, 0.0), axis=1, keepdims=True)
    dt = dt_ref[...]
    c3 = bdot(stack3(dt * rate), upper, 1, 0)
    cum_t = c3[0:8] + c3[8:16] + c3[16:24]
    c3 = bdot(eye, stack3(cum_t), 1, 1)
    cum = c3[:, 0:8] + c3[:, 8:16] + c3[:, 16:24]
    towards = jnp.exp(cum_t[:, TOK - 1 : TOK] - cum_t) * dt
    own = dot3(xc[...] * widen(towards), bc[...], 0, 0)
    sst[:, 0:4, :, :] = own.reshape(16, 4, 8, ND)
    growth = jnp.broadcast_to(jnp.exp(cum_t[:, TOK - 1 : TOK]), (HEADS, ND))
    for hh in range(HEADS):
        g8 = jnp.broadcast_to(growth[hh : hh + 1, :], (8, ND))
        sst[2 * hh, 4, :, :] = g8
        sst[2 * hh + 1, 4, :, :] = g8

    def to_mate():
        return rcopy(sst.at[pl.ds(8 * (1 - c), 8)], part, sp_send.at[0], sp_recv.at[0], mate)

    to_mate().start()

    q_up(0).wait_recv()
    q_relay_up().start()
    q_down(1).wait_recv()
    q_relay_down().start()

    def kvrows(blk):
        return kvbuf.at[blk, mine, :]

    def share(blk):
        return rcopy(kvrows(blk), kvrows(blk), part_send.at[blk], part_recv.at[blk], mate)

    def right(hb, blk, sem):
        return rcopy(kvrows(blk), kvrows(blk), sem.at[hb], x_recv.at[blk], xid(1))

    def left(hb, blk, sem):
        return rcopy(kvrows(blk), kvrows(blk), sem.at[hb], x_recv.at[blk], xid(-1))

    goes_left = jnp.logical_or(x == 0, jnp.logical_and(x == 1, c == 1))

    def ready(hb):
        blk = 2 * x + hb
        share(blk).start()

        @pl.when(x < NX - 1)
        def _():
            right(hb, blk, r_send).start()

        @pl.when(goes_left)
        def _():
            left(hb, blk, l_send).start()

    zplus(2).wait_recv()
    zplus(3).start()
    ready(0)
    zminus(2).wait_recv()
    zminus(3).start()

    cc[...] = conv(cp, wc_ref)
    inter = dot3(cc[...], bc[...], 1, 1)
    dt_x = widen(dt)
    ecum[...] = widen(jnp.exp(cum_t))
    causal = col_t <= row_t
    first = lax.broadcasted_iota(jnp.int32, (TOK, 128), 1) < PD
    def inside(pair):
        lanes = pl.ds(pair * 128, 128)
        xd = xc[:, pair * 128 : (pair + 1) * 128] * dt_x[:, pair * 128 : (pair + 1) * 128]
        xd = jnp.concatenate(split2(xd), axis=1)
        outs = []
        for k in range(2):
            hh = 2 * pair + k
            gap = cum[:, hh : hh + 1] - cum_t[hh : hh + 1, :]
            mixing = inter * jnp.where(causal, jnp.exp(jnp.minimum(gap, 0.0)), 0.0)
            both = bdot(jnp.concatenate(split2(mixing), axis=0), xd, 1, 0)
            both = both[0:TOK] + both[TOK : 2 * TOK]
            outs.append(both[:, 0:128] + both[:, 128:256])
        ybuf[:, lanes] = jnp.where(first, outs[0], outs[1])

    inside(0)
    inside(1)

    zplus(3).wait_recv()
    zplus(4).start()
    zminus(3).wait_recv()

    to_mate().wait_recv()
    whole = pl.ds(8 * c, 8)
    mine_s = sst[whole]
    theirs = part[...]
    g_mine, g_theirs = mine_s[:, 4:5], theirs[:, 4:5]
    chip = jnp.where(
        c == 0, g_theirs * mine_s[:, 0:4] + theirs[:, 0:4], g_mine * theirs[:, 0:4] + mine_s[:, 0:4]
    )
    merged[:, 0:4] = chip
    merged[:, 4:5] = g_mine * g_theirs

    def to_owner(d):
        k = lax.rem(z + d, NZ)
        return rcopy(merged.at[k], rin.at[z], a2a_send.at[d - 1], a2a_recv.at[d - 1], zid(d))

    def from_peer(d):
        return rcopy(merged.at[z], rin.at[lax.rem(z + NZ - d, NZ)], a2a_send.at[d - 1], a2a_recv.at[d - 1], zid(d))

    for d in (4, 3, 5, 2, 6, 1, 7):
        to_owner(d).start()
    rin[z] = merged[z]

    def convert(blk):
        kv = kvbuf[blk]
        hi, lo = split2(kv[:, 0:E])
        kcat[blk, :, 0:128] = hi
        kcat[blk, :, 128:256] = hi
        kcat[blk, :, 256:384] = lo
        hi, lo = split2(kv[:, E : 2 * E])
        vcat[blk, :, 0:128] = hi
        vcat[blk, :, 128:256] = lo

    def attend(g, blk, hb):
        s = bdot(qs[g], kcat[blk], 1, 1)
        if hb is not None:
            bias = bias_ref[hb]
            s = s + jnp.concatenate([bias, bias], axis=0)
        m_old = mrow[g]
        m_new = jnp.maximum(m_old, jnp.max(s, axis=1, keepdims=True))
        alpha = jnp.exp2(m_old - m_new)
        p = jnp.exp2(s - jnp.concatenate([m_new] * 4, axis=1))
        lrow[g] = lrow[g] * alpha + ((p[:, 0:128] + p[:, 128:256]) + (p[:, 256:384] + p[:, 384:512]))
        o = bdot(jnp.concatenate(split2(p), axis=0), vcat[blk], 1, 0)
        o = o[0:512] + o[512:1024]
        acc[g] = acc[g] * alpha + (o[:, 0:128] + o[:, 128:256])
        mrow[g] = m_new

    def got(blk):
        return right(0, blk, fr_send)

    def relay(hb):
        @pl.when(jnp.logical_and(x == 0, c == 1))
        def _():
            got(2 + hb).wait_recv()
            left(hb, 2 + hb, fl_send).start()

    def turn_of(k):
        u3 = jnp.where(k < 4, 2 * lax.rem(k, 2), 1)
        hb3 = jnp.where(k < 4, k // 2, k - 4)
        u = jnp.where(x == 3, u3, jnp.where(x == 2, 1 - k // 2, 0))
        return u, jnp.where(x == 3, hb3, lax.rem(k, 2))

    def block_of(k):
        u, hb = turn_of(k)
        return 2 * u + hb

    def arrive(k):
        u, hb = turn_of(k)
        blk = 2 * u + hb
        got(blk).wait_recv()
        share(blk).start()

        @pl.when(jnp.logical_and(x == 3, u == 0))
        def _():
            left(hb, blk, fl_send).start()

        @pl.when(jnp.logical_and(jnp.logical_and(x == 2, u == 1), c == 0))
        def _():
            right(hb, blk, fr_send).start()

    share(2 * x).wait_recv()
    convert(2 * x)
    attend(0, 2 * x, 0)
    q_up(1).wait_recv()
    load_q(1, qbuf[0])
    attend(1, 2 * x, 0)
    zplus(4).wait_recv()
    ready(1)
    inside(2)
    inside(3)
    q_down(0).wait_recv()
    load_q(2, qbuf[1])
    attend(2, 2 * x, 0)

    for d in range(1, NZ):
        from_peer(d).wait_recv()
    run = jnp.zeros((4, 8, ND), F32)
    gprod = jnp.ones((1, 8, ND), F32)
    for zz in range(NZ):
        pre[zz, 0:4] = run
        pre[zz, 4:5] = gprod
        gz = rin[zz, 4:5]
        run = gz * run + rin[zz, 0:4]
        gprod = gprod * gz
    tot[0:4] = run
    tot[4:5] = gprod

    def to_x(d):
        return rcopy(tot, xtot.at[x], xt_send.at[d - 1], xt_recv.at[d - 1], (h, at(x + d, z, c)))

    def from_x(d):
        return rcopy(tot, xtot.at[x - d], xt_send.at[d - 1], xt_recv.at[d - 1], (h, at(x - d, z, c)))

    for d in range(1, NX):

        @pl.when(x + d < NX)
        def _():
            to_x(d).start()

    relay(0)
    q_relay_up().wait_recv()
    q_relay_down().wait_recv()
    load_q(3, qbuf[2])
    attend(3, 2 * x, 0)

    @pl.when(x >= 1)
    def _():
        arrive(0)

    share(2 * x + 1).wait_recv()
    convert(2 * x + 1)

    def own_b(g, carry):
        attend(g, 2 * x + 1, 1)
        return carry

    lax.fori_loop(0, 4, own_b, 0)
    relay(1)

    for d in range(1, NX):

        @pl.when(x >= d)
        def _():
            from_x(d).wait_recv()

    before = jnp.zeros((4, 8, ND), F32)
    for xs in range(NX - 1):
        before = jnp.where(xs < x, xtot[xs, 4:5] * before + xtot[xs, 0:4], before)
    for zz in range(NZ):
        fin[zz] = pre[zz, 0:4] + pre[zz, 4:5] * before

    def to_block(d):
        k = lax.rem(z + d, NZ)
        return rcopy(fin.at[k], iin.at[z], f_send.at[d - 1], f_recv.at[d - 1], zid(d))

    def from_owner(d):
        return rcopy(fin.at[z], iin.at[lax.rem(z + NZ - d, NZ)], f_send.at[d - 1], f_recv.at[d - 1], zid(d))

    for d in (4, 3, 5, 2, 6, 1, 7):
        to_block(d).start()
    iin[z] = fin[z]

    def other(k, carry):
        blk = block_of(k)
        share(blk).wait_recv()
        convert(blk)

        def step(g, inner):
            attend(g, blk, None)
            return inner

        lax.fori_loop(0, 2, step, 0)
        arrive(k + 1)
        lax.fori_loop(2, 4, step, 0)
        return carry

    lax.fori_loop(0, jnp.maximum(2 * x - 2, 0), other, 0)

    @pl.when(x >= 1)
    def _():
        arrive(2 * x - 1)

    for d in range(1, NZ):
        from_owner(d).wait_recv()
    chip_in = iin[...]
    mine_s = sst[whole]
    theirs = part[...]
    second = jnp.where(c == 0, mine_s[:, 4:5], theirs[:, 4:5]) * chip_in + jnp.where(
        c == 0, mine_s[:, 0:4], theirs[:, 0:4]
    )
    dsend[...] = jnp.where(c == 0, second, chip_in)
    inc[whole] = jnp.where(c == 0, chip_in, second)

    def to_mate_in():
        return rcopy(dsend, inc.at[whole], d_send.at[0], d_recv.at[0], mate)

    to_mate_in().start()

    @pl.when(x >= 1)
    def _():
        for k in (2 * x - 2, 2 * x - 1):
            blk = block_of(k)
            share(blk).wait_recv()
            convert(blk)

    def last_unit(g):
        @pl.when(x >= 1)
        def _():
            def step(k, carry):
                attend(g, block_of(k), None)
                return carry

            lax.fori_loop(2 * x - 2, 2 * x, step, 0)

    pick_r = lax.broadcasted_iota(jnp.int32, (8, 128), 0)
    pick = jnp.where(pick_r == lax.broadcasted_iota(jnp.int32, (8, 128), 1), 1.0, 0.0).astype(BF16)

    def sums(g):
        return jnp.sum(lrow[g], axis=1, keepdims=True)

    def turn(cols):
        rows = cols[0].shape[0]
        lane = lax.broadcasted_iota(jnp.int32, (rows, 128), 1)
        laid = jnp.zeros((rows, 128), F32)
        for k, col in enumerate(cols):
            for n, part_ in enumerate(parts3(col)):
                laid = jnp.where(lane == 3 * k + n, part_, laid)
        return bdot(pick, laid.astype(BF16), 1, 1)

    def pack_ml(g):
        mlsend[g - 1] = turn([mrow[g], jnp.broadcast_to(sums(g), (512, 128))])

    def ml_copy(g):
        k = g - 1
        return rcopy(mlsend.at[k], mlrecv.at[k], ml_send.at[k], ml_rsem.at[k], yid((-1, 1, 2)[k]))

    def acc_copy(g):
        k = g - 1
        return rcopy(acc.at[g], crecv.at[k], c_send.at[k], c_rsem.at[k], yid((-1, 1)[k]))

    def acc_far(k):
        return rcopy(acc.at[3, pl.ds(k * 256, 256), :], crelay.at[k], cr_send.at[k], cr_recv.at[k], yid((1, -1)[k]))

    def acc_far_on(k):
        return rcopy(crelay.at[k], crecv.at[2, pl.ds(k * 256, 256), :], cf_send.at[k], c_rsem.at[2 + k], yid((1, -1)[k]))

    last_unit(3)
    pack_ml(3)
    acc_far(0).start()
    acc_far(1).start()
    ml_copy(3).start()
    last_unit(1)
    pack_ml(1)
    acc_copy(1).start()
    ml_copy(1).start()
    last_unit(2)
    pack_ml(2)
    acc_copy(2).start()
    ml_copy(2).start()
    for k in range(2):
        acc_far(k).wait_recv()
        acc_far_on(k).start()
    last_unit(0)

    to_mate_in().wait_recv()
    carried = dot3(cc[...], inc[...].reshape(XW, ND), 1, 1)
    gated = (ybuf[...] + ecum[...] * carried) * silu(zv[...])
    ybuf[...] = gated
    sq = gated * gated
    sq = (sq[:, 0:128] + sq[:, 128:256]) + (sq[:, 256:384] + sq[:, 384:512])
    ss_own[...] = turn([jnp.broadcast_to(jnp.sum(sq, axis=1, keepdims=True), (TOK, 128))])

    def ss_copy(d):
        return rcopy(ss_own, ss_in.at[d - 1], ss_send.at[d - 1], ss_recv.at[d - 1], yid(d))

    for d in range(1, NY):
        ss_copy(d).start()

    for k in range(3):
        ml_copy(k + 1).wait_recv()
    ms = [mrow[0]]
    ls = [jnp.broadcast_to(sums(0), (512, 128))]
    back_r = lax.broadcasted_iota(jnp.int32, (8, 256), 0)
    back_c = lax.broadcasted_iota(jnp.int32, (8, 256), 1)
    back = jnp.where(back_r // 3 == back_c // 128, 1.0, 0.0).astype(BF16)
    for k in range(3):
        col = bdot(mlrecv[k].astype(BF16), back, 0, 0)
        ms.append(col[:, 0:128])
        ls.append(col[:, 128:256])
    top = jnp.maximum(jnp.maximum(ms[0], ms[1]), jnp.maximum(ms[2], ms[3]))
    ws = [jnp.exp2(m - top) for m in ms]
    den = ws[0] * ls[0] + ws[1] * ls[1] + ws[2] * ls[2] + ws[3] * ls[3]
    inv = 1.0 / den
    acc_copy(1).wait_recv()
    acc_copy(2).wait_recv()
    for k in range(2):
        acc_far_on(k).wait_recv()
    joined = acc[0] * (ws[0] * inv)
    for k in range(3):
        joined = joined + crecv[k] * (ws[k + 1] * inv)
    att_ref[:, 0:128] = joined[0:256]
    att_ref[:, 128:256] = joined[256:512]

    for d in range(1, NY):
        ss_copy(d).wait_recv()
    ss = jnp.concatenate([ss_own[...], ss_in[0], ss_in[1], ss_in[2]], axis=0).astype(BF16)
    every = jnp.where(lax.rem(lax.broadcasted_iota(jnp.int32, (32, 128), 0), 8) < 3, 1.0, 0.0).astype(BF16)
    strength = bdot(ss, every, 0, 0) / (XW * NY)
    strength = lax.rsqrt(strength + 1e-05)
    mix_ref[...] = ybuf[...] * jnp.concatenate([strength] * 4, axis=1) * gain_ref[...]

    @pl.when(i < NX * NZ * NC - 1)
    def _():
        for cpy in halos():
            cpy.wait_send()

    for s in range(1, 5):
        zplus(s).wait_send()
    for s in range(1, 4):
        zminus(s).wait_send()
    for k in range(2):
        q_up(k).wait_send()
        q_down(k).wait_send()
    q_relay_up().wait_send()
    q_relay_down().wait_send()
    to_mate().wait_send()
    for hb in range(2):
        share(2 * x + hb).wait_send()

        @pl.when(x < NX - 1)
        def _():
            right(hb, 2 * x + hb, r_send).wait_send()

        @pl.when(goes_left)
        def _():
            left(hb, 2 * x + hb, l_send).wait_send()

        for u in range(NX - 1):

            @pl.when(u < x)
            def _():
                share(2 * u + hb).wait_send()

        @pl.when(jnp.logical_or(x == 3, jnp.logical_and(x == 0, c == 1)))
        def _():
            left(hb, 2 + hb, fl_send).wait_send()

        @pl.when(jnp.logical_and(x == 2, c == 0))
        def _():
            right(hb, 2 + hb, fr_send).wait_send()

    for d in range(1, NZ):
        to_owner(d).wait_send()
        to_block(d).wait_send()
    for d in range(1, NX):

        @pl.when(x + d < NX)
        def _():
            to_x(d).wait_send()

    to_mate_in().wait_send()
    for g in range(1, 4):
        ml_copy(g).wait_send()
    for k in range(2):
        acc_copy(k + 1).wait_send()
        acc_far(k).wait_send()
        acc_far_on(k).wait_send()
    for d in range(1, NY):
        ss_copy(d).wait_send()


def vm(*shape, dtype=F32):
    return pltpu.VMEM(shape, dtype)


def dma(*shape):
    return pltpu.SemaphoreType.DMA(shape)


SCRATCH = [
    vm(256, 256), vm(TOK, XW), vm(3, 256, 256), vm(4, 512, 384, dtype=BF16), vm(8, 512, 256),
    vm(8, 512, 384, dtype=BF16), vm(8, 512, 256, dtype=BF16),
    vm(4, 512, 128), vm(4, 512, 128), vm(4, 512, 128),
    vm(3, 8, 512), vm(3, 8, 512), vm(3, 512, 128), vm(2, 256, 128),
    vm(2, TOK, 512), vm(8, XW), vm(8, ND), vm(8, ND), vm(TOK + 8, XW), vm(TOK + 8, ND), vm(TOK + 8, ND),
    vm(TOK, XW), vm(TOK, ND), vm(TOK, ND), vm(TOK, XW), vm(TOK, XW),
    vm(16, 5, 8, ND), vm(8, 5, 8, ND), vm(8, 5, 8, ND),
    vm(8, 5, 8, ND), vm(8, 5, 8, ND), vm(5, 8, ND), vm(4, 5, 8, ND),
    vm(8, 4, 8, ND), vm(8, 4, 8, ND), vm(8, 4, 8, ND), vm(16, 4, 8, ND),
    vm(8, TOK), vm(3, 8, TOK),
    dma(5), dma(6), dma(3, 2), dma(3), dma(3), dma(2), dma(4), dma(4), dma(3), dma(3),
    dma(8), dma(8), dma(8), dma(2), dma(2), dma(2), dma(2),
    dma(1), dma(1), dma(7), dma(7), dma(3), dma(3), dma(7), dma(7), dma(1), dma(1),
    dma(3), dma(3), dma(2), dma(4), dma(2), dma(2), dma(2), dma(3), dma(3),
]


def on_device(
    ssm_x, ssm_z, ssm_b, ssm_c, step_sizes, a_log, conv_x, conv_b, conv_c, norm_gain,
    queries, keys, values,
):
    spec = pl.BlockSpec(memory_space=pltpu.VMEM)
    anyw = pl.BlockSpec(memory_space=pl.ANY)
    return pl.pallas_call(
        body,
        out_shape=(
            jax.ShapeDtypeStruct((TOK, XW), F32),
            jax.ShapeDtypeStruct((TOK, 256), F32),
        ),
        in_specs=[anyw] * 4 + [spec] * 6 + [anyw] * 3,
        out_specs=(spec, spec),
        scratch_shapes=SCRATCH,
        compiler_params=pltpu.CompilerParams(
            collective_id=0, has_side_effects=True, vmem_limit_bytes=60 * 1024 * 1024
        ),
        name="layer",
    )(
        ssm_x, ssm_z, ssm_b, ssm_c, step_sizes.T, a_log.reshape(1, HEADS), conv_x, conv_b, conv_c,
        norm_gain.reshape(1, XW), queries, keys, values,
    )


def solution(mesh):
    placed = (
        P("ctx", "head"),
        P("ctx", "head"),
        P("ctx", None),
        P("ctx", None),
        P("ctx", "head"),
        P("head"),
        P(None, "head"),
        P(),
        P(),
        P("head"),
        P("ctx", "head"),
        P("ctx", None),
        P("ctx", None),
    )
    return jax.shard_map(
        on_device,
        mesh=mesh,
        in_specs=placed,
        out_specs=(P("ctx", "head"), P("ctx", "head")),
        check_vma=False,
    )
```

```python
import math

import jax
import jax.numpy as jnp
from jax import lax
from jax.experimental import pallas as pl
from jax.experimental.pallas import tpu as pltpu
from jax.sharding import PartitionSpec as P

F32 = jnp.float32
BF16 = jnp.bfloat16
FLOOR = -1e30
MESH = pl.DeviceIdType.MESH
NY, NX, NZ, NC = 4, 4, 8, 2
TOK = 256
SHARD = TOK // NY
E = 128
PD = 64
ND = 256
HEADS = 8
XW = HEADS * PD


def split2(v):
    hi = v.astype(BF16)
    lo = (v - hi.astype(F32)).astype(BF16)
    return hi, lo


def bdot(a, b, ca, cb):
    return lax.dot_general(a, b, (((ca,), (cb,)), ((), ())), preferred_element_type=F32)


def dot3(a, b, ca, cb):
    ah, al = split2(a)
    bh, bl = split2(b)
    return bdot(ah, bh, ca, cb) + (bdot(ah, bl, ca, cb) + bdot(al, bh, ca, cb))


def parts3(v):
    hi = v.astype(BF16).astype(F32)
    mid = (v - hi).astype(BF16).astype(F32)
    low = (v - hi) - mid
    return hi, mid, low


def stack3(v):
    hi, mid, low = parts3(v)
    return jnp.concatenate([hi, mid, low, jnp.zeros_like(v)], axis=0).astype(BF16)


def silu(v):
    return v / (1.0 + jnp.exp(-v))


def body(
    x_ref, z_ref, b_ref, c_ref, dt_ref, alog_ref, wx_ref, wb_ref, wc_ref, gain_ref,
    q_ref, k_ref, v_ref,
    mix_ref, att_ref,
    qown, zv, qbuf, qs, kvbuf, kcat, vcat, acc, mrow, lrow, mlsend, mlrecv, crecv, crelay,
    bias_ref, halo_x, halo_b, halo_c, xp, bp, cp, xc, bc, cc, ybuf, ecum, sst, part, merged,
    rin, pre, tot, xtot, fin, iin, dsend, inc, ss_own, ss_in,
    in_sem, q_send, q_recv, halo_send, halo_recv, kv_sem, z_send, z_recv,
    part_send, part_recv, x_recv, r_send, l_send, fr_send, fl_send,
    sp_send, sp_recv, a2a_send, a2a_recv, xt_send, xt_recv, f_send, f_recv, d_send, d_recv,
    ml_send, ml_rsem, c_send, c_rsem, cr_send, cr_recv, cf_send, ss_send, ss_recv,
):
    h = lax.axis_index("head")
    i = lax.axis_index("ctx")
    c = lax.rem(i, NC)
    z = lax.rem(i // NC, NZ)
    x = i // (NC * NZ)

    def at(xx, zz, c_):
        return (xx * NZ + zz) * NC + c_

    def yid(d):
        return (lax.rem(h + d + NY, NY), i)

    def zid(d):
        return (h, at(x, lax.rem(z + d + NZ, NZ), c))

    def xid(d):
        return (h, at(lax.rem(x + d + NX, NX), z, c))

    mate = (h, i + 1 - 2 * c)

    def rcopy(src, dst, ssem, rsem, dev):
        return pltpu.make_async_remote_copy(
            src_ref=src, dst_ref=dst, send_sem=ssem, recv_sem=rsem,
            device_id=dev, device_id_type=MESH,
        )

    body_rows = pl.ds(8, TOK)

    def load(n):
        src = (q_ref, b_ref, x_ref, c_ref, z_ref)[n]
        dst = (qown, bp.at[body_rows, :], xp.at[body_rows, :], cp.at[body_rows, :], zv)[n]
        return pltpu.make_async_copy(src, dst, in_sem.at[n])

    barrier = pltpu.get_barrier_semaphore()

    def hello(dev):
        pl.semaphore_signal(barrier, inc=1, device_id=dev, device_id_type=MESH)

    for d in range(1, NY):
        hello(yid(d))
    for d in range(1, NZ):
        hello(zid(d))
    for d in range(1, NX):
        hello(xid(d))
    hello(mate)

    @pl.when(i > 0)
    def _():
        hello((h, i - 1))

    @pl.when(i < NX * NZ * NC - 1)
    def _():
        hello((h, i + 1))

    own_a = 2 * x
    mine = pl.ds(c * 256, 256)

    def slot(n):
        return kvbuf.at[2 * x + n // 4, pl.ds(c * 256 + (n % 4) * SHARD, SHARD), :]

    def local_kv():
        ours = pl.ds(h * SHARD, SHARD)
        rows = pl.ds(c * 256, SHARD)
        return (
            pltpu.make_async_copy(k_ref.at[ours, :], kvbuf.at[own_a, rows, pl.ds(0, E)], kv_sem.at[0]),
            pltpu.make_async_copy(v_ref.at[ours, :], kvbuf.at[own_a, rows, pl.ds(E, E)], kv_sem.at[1]),
        )

    for cpy in local_kv():
        cpy.start()
    for n in range(5):
        load(n).start()
    for cpy in local_kv():
        cpy.wait()

    pl.semaphore_wait(
        barrier,
        (NY - 1) + (NZ - 1) + (NX - 1) + 1
        + jnp.where(i > 0, 1, 0) + jnp.where(i < NX * NZ * NC - 1, 1, 0),
    )

    def halo(k, src, dst):
        return rcopy(
            src.at[pl.ds(TOK - 8, 8), :], dst, halo_send.at[k], halo_recv.at[k], (h, i + 1)
        )

    def halos():
        return (halo(0, x_ref, halo_x), halo(1, b_ref, halo_b), halo(2, c_ref, halo_c))

    @pl.when(i < NX * NZ * NC - 1)
    def _():
        for cpy in halos():
            cpy.start()

    far_dir = 2 - 4 * c

    def zcopy(n):
        if n <= 4:
            src, to = slot(0), (1, -1, 2, -2)[n - 1]
        elif n < 7:
            src, to = slot(n - 2), (1, -1)[n - 5]
        else:
            src, to = slot(3 + c), far_dir
        return rcopy(src, slot(n), z_send.at[n - 1], z_recv.at[n - 1], zid(to))

    for n in range(1, 5):
        zcopy(n).start()

    def qhalf(ref, k):
        return ref.at[pl.ds(k * 128, 128), :]

    def q_up(k):
        return rcopy(qhalf(q_ref, k), qbuf.at[0, pl.ds(k * 128, 128), :], q_send.at[k], q_recv.at[0, k], yid(1))

    def q_down(k):
        return rcopy(qhalf(q_ref, k), qbuf.at[1, pl.ds(k * 128, 128), :], q_send.at[2 + k], q_recv.at[1, k], yid(-1))

    def q_relay_up():
        return rcopy(qbuf.at[0, pl.ds(0, 128), :], qbuf.at[2, pl.ds(0, 128), :], q_send.at[4], q_recv.at[2, 0], yid(1))

    def q_relay_down():
        return rcopy(qbuf.at[1, pl.ds(128, 128), :], qbuf.at[2, pl.ds(128, 128), :], q_send.at[5], q_recv.at[2, 1], yid(-1))

    q_up(0).start()
    q_down(1).start()
    q_up(1).start()
    q_down(0).start()

    acc[...] = jnp.zeros_like(acc)
    lrow[...] = jnp.zeros_like(lrow)
    mrow[...] = jnp.full(mrow.shape, FLOOR, F32)

    qscale = math.log2(math.e) / math.sqrt(E)

    def load_q(g, src):
        for a in range(2):
            hi, lo = split2(src[:, a * E : (a + 1) * E] * qscale)
            qs[g, pl.ds(a * 256, 256), 0:128] = hi
            qs[g, pl.ds(a * 256, 256), 128:256] = lo
            qs[g, pl.ds(a * 256, 256), 256:384] = hi

    load(0).wait()
    load_q(0, qown[...])

    for hb in range(2):
        kidx = lax.broadcasted_iota(jnp.int32, (1, 512), 1)
        n = hb * 4 + lax.rem(kidx // SHARD, 4)
        rho = jnp.where(lax.rem(n, 2) == 1, -((n + 1) // 2), n // 2)
        kz = lax.rem(z + rho + NZ, NZ)
        kpos = at(x, kz, kidx // 256) * TOK + h * SHARD + lax.rem(kidx, SHARD)
        qpos = i * TOK + lax.broadcasted_iota(jnp.int32, (TOK, 512), 0)
        bias_ref[hb] = jnp.where(kpos <= qpos, 0.0, FLOOR)

    for n in range(1, 5):
        load(n).wait()

    @pl.when(i > 0)
    def _():
        for cpy in halos():
            cpy.wait_recv()
        xp[0:8, :] = halo_x[...]
        bp[0:8, :] = halo_b[...]
        cp[0:8, :] = halo_c[...]

    @pl.when(i == 0)
    def _():
        xp[0:8, :] = jnp.zeros((8, XW), F32)
        bp[0:8, :] = jnp.zeros((8, ND), F32)
        cp[0:8, :] = jnp.zeros((8, ND), F32)

    def conv(pad, w_ref):
        total = w_ref[0:1, :] * pad[pl.ds(5, TOK), :]
        for k in range(1, 4):
            total = total + w_ref[k : k + 1, :] * pad[pl.ds(5 + k, TOK), :]
        return silu(total)

    bc[...] = conv(bp, wb_ref)
    xc[...] = conv(xp, wx_ref)

    row_t = lax.broadcasted_iota(jnp.int32, (TOK, TOK), 0)
    col_t = lax.broadcasted_iota(jnp.int32, (TOK, TOK), 1)
    upper = jnp.where(row_t <= col_t, 1.0, 0.0).astype(BF16)
    eye = jnp.where(col_t == row_t, 1.0, 0.0).astype(BF16)
    spread_h = lax.broadcasted_iota(jnp.int32, (32, XW), 0)
    spread_c = lax.broadcasted_iota(jnp.int32, (32, XW), 1)
    expand = jnp.where(
        jnp.logical_and(spread_c // PD == spread_h % HEADS, spread_h < 3 * HEADS), 1.0, 0.0
    ).astype(BF16)

    def widen(rows):
        return bdot(stack3(rows), expand, 0, 0)

    head_r = lax.broadcasted_iota(jnp.int32, (HEADS, HEADS), 0)
    head_c = lax.broadcasted_iota(jnp.int32, (HEADS, HEADS), 1)
    rate = -jnp.exp(alog_ref[...])
    rate = jnp.sum(jnp.where(head_r == head_c, rate, 0.0), axis=1, keepdims=True)
    dt = dt_ref[...]
    c3 = bdot(stack3(dt * rate), upper, 1, 0)
    cum_t = c3[0:8] + c3[8:16] + c3[16:24]
    c3 = bdot(eye, stack3(cum_t), 1, 1)
    cum = c3[:, 0:8] + c3[:, 8:16] + c3[:, 16:24]
    towards = jnp.exp(cum_t[:, TOK - 1 : TOK] - cum_t) * dt
    own = dot3(xc[...] * widen(towards), bc[...], 0, 0)
    sst[:, 0:4, :, :] = own.reshape(16, 4, 8, ND)
    growth = jnp.broadcast_to(jnp.exp(cum_t[:, TOK - 1 : TOK]), (HEADS, ND))
    for hh in range(HEADS):
        g8 = jnp.broadcast_to(growth[hh : hh + 1, :], (8, ND))
        sst[2 * hh, 4, :, :] = g8
        sst[2 * hh + 1, 4, :, :] = g8

    def to_mate():
        return rcopy(sst.at[pl.ds(8 * (1 - c), 8)], part, sp_send.at[0], sp_recv.at[0], mate)

    to_mate().start()

    q_up(0).wait_recv()
    q_relay_up().start()
    q_down(1).wait_recv()
    q_relay_down().start()

    def kvrows(blk):
        return kvbuf.at[blk, mine, :]

    def share(blk):
        return rcopy(kvrows(blk), kvrows(blk), part_send.at[blk], part_recv.at[blk], mate)

    def right(hb, blk, sem):
        return rcopy(kvrows(blk), kvrows(blk), sem.at[hb], x_recv.at[blk], xid(1))

    def left(hb, blk, sem):
        return rcopy(kvrows(blk), kvrows(blk), sem.at[hb], x_recv.at[blk], xid(-1))

    goes_left = jnp.logical_or(x == 0, jnp.logical_and(x == 1, c == 1))

    def ready(hb):
        blk = 2 * x + hb
        share(blk).start()

        @pl.when(x < NX - 1)
        def _():
            right(hb, blk, r_send).start()

        @pl.when(goes_left)
        def _():
            left(hb, blk, l_send).start()

    for n in range(1, 4):
        zcopy(n).wait_recv()
    ready(0)
    zcopy(5).start()
    zcopy(4).wait_recv()
    zcopy(6).start()
    zcopy(7).start()

    cc[...] = conv(cp, wc_ref)
    inter = dot3(cc[...], bc[...], 1, 1)
    dt_x = widen(dt)
    ecum[...] = widen(jnp.exp(cum_t))
    causal = col_t <= row_t
    first = lax.broadcasted_iota(jnp.int32, (TOK, 128), 1) < PD
    def inside(pair):
        lanes = pl.ds(pair * 128, 128)
        xd = xc[:, pair * 128 : (pair + 1) * 128] * dt_x[:, pair * 128 : (pair + 1) * 128]
        xd = jnp.concatenate(split2(xd), axis=1)
        outs = []
        for k in range(2):
            hh = 2 * pair + k
            gap = cum[:, hh : hh + 1] - cum_t[hh : hh + 1, :]
            mixing = inter * jnp.where(causal, jnp.exp(jnp.minimum(gap, 0.0)), 0.0)
            both = bdot(jnp.concatenate(split2(mixing), axis=0), xd, 1, 0)
            both = both[0:TOK] + both[TOK : 2 * TOK]
            outs.append(both[:, 0:128] + both[:, 128:256])
        ybuf[:, lanes] = jnp.where(first, outs[0], outs[1])

    inside(0)
    inside(1)

    to_mate().wait_recv()
    whole = pl.ds(8 * c, 8)
    mine_s = sst[whole]
    theirs = part[...]
    g_mine, g_theirs = mine_s[:, 4:5], theirs[:, 4:5]
    chip = jnp.where(
        c == 0, g_theirs * mine_s[:, 0:4] + theirs[:, 0:4], g_mine * theirs[:, 0:4] + mine_s[:, 0:4]
    )
    merged[:, 0:4] = chip
    merged[:, 4:5] = g_mine * g_theirs

    def to_owner(d):
        k = lax.rem(z + d, NZ)
        return rcopy(merged.at[k], rin.at[z], a2a_send.at[d - 1], a2a_recv.at[d - 1], zid(d))

    def from_peer(d):
        return rcopy(merged.at[z], rin.at[lax.rem(z + NZ - d, NZ)], a2a_send.at[d - 1], a2a_recv.at[d - 1], zid(d))

    for d in (4, 3, 5, 2, 6, 1, 7):
        to_owner(d).start()
    rin[z] = merged[z]

    def convert(blk):
        kv = kvbuf[blk]
        hi, lo = split2(kv[:, 0:E])
        kcat[blk, :, 0:128] = hi
        kcat[blk, :, 128:256] = hi
        kcat[blk, :, 256:384] = lo
        hi, lo = split2(kv[:, E : 2 * E])
        vcat[blk, :, 0:128] = hi
        vcat[blk, :, 128:256] = lo

    def attend(g, blk, hb):
        s = bdot(qs[g], kcat[blk], 1, 1)
        if hb is not None:
            bias = bias_ref[hb]
            s = s + jnp.concatenate([bias, bias], axis=0)
        m_old = mrow[g]
        m_new = jnp.maximum(m_old, jnp.max(s, axis=1, keepdims=True))
        alpha = jnp.exp2(m_old - m_new)
        p = jnp.exp2(s - jnp.concatenate([m_new] * 4, axis=1))
        lrow[g] = lrow[g] * alpha + ((p[:, 0:128] + p[:, 128:256]) + (p[:, 256:384] + p[:, 384:512]))
        o = bdot(jnp.concatenate(split2(p), axis=0), vcat[blk], 1, 0)
        o = o[0:512] + o[512:1024]
        acc[g] = acc[g] * alpha + (o[:, 0:128] + o[:, 128:256])
        mrow[g] = m_new

    def got(blk):
        return right(0, blk, fr_send)

    def relay(hb):
        @pl.when(jnp.logical_and(x == 0, c == 1))
        def _():
            got(2 + hb).wait_recv()
            left(hb, 2 + hb, fl_send).start()

    def turn_of(k):
        u3 = jnp.where(k < 4, 2 * lax.rem(k, 2), 1)
        hb3 = jnp.where(k < 4, k // 2, k - 4)
        u = jnp.where(x == 3, u3, jnp.where(x == 2, 1 - k // 2, 0))
        return u, jnp.where(x == 3, hb3, lax.rem(k, 2))

    def block_of(k):
        u, hb = turn_of(k)
        return 2 * u + hb

    def arrive(k):
        u, hb = turn_of(k)
        blk = 2 * u + hb
        got(blk).wait_recv()
        share(blk).start()

        @pl.when(jnp.logical_and(x == 3, u == 0))
        def _():
            left(hb, blk, fl_send).start()

        @pl.when(jnp.logical_and(jnp.logical_and(x == 2, u == 1), c == 0))
        def _():
            right(hb, blk, fr_send).start()

    share(2 * x).wait_recv()
    convert(2 * x)
    attend(0, 2 * x, 0)
    q_up(1).wait_recv()
    load_q(1, qbuf[0])
    attend(1, 2 * x, 0)
    for n in range(5, 8):
        zcopy(n).wait_recv()
    ready(1)
    inside(2)
    inside(3)
    q_down(0).wait_recv()
    load_q(2, qbuf[1])
    attend(2, 2 * x, 0)

    for d in range(1, NZ):
        from_peer(d).wait_recv()
    run = jnp.zeros((4, 8, ND), F32)
    gprod = jnp.ones((1, 8, ND), F32)
    for zz in range(NZ):
        pre[zz, 0:4] = run
        pre[zz, 4:5] = gprod
        gz = rin[zz, 4:5]
        run = gz * run + rin[zz, 0:4]
        gprod = gprod * gz
    tot[0:4] = run
    tot[4:5] = gprod

    def to_x(d):
        return rcopy(tot, xtot.at[x], xt_send.at[d - 1], xt_recv.at[d - 1], (h, at(x + d, z, c)))

    def from_x(d):
        return rcopy(tot, xtot.at[x - d], xt_send.at[d - 1], xt_recv.at[d - 1], (h, at(x - d, z, c)))

    for d in range(1, NX):

        @pl.when(x + d < NX)
        def _():
            to_x(d).start()

    relay(0)
    q_relay_up().wait_recv()
    q_relay_down().wait_recv()
    load_q(3, qbuf[2])
    attend(3, 2 * x, 0)

    @pl.when(x >= 1)
    def _():
        arrive(0)

    share(2 * x + 1).wait_recv()
    convert(2 * x + 1)

    def own_b(g, carry):
        attend(g, 2 * x + 1, 1)
        return carry

    lax.fori_loop(0, 4, own_b, 0)
    relay(1)

    for d in range(1, NX):

        @pl.when(x >= d)
        def _():
            from_x(d).wait_recv()

    before = jnp.zeros((4, 8, ND), F32)
    for xs in range(NX - 1):
        before = jnp.where(xs < x, xtot[xs, 4:5] * before + xtot[xs, 0:4], before)
    for zz in range(NZ):
        fin[zz] = pre[zz, 0:4] + pre[zz, 4:5] * before

    def to_block(d):
        k = lax.rem(z + d, NZ)
        return rcopy(fin.at[k], iin.at[z], f_send.at[d - 1], f_recv.at[d - 1], zid(d))

    def from_owner(d):
        return rcopy(fin.at[z], iin.at[lax.rem(z + NZ - d, NZ)], f_send.at[d - 1], f_recv.at[d - 1], zid(d))

    for d in (4, 3, 5, 2, 6, 1, 7):
        to_block(d).start()
    iin[z] = fin[z]

    def other(k, carry):
        blk = block_of(k)
        share(blk).wait_recv()
        convert(blk)

        def step(g, inner):
            attend(g, blk, None)
            return inner

        lax.fori_loop(1, 3, step, 0)
        arrive(k + 1)
        attend(3, blk, None)
        return carry

    lax.fori_loop(0, jnp.maximum(2 * x - 2, 0), other, 0)

    @pl.when(x >= 1)
    def _():
        arrive(2 * x - 1)

    for d in range(1, NZ):
        from_owner(d).wait_recv()
    chip_in = iin[...]
    mine_s = sst[whole]
    theirs = part[...]
    second = jnp.where(c == 0, mine_s[:, 4:5], theirs[:, 4:5]) * chip_in + jnp.where(
        c == 0, mine_s[:, 0:4], theirs[:, 0:4]
    )
    dsend[...] = jnp.where(c == 0, second, chip_in)
    inc[whole] = jnp.where(c == 0, chip_in, second)

    def to_mate_in():
        return rcopy(dsend, inc.at[whole], d_send.at[0], d_recv.at[0], mate)

    to_mate_in().start()

    @pl.when(x >= 1)
    def _():
        for k in (2 * x - 2, 2 * x - 1):
            blk = block_of(k)
            share(blk).wait_recv()
            convert(blk)

    def last_unit(g):
        @pl.when(x >= 1)
        def _():
            def step(k, carry):
                attend(g, block_of(k), None)
                return carry

            lax.fori_loop(2 * x - 2, 2 * x, step, 0)

    pick_r = lax.broadcasted_iota(jnp.int32, (8, 128), 0)
    pick = jnp.where(pick_r == lax.broadcasted_iota(jnp.int32, (8, 128), 1), 1.0, 0.0).astype(BF16)

    def sums(g):
        return jnp.sum(lrow[g], axis=1, keepdims=True)

    def turn(cols):
        rows = cols[0].shape[0]
        lane = lax.broadcasted_iota(jnp.int32, (rows, 128), 1)
        laid = jnp.zeros((rows, 128), F32)
        for k, col in enumerate(cols):
            for n, part_ in enumerate(parts3(col)):
                laid = jnp.where(lane == 3 * k + n, part_, laid)
        return bdot(pick, laid.astype(BF16), 1, 1)

    def pack_ml(g):
        mlsend[g - 1] = turn([mrow[g], jnp.broadcast_to(sums(g), (512, 128))])

    def ml_copy(g):
        k = g - 1
        return rcopy(mlsend.at[k], mlrecv.at[k], ml_send.at[k], ml_rsem.at[k], yid((-1, 1, 2)[k]))

    def acc_copy(g):
        k = g - 1
        return rcopy(acc.at[g], crecv.at[k], c_send.at[k], c_rsem.at[k], yid((-1, 1)[k]))

    def acc_far(k):
        return rcopy(acc.at[3, pl.ds(k * 256, 256), :], crelay.at[k], cr_send.at[k], cr_recv.at[k], yid((1, -1)[k]))

    def acc_far_on(k):
        return rcopy(crelay.at[k], crecv.at[2, pl.ds(k * 256, 256), :], cf_send.at[k], c_rsem.at[2 + k], yid((1, -1)[k]))

    last_unit(3)
    pack_ml(3)
    acc_far(0).start()
    acc_far(1).start()
    ml_copy(3).start()
    last_unit(1)
    pack_ml(1)
    acc_copy(1).start()
    ml_copy(1).start()
    last_unit(2)
    pack_ml(2)
    acc_copy(2).start()
    ml_copy(2).start()
    to_mate_in().wait_recv()
    carried = dot3(cc[...], inc[...].reshape(XW, ND), 1, 1)
    gated = (ybuf[...] + ecum[...] * carried) * silu(zv[...])
    ybuf[...] = gated
    sq = gated * gated
    sq = (sq[:, 0:128] + sq[:, 128:256]) + (sq[:, 256:384] + sq[:, 384:512])
    ss_own[...] = turn([jnp.broadcast_to(jnp.sum(sq, axis=1, keepdims=True), (TOK, 128))])

    def ss_copy(d):
        return rcopy(ss_own, ss_in.at[d - 1], ss_send.at[d - 1], ss_recv.at[d - 1], yid(d))

    for d in range(1, NY):
        ss_copy(d).start()

    def own_group(k, none):
        attend(0, block_of(k), None)
        return none

    lax.fori_loop(0, x, own_group, 0)
    for k in range(2):
        acc_far(k).wait_recv()
        acc_far_on(k).start()
    lax.fori_loop(x, 2 * x, own_group, 0)

    for k in range(3):
        ml_copy(k + 1).wait_recv()
    ms = [mrow[0]]
    ls = [jnp.broadcast_to(sums(0), (512, 128))]
    back_r = lax.broadcasted_iota(jnp.int32, (8, 256), 0)
    back_c = lax.broadcasted_iota(jnp.int32, (8, 256), 1)
    back = jnp.where(back_r // 3 == back_c // 128, 1.0, 0.0).astype(BF16)
    for k in range(3):
        col = bdot(mlrecv[k].astype(BF16), back, 0, 0)
        ms.append(col[:, 0:128])
        ls.append(col[:, 128:256])
    top = jnp.maximum(jnp.maximum(ms[0], ms[1]), jnp.maximum(ms[2], ms[3]))
    ws = [jnp.exp2(m - top) for m in ms]
    den = ws[0] * ls[0] + ws[1] * ls[1] + ws[2] * ls[2] + ws[3] * ls[3]
    inv = 1.0 / den
    acc_copy(1).wait_recv()
    acc_copy(2).wait_recv()
    for k in range(2):
        acc_far_on(k).wait_recv()
    joined = acc[0] * (ws[0] * inv)
    for k in range(3):
        joined = joined + crecv[k] * (ws[k + 1] * inv)
    att_ref[:, 0:128] = joined[0:256]
    att_ref[:, 128:256] = joined[256:512]

    for d in range(1, NY):
        ss_copy(d).wait_recv()
    ss = jnp.concatenate([ss_own[...], ss_in[0], ss_in[1], ss_in[2]], axis=0).astype(BF16)
    every = jnp.where(lax.rem(lax.broadcasted_iota(jnp.int32, (32, 128), 0), 8) < 3, 1.0, 0.0).astype(BF16)
    strength = bdot(ss, every, 0, 0) / (XW * NY)
    strength = lax.rsqrt(strength + 1e-05)
    mix_ref[...] = ybuf[...] * jnp.concatenate([strength] * 4, axis=1) * gain_ref[...]

    @pl.when(i < NX * NZ * NC - 1)
    def _():
        for cpy in halos():
            cpy.wait_send()

    for n in range(1, 8):
        zcopy(n).wait_send()
    for k in range(2):
        q_up(k).wait_send()
        q_down(k).wait_send()
    q_relay_up().wait_send()
    q_relay_down().wait_send()
    to_mate().wait_send()
    for hb in range(2):
        share(2 * x + hb).wait_send()

        @pl.when(x < NX - 1)
        def _():
            right(hb, 2 * x + hb, r_send).wait_send()

        @pl.when(goes_left)
        def _():
            left(hb, 2 * x + hb, l_send).wait_send()

        for u in range(NX - 1):

            @pl.when(u < x)
            def _():
                share(2 * u + hb).wait_send()

        @pl.when(jnp.logical_or(x == 3, jnp.logical_and(x == 0, c == 1)))
        def _():
            left(hb, 2 + hb, fl_send).wait_send()

        @pl.when(jnp.logical_and(x == 2, c == 0))
        def _():
            right(hb, 2 + hb, fr_send).wait_send()

    for d in range(1, NZ):
        to_owner(d).wait_send()
        to_block(d).wait_send()
    for d in range(1, NX):

        @pl.when(x + d < NX)
        def _():
            to_x(d).wait_send()

    to_mate_in().wait_send()
    for g in range(1, 4):
        ml_copy(g).wait_send()
    for k in range(2):
        acc_copy(k + 1).wait_send()
        acc_far(k).wait_send()
        acc_far_on(k).wait_send()
    for d in range(1, NY):
        ss_copy(d).wait_send()


def vm(*shape, dtype=F32):
    return pltpu.VMEM(shape, dtype)


def dma(*shape):
    return pltpu.SemaphoreType.DMA(shape)


SCRATCH = [
    vm(256, 256), vm(TOK, XW), vm(3, 256, 256), vm(4, 512, 384, dtype=BF16), vm(8, 512, 256),
    vm(8, 512, 384, dtype=BF16), vm(8, 512, 256, dtype=BF16),
    vm(4, 512, 128), vm(4, 512, 128), vm(4, 512, 128),
    vm(3, 8, 512), vm(3, 8, 512), vm(3, 512, 128), vm(2, 256, 128),
    vm(2, TOK, 512), vm(8, XW), vm(8, ND), vm(8, ND), vm(TOK + 8, XW), vm(TOK + 8, ND), vm(TOK + 8, ND),
    vm(TOK, XW), vm(TOK, ND), vm(TOK, ND), vm(TOK, XW), vm(TOK, XW),
    vm(16, 5, 8, ND), vm(8, 5, 8, ND), vm(8, 5, 8, ND),
    vm(8, 5, 8, ND), vm(8, 5, 8, ND), vm(5, 8, ND), vm(4, 5, 8, ND),
    vm(8, 4, 8, ND), vm(8, 4, 8, ND), vm(8, 4, 8, ND), vm(16, 4, 8, ND),
    vm(8, TOK), vm(3, 8, TOK),
    dma(5), dma(6), dma(3, 2), dma(3), dma(3), dma(2), dma(7), dma(7),
    dma(8), dma(8), dma(8), dma(2), dma(2), dma(2), dma(2),
    dma(1), dma(1), dma(7), dma(7), dma(3), dma(3), dma(7), dma(7), dma(1), dma(1),
    dma(3), dma(3), dma(2), dma(4), dma(2), dma(2), dma(2), dma(3), dma(3),
]


def on_device(
    ssm_x, ssm_z, ssm_b, ssm_c, step_sizes, a_log, conv_x, conv_b, conv_c, norm_gain,
    queries, keys, values,
):
    spec = pl.BlockSpec(memory_space=pltpu.VMEM)
    anyw = pl.BlockSpec(memory_space=pl.ANY)
    return pl.pallas_call(
        body,
        out_shape=(
            jax.ShapeDtypeStruct((TOK, XW), F32),
            jax.ShapeDtypeStruct((TOK, 256), F32),
        ),
        in_specs=[anyw] * 4 + [spec] * 6 + [anyw] * 3,
        out_specs=(spec, spec),
        scratch_shapes=SCRATCH,
        compiler_params=pltpu.CompilerParams(
            collective_id=0, has_side_effects=True, vmem_limit_bytes=60 * 1024 * 1024
        ),
        name="layer",
    )(
        ssm_x, ssm_z, ssm_b, ssm_c, step_sizes.T, a_log.reshape(1, HEADS), conv_x, conv_b, conv_c,
        norm_gain.reshape(1, XW), queries, keys, values,
    )


def solution(mesh):
    placed = (
        P("ctx", "head"),
        P("ctx", "head"),
        P("ctx", None),
        P("ctx", None),
        P("ctx", "head"),
        P("head"),
        P(None, "head"),
        P(),
        P(),
        P("head"),
        P("ctx", "head"),
        P("ctx", None),
        P("ctx", None),
    )
    return jax.shard_map(
        on_device,
        mesh=mesh,
        in_specs=placed,
        out_specs=(P("ctx", "head"), P("ctx", "head")),
        check_vma=False,
    )
```

```python
import math

import jax
import jax.numpy as jnp
from jax import lax
from jax.experimental import pallas as pl
from jax.experimental.pallas import tpu as pltpu
from jax.sharding import PartitionSpec as P

F32 = jnp.float32
BF16 = jnp.bfloat16
FLOOR = -1e30
MESH = pl.DeviceIdType.MESH
NY, NX, NZ, NC = 4, 4, 8, 2
TOK = 256
SHARD = TOK // NY
E = 128
PD = 64
ND = 256
HEADS = 8
XW = HEADS * PD


def split2(v):
    hi = v.astype(BF16)
    lo = (v - hi.astype(F32)).astype(BF16)
    return hi, lo


def bdot(a, b, ca, cb):
    return lax.dot_general(a, b, (((ca,), (cb,)), ((), ())), preferred_element_type=F32)


def dot3(a, b, ca, cb):
    ah, al = split2(a)
    bh, bl = split2(b)
    return bdot(ah, bh, ca, cb) + (bdot(ah, bl, ca, cb) + bdot(al, bh, ca, cb))


def parts3(v):
    hi = v.astype(BF16).astype(F32)
    mid = (v - hi).astype(BF16).astype(F32)
    low = (v - hi) - mid
    return hi, mid, low


def stack3(v):
    hi, mid, low = parts3(v)
    return jnp.concatenate([hi, mid, low, jnp.zeros_like(v)], axis=0).astype(BF16)


def silu(v):
    return v / (1.0 + jnp.exp(-v))


def body(
    x_ref, z_ref, b_ref, c_ref, dt_ref, alog_ref, wx_ref, wb_ref, wc_ref, gain_ref,
    q_ref, k_ref, v_ref,
    mix_ref, att_ref,
    qown, zv, qbuf, qs, kvbuf, kcat, vcat, acc, mrow, lrow, mlsend, mlrecv, crecv, crelay,
    bias_ref, halo_x, halo_b, halo_c, xp, bp, cp, xc, bc, cc, ybuf, ecum, sst, part, merged,
    rin, pre, tot, xtot, fin, iin, dsend, inc, ss_own, ss_in,
    in_sem, q_send, q_recv, halo_send, halo_recv, kv_sem, z_send, z_recv,
    part_send, part_recv, x_recv, r_send, l_send, fr_send, fl_send,
    sp_send, sp_recv, a2a_send, a2a_recv, xt_send, xt_recv, f_send, f_recv, d_send, d_recv,
    ml_send, ml_rsem, c_send, c_rsem, cr_send, cr_recv, cf_send, ss_send, ss_recv,
):
    h = lax.axis_index("head")
    i = lax.axis_index("ctx")
    c = lax.rem(i, NC)
    z = lax.rem(i // NC, NZ)
    x = i // (NC * NZ)

    def at(xx, zz, c_):
        return (xx * NZ + zz) * NC + c_

    def yid(d):
        return (lax.rem(h + d + NY, NY), i)

    def zid(d):
        return (h, at(x, lax.rem(z + d + NZ, NZ), c))

    def xid(d):
        return (h, at(lax.rem(x + d + NX, NX), z, c))

    mate = (h, i + 1 - 2 * c)

    def rcopy(src, dst, ssem, rsem, dev):
        return pltpu.make_async_remote_copy(
            src_ref=src, dst_ref=dst, send_sem=ssem, recv_sem=rsem,
            device_id=dev, device_id_type=MESH,
        )

    body_rows = pl.ds(8, TOK)

    def load(n):
        src = (q_ref, b_ref, x_ref, c_ref, z_ref)[n]
        dst = (qown, bp.at[body_rows, :], xp.at[body_rows, :], cp.at[body_rows, :], zv)[n]
        return pltpu.make_async_copy(src, dst, in_sem.at[n])

    barrier = pltpu.get_barrier_semaphore()

    def hello(dev):
        pl.semaphore_signal(barrier, inc=1, device_id=dev, device_id_type=MESH)

    for d in range(1, NY):
        hello(yid(d))
    for d in range(1, NZ):
        hello(zid(d))
    for d in range(1, NX):
        hello(xid(d))
    hello(mate)

    @pl.when(i > 0)
    def _():
        hello((h, i - 1))

    @pl.when(i < NX * NZ * NC - 1)
    def _():
        hello((h, i + 1))

    own_a = 2 * x
    mine = pl.ds(c * 256, 256)

    def slot(n):
        return kvbuf.at[2 * x + n // 4, pl.ds(c * 256 + (n % 4) * SHARD, SHARD), :]

    def local_kv():
        ours = pl.ds(h * SHARD, SHARD)
        rows = pl.ds(c * 256, SHARD)
        return (
            pltpu.make_async_copy(k_ref.at[ours, :], kvbuf.at[own_a, rows, pl.ds(0, E)], kv_sem.at[0]),
            pltpu.make_async_copy(v_ref.at[ours, :], kvbuf.at[own_a, rows, pl.ds(E, E)], kv_sem.at[1]),
        )

    for cpy in local_kv():
        cpy.start()
    for n in range(5):
        load(n).start()
    for cpy in local_kv():
        cpy.wait()

    pl.semaphore_wait(
        barrier,
        (NY - 1) + (NZ - 1) + (NX - 1) + 1
        + jnp.where(i > 0, 1, 0) + jnp.where(i < NX * NZ * NC - 1, 1, 0),
    )

    def halo(k, src, dst):
        return rcopy(
            src.at[pl.ds(TOK - 8, 8), :], dst, halo_send.at[k], halo_recv.at[k], (h, i + 1)
        )

    def halos():
        return (halo(0, x_ref, halo_x), halo(1, b_ref, halo_b), halo(2, c_ref, halo_c))

    @pl.when(i < NX * NZ * NC - 1)
    def _():
        for cpy in halos():
            cpy.start()

    far_dir = 2 - 4 * c

    def zcopy(n):
        if n <= 4:
            src, to = slot(0), (1, -1, 2, -2)[n - 1]
        elif n < 7:
            src, to = slot(n - 2), (1, -1)[n - 5]
        else:
            src, to = slot(3 + c), far_dir
        return rcopy(src, slot(n), z_send.at[n - 1], z_recv.at[n - 1], zid(to))

    for n in range(1, 5):
        zcopy(n).start()

    def qhalf(ref, k):
        return ref.at[pl.ds(k * 128, 128), :]

    def q_up(k):
        return rcopy(qhalf(q_ref, k), qbuf.at[0, pl.ds(k * 128, 128), :], q_send.at[k], q_recv.at[0, k], yid(1))

    def q_down(k):
        return rcopy(qhalf(q_ref, k), qbuf.at[1, pl.ds(k * 128, 128), :], q_send.at[2 + k], q_recv.at[1, k], yid(-1))

    def q_relay_up():
        return rcopy(qbuf.at[0, pl.ds(0, 128), :], qbuf.at[2, pl.ds(0, 128), :], q_send.at[4], q_recv.at[2, 0], yid(1))

    def q_relay_down():
        return rcopy(qbuf.at[1, pl.ds(128, 128), :], qbuf.at[2, pl.ds(128, 128), :], q_send.at[5], q_recv.at[2, 1], yid(-1))

    q_up(0).start()
    q_down(1).start()
    q_up(1).start()
    q_down(0).start()

    acc[...] = jnp.zeros_like(acc)
    lrow[...] = jnp.zeros_like(lrow)
    mrow[...] = jnp.full(mrow.shape, FLOOR, F32)

    qscale = math.log2(math.e) / math.sqrt(E)

    def load_q(g, src):
        for a in range(2):
            hi, lo = split2(src[:, a * E : (a + 1) * E] * qscale)
            qs[g, pl.ds(a * 256, 256), 0:128] = hi
            qs[g, pl.ds(a * 256, 256), 128:256] = lo
            qs[g, pl.ds(a * 256, 256), 256:384] = hi

    load(0).wait()
    load_q(0, qown[...])

    for hb in range(2):
        kidx = lax.broadcasted_iota(jnp.int32, (1, 512), 1)
        n = hb * 4 + lax.rem(kidx // SHARD, 4)
        rho = jnp.where(lax.rem(n, 2) == 1, -((n + 1) // 2), n // 2)
        kz = lax.rem(z + rho + NZ, NZ)
        kpos = at(x, kz, kidx // 256) * TOK + h * SHARD + lax.rem(kidx, SHARD)
        qpos = i * TOK + lax.broadcasted_iota(jnp.int32, (TOK, 512), 0)
        bias_ref[hb] = jnp.where(kpos <= qpos, 0.0, FLOOR)

    for n in range(1, 5):
        load(n).wait()

    @pl.when(i > 0)
    def _():
        for cpy in halos():
            cpy.wait_recv()
        xp[0:8, :] = halo_x[...]
        bp[0:8, :] = halo_b[...]
        cp[0:8, :] = halo_c[...]

    @pl.when(i == 0)
    def _():
        xp[0:8, :] = jnp.zeros((8, XW), F32)
        bp[0:8, :] = jnp.zeros((8, ND), F32)
        cp[0:8, :] = jnp.zeros((8, ND), F32)

    def conv(pad, w_ref):
        total = w_ref[0:1, :] * pad[pl.ds(5, TOK), :]
        for k in range(1, 4):
            total = total + w_ref[k : k + 1, :] * pad[pl.ds(5 + k, TOK), :]
        return silu(total)

    bc[...] = conv(bp, wb_ref)
    xc[...] = conv(xp, wx_ref)

    row_t = lax.broadcasted_iota(jnp.int32, (TOK, TOK), 0)
    col_t = lax.broadcasted_iota(jnp.int32, (TOK, TOK), 1)
    upper = jnp.where(row_t <= col_t, 1.0, 0.0).astype(BF16)
    eye = jnp.where(col_t == row_t, 1.0, 0.0).astype(BF16)
    spread_h = lax.broadcasted_iota(jnp.int32, (32, XW), 0)
    spread_c = lax.broadcasted_iota(jnp.int32, (32, XW), 1)
    expand = jnp.where(
        jnp.logical_and(spread_c // PD == spread_h % HEADS, spread_h < 3 * HEADS), 1.0, 0.0
    ).astype(BF16)

    def widen(rows):
        return bdot(stack3(rows), expand, 0, 0)

    head_r = lax.broadcasted_iota(jnp.int32, (HEADS, HEADS), 0)
    head_c = lax.broadcasted_iota(jnp.int32, (HEADS, HEADS), 1)
    rate = -jnp.exp(alog_ref[...])
    rate = jnp.sum(jnp.where(head_r == head_c, rate, 0.0), axis=1, keepdims=True)
    dt = dt_ref[...]
    c3 = bdot(stack3(dt * rate), upper, 1, 0)
    cum_t = c3[0:8] + c3[8:16] + c3[16:24]
    c3 = bdot(eye, stack3(cum_t), 1, 1)
    cum = c3[:, 0:8] + c3[:, 8:16] + c3[:, 16:24]
    towards = jnp.exp(cum_t[:, TOK - 1 : TOK] - cum_t) * dt
    own = dot3(xc[...] * widen(towards), bc[...], 0, 0)
    sst[:, 0:4, :, :] = own.reshape(16, 4, 8, ND)
    growth = jnp.broadcast_to(jnp.exp(cum_t[:, TOK - 1 : TOK]), (HEADS, ND))
    for hh in range(HEADS):
        g8 = jnp.broadcast_to(growth[hh : hh + 1, :], (8, ND))
        sst[2 * hh, 4, :, :] = g8
        sst[2 * hh + 1, 4, :, :] = g8

    def to_mate():
        return rcopy(sst.at[pl.ds(8 * (1 - c), 8)], part, sp_send.at[0], sp_recv.at[0], mate)

    to_mate().start()

    q_up(0).wait_recv()
    q_relay_up().start()
    q_down(1).wait_recv()
    q_relay_down().start()

    def kvrows(blk):
        return kvbuf.at[blk, mine, :]

    def share(blk):
        return rcopy(kvrows(blk), kvrows(blk), part_send.at[blk], part_recv.at[blk], mate)

    def right(hb, blk, sem):
        return rcopy(kvrows(blk), kvrows(blk), sem.at[hb], x_recv.at[blk], xid(1))

    def left(hb, blk, sem):
        return rcopy(kvrows(blk), kvrows(blk), sem.at[hb], x_recv.at[blk], xid(-1))

    goes_left = jnp.logical_or(x == 0, jnp.logical_and(x == 1, c == 1))

    def ready(hb):
        blk = 2 * x + hb
        share(blk).start()

        @pl.when(x < NX - 1)
        def _():
            right(hb, blk, r_send).start()

        @pl.when(goes_left)
        def _():
            left(hb, blk, l_send).start()

    for n in range(1, 4):
        zcopy(n).wait_recv()
    ready(0)
    zcopy(5).start()
    zcopy(4).wait_recv()
    zcopy(6).start()
    zcopy(7).start()

    cc[...] = conv(cp, wc_ref)
    inter = dot3(cc[...], bc[...], 1, 1)
    dt_x = widen(dt)
    ecum[...] = widen(jnp.exp(cum_t))
    causal = col_t <= row_t
    first = lax.broadcasted_iota(jnp.int32, (TOK, 128), 1) < PD
    def inside(pair):
        lanes = pl.ds(pair * 128, 128)
        xd = xc[:, pair * 128 : (pair + 1) * 128] * dt_x[:, pair * 128 : (pair + 1) * 128]
        xd = jnp.concatenate(split2(xd), axis=1)
        outs = []
        for k in range(2):
            hh = 2 * pair + k
            gap = cum[:, hh : hh + 1] - cum_t[hh : hh + 1, :]
            mixing = inter * jnp.where(causal, jnp.exp(jnp.minimum(gap, 0.0)), 0.0)
            both = bdot(jnp.concatenate(split2(mixing), axis=0), xd, 1, 0)
            both = both[0:TOK] + both[TOK : 2 * TOK]
            outs.append(both[:, 0:128] + both[:, 128:256])
        ybuf[:, lanes] = jnp.where(first, outs[0], outs[1])

    inside(0)
    inside(1)

    to_mate().wait_recv()
    whole = pl.ds(8 * c, 8)
    mine_s = sst[whole]
    theirs = part[...]
    g_mine, g_theirs = mine_s[:, 4:5], theirs[:, 4:5]
    chip = jnp.where(
        c == 0, g_theirs * mine_s[:, 0:4] + theirs[:, 0:4], g_mine * theirs[:, 0:4] + mine_s[:, 0:4]
    )
    merged[:, 0:4] = chip
    merged[:, 4:5] = g_mine * g_theirs

    def to_owner(d):
        k = lax.rem(z + d, NZ)
        return rcopy(merged.at[k], rin.at[z], a2a_send.at[d - 1], a2a_recv.at[d - 1], zid(d))

    def from_peer(d):
        return rcopy(merged.at[z], rin.at[lax.rem(z + NZ - d, NZ)], a2a_send.at[d - 1], a2a_recv.at[d - 1], zid(d))

    for d in (4, 3, 5, 2, 6, 1, 7):
        to_owner(d).start()
    rin[z] = merged[z]

    def convert(blk):
        kv = kvbuf[blk]
        hi, lo = split2(kv[:, 0:E])
        kcat[blk, :, 0:128] = hi
        kcat[blk, :, 128:256] = hi
        kcat[blk, :, 256:384] = lo
        hi, lo = split2(kv[:, E : 2 * E])
        vcat[blk, :, 0:128] = hi
        vcat[blk, :, 128:256] = lo

    def attend(g, blk, hb):
        s = bdot(qs[g], kcat[blk], 1, 1)
        if hb is not None:
            bias = bias_ref[hb]
            s = s + jnp.concatenate([bias, bias], axis=0)
        m_old = mrow[g]
        m_new = jnp.maximum(m_old, jnp.max(s, axis=1, keepdims=True))
        alpha = jnp.exp2(m_old - m_new)
        p = jnp.exp2(s - jnp.concatenate([m_new] * 4, axis=1))
        lrow[g] = lrow[g] * alpha + ((p[:, 0:128] + p[:, 128:256]) + (p[:, 256:384] + p[:, 384:512]))
        o = bdot(jnp.concatenate(split2(p), axis=0), vcat[blk], 1, 0)
        o = o[0:512] + o[512:1024]
        acc[g] = acc[g] * alpha + (o[:, 0:128] + o[:, 128:256])
        mrow[g] = m_new

    def got(blk):
        return right(0, blk, fr_send)

    def relay(hb):
        @pl.when(jnp.logical_and(x == 0, c == 1))
        def _():
            got(2 + hb).wait_recv()
            left(hb, 2 + hb, fl_send).start()

    def turn_of(k):
        u3 = jnp.where(k < 4, 2 * lax.rem(k, 2), 1)
        hb3 = jnp.where(k < 4, k // 2, k - 4)
        u = jnp.where(x == 3, u3, jnp.where(x == 2, 1 - k // 2, 0))
        return u, jnp.where(x == 3, hb3, lax.rem(k, 2))

    def block_of(k):
        u, hb = turn_of(k)
        return 2 * u + hb

    def arrive(k):
        u, hb = turn_of(k)
        blk = 2 * u + hb
        got(blk).wait_recv()
        share(blk).start()

        @pl.when(jnp.logical_and(x == 3, u == 0))
        def _():
            left(hb, blk, fl_send).start()

        @pl.when(jnp.logical_and(jnp.logical_and(x == 2, u == 1), c == 0))
        def _():
            right(hb, blk, fr_send).start()

    share(2 * x).wait_recv()
    convert(2 * x)
    attend(0, 2 * x, 0)
    q_up(1).wait_recv()
    load_q(1, qbuf[0])
    attend(1, 2 * x, 0)
    for n in range(5, 8):
        zcopy(n).wait_recv()
    ready(1)
    inside(2)
    inside(3)
    q_down(0).wait_recv()
    load_q(2, qbuf[1])
    attend(2, 2 * x, 0)

    relay(0)
    q_relay_up().wait_recv()
    q_relay_down().wait_recv()
    load_q(3, qbuf[2])
    attend(3, 2 * x, 0)

    @pl.when(x >= 1)
    def _():
        arrive(0)

    share(2 * x + 1).wait_recv()
    convert(2 * x + 1)

    def own_b(g, carry):
        attend(g, 2 * x + 1, 1)
        return carry

    lax.fori_loop(0, 4, own_b, 0)
    relay(1)

    @pl.when(x >= 1)
    def _():
        arrive(1)

    for d in range(1, NZ):
        from_peer(d).wait_recv()
    run = jnp.zeros((4, 8, ND), F32)
    gprod = jnp.ones((1, 8, ND), F32)
    for zz in range(NZ):
        pre[zz, 0:4] = run
        pre[zz, 4:5] = gprod
        gz = rin[zz, 4:5]
        run = gz * run + rin[zz, 0:4]
        gprod = gprod * gz
    tot[0:4] = run
    tot[4:5] = gprod

    def to_x(d):
        return rcopy(tot, xtot.at[x], xt_send.at[d - 1], xt_recv.at[d - 1], (h, at(x + d, z, c)))

    def from_x(d):
        return rcopy(tot, xtot.at[x - d], xt_send.at[d - 1], xt_recv.at[d - 1], (h, at(x - d, z, c)))

    for d in range(1, NX):

        @pl.when(x + d < NX)
        def _():
            to_x(d).start()

    def to_block(d):
        k = lax.rem(z + d, NZ)
        return rcopy(fin.at[k], iin.at[z], f_send.at[d - 1], f_recv.at[d - 1], zid(d))

    def from_owner(d):
        return rcopy(fin.at[z], iin.at[lax.rem(z + NZ - d, NZ)], f_send.at[d - 1], f_recv.at[d - 1], zid(d))

    def hand_back():
        for d in range(1, NX):

            @pl.when(x >= d)
            def _():
                from_x(d).wait_recv()

        before = jnp.zeros((4, 8, ND), F32)
        for xs in range(NX - 1):
            before = jnp.where(xs < x, xtot[xs, 4:5] * before + xtot[xs, 0:4], before)
        for zz in range(NZ):
            fin[zz] = pre[zz, 0:4] + pre[zz, 4:5] * before

        for d in (4, 3, 5, 2, 6, 1, 7):
            to_block(d).start()
        iin[z] = fin[z]


    def other(k, carry):
        blk = block_of(k)
        share(blk).wait_recv()
        convert(blk)

        def step(g, inner):
            attend(g, blk, None)
            return inner

        lax.fori_loop(1, 3, step, 0)
        arrive(k + 2)
        attend(3, blk, None)

        @pl.when(k == 0)
        def _():
            hand_back()

        return carry

    lax.fori_loop(0, jnp.maximum(2 * x - 2, 0), other, 0)

    @pl.when(x < 2)
    def _():
        hand_back()

    @pl.when(x >= 1)
    def _():
        for k in (2 * x - 2, 2 * x - 1):
            blk = block_of(k)
            share(blk).wait_recv()
            convert(blk)

    def last_unit(g):
        @pl.when(x >= 1)
        def _():
            def step(k, carry):
                attend(g, block_of(k), None)
                return carry

            lax.fori_loop(2 * x - 2, 2 * x, step, 0)

    pick_r = lax.broadcasted_iota(jnp.int32, (8, 128), 0)
    pick = jnp.where(pick_r == lax.broadcasted_iota(jnp.int32, (8, 128), 1), 1.0, 0.0).astype(BF16)

    def sums(g):
        return jnp.sum(lrow[g], axis=1, keepdims=True)

    def turn(cols):
        rows = cols[0].shape[0]
        lane = lax.broadcasted_iota(jnp.int32, (rows, 128), 1)
        laid = jnp.zeros((rows, 128), F32)
        for k, col in enumerate(cols):
            for n, part_ in enumerate(parts3(col)):
                laid = jnp.where(lane == 3 * k + n, part_, laid)
        return bdot(pick, laid.astype(BF16), 1, 1)

    def pack_ml(g):
        mlsend[g - 1] = turn([mrow[g], jnp.broadcast_to(sums(g), (512, 128))])

    def ml_copy(g):
        k = g - 1
        return rcopy(mlsend.at[k], mlrecv.at[k], ml_send.at[k], ml_rsem.at[k], yid((-1, 1, 2)[k]))

    def acc_copy(g):
        k = g - 1
        return rcopy(acc.at[g], crecv.at[k], c_send.at[k], c_rsem.at[k], yid((-1, 1)[k]))

    def acc_far(k):
        return rcopy(acc.at[3, pl.ds(k * 256, 256), :], crelay.at[k], cr_send.at[k], cr_recv.at[k], yid((1, -1)[k]))

    def acc_far_on(k):
        return rcopy(crelay.at[k], crecv.at[2, pl.ds(k * 256, 256), :], cf_send.at[k], c_rsem.at[2 + k], yid((1, -1)[k]))

    last_unit(3)
    pack_ml(3)
    acc_far(0).start()
    acc_far(1).start()
    ml_copy(3).start()
    last_unit(1)
    pack_ml(1)
    acc_copy(1).start()
    ml_copy(1).start()
    for d in range(1, NZ):
        from_owner(d).wait_recv()
    chip_in = iin[...]
    mine_s = sst[whole]
    theirs = part[...]
    second = jnp.where(c == 0, mine_s[:, 4:5], theirs[:, 4:5]) * chip_in + jnp.where(
        c == 0, mine_s[:, 0:4], theirs[:, 0:4]
    )
    dsend[...] = jnp.where(c == 0, second, chip_in)
    inc[whole] = jnp.where(c == 0, chip_in, second)

    def to_mate_in():
        return rcopy(dsend, inc.at[whole], d_send.at[0], d_recv.at[0], mate)

    to_mate_in().start()

    last_unit(2)
    pack_ml(2)
    acc_copy(2).start()
    ml_copy(2).start()
    def own_group(k, none):
        attend(0, block_of(k), None)
        return none

    lax.fori_loop(0, x, own_group, 0)
    for k in range(2):
        acc_far(k).wait_recv()
        acc_far_on(k).start()

    to_mate_in().wait_recv()
    carried = dot3(cc[...], inc[...].reshape(XW, ND), 1, 1)
    gated = (ybuf[...] + ecum[...] * carried) * silu(zv[...])
    ybuf[...] = gated
    sq = gated * gated
    sq = (sq[:, 0:128] + sq[:, 128:256]) + (sq[:, 256:384] + sq[:, 384:512])
    ss_own[...] = turn([jnp.broadcast_to(jnp.sum(sq, axis=1, keepdims=True), (TOK, 128))])

    def ss_copy(d):
        return rcopy(ss_own, ss_in.at[d - 1], ss_send.at[d - 1], ss_recv.at[d - 1], yid(d))

    for d in range(1, NY):
        ss_copy(d).start()

    lax.fori_loop(x, 2 * x, own_group, 0)

    for k in range(3):
        ml_copy(k + 1).wait_recv()
    ms = [mrow[0]]
    ls = [jnp.broadcast_to(sums(0), (512, 128))]
    back_r = lax.broadcasted_iota(jnp.int32, (8, 256), 0)
    back_c = lax.broadcasted_iota(jnp.int32, (8, 256), 1)
    back = jnp.where(back_r // 3 == back_c // 128, 1.0, 0.0).astype(BF16)
    for k in range(3):
        col = bdot(mlrecv[k].astype(BF16), back, 0, 0)
        ms.append(col[:, 0:128])
        ls.append(col[:, 128:256])
    top = jnp.maximum(jnp.maximum(ms[0], ms[1]), jnp.maximum(ms[2], ms[3]))
    ws = [jnp.exp2(m - top) for m in ms]
    den = ws[0] * ls[0] + ws[1] * ls[1] + ws[2] * ls[2] + ws[3] * ls[3]
    inv = 1.0 / den
    acc_copy(1).wait_recv()
    acc_copy(2).wait_recv()
    for k in range(2):
        acc_far_on(k).wait_recv()
    joined = acc[0] * (ws[0] * inv)
    for k in range(3):
        joined = joined + crecv[k] * (ws[k + 1] * inv)
    att_ref[:, 0:128] = joined[0:256]
    att_ref[:, 128:256] = joined[256:512]

    for d in range(1, NY):
        ss_copy(d).wait_recv()
    ss = jnp.concatenate([ss_own[...], ss_in[0], ss_in[1], ss_in[2]], axis=0).astype(BF16)
    every = jnp.where(lax.rem(lax.broadcasted_iota(jnp.int32, (32, 128), 0), 8) < 3, 1.0, 0.0).astype(BF16)
    strength = bdot(ss, every, 0, 0) / (XW * NY)
    strength = lax.rsqrt(strength + 1e-05)
    mix_ref[...] = ybuf[...] * jnp.concatenate([strength] * 4, axis=1) * gain_ref[...]

    @pl.when(i < NX * NZ * NC - 1)
    def _():
        for cpy in halos():
            cpy.wait_send()

    for n in range(1, 8):
        zcopy(n).wait_send()
    for k in range(2):
        q_up(k).wait_send()
        q_down(k).wait_send()
    q_relay_up().wait_send()
    q_relay_down().wait_send()
    to_mate().wait_send()
    for hb in range(2):
        share(2 * x + hb).wait_send()

        @pl.when(x < NX - 1)
        def _():
            right(hb, 2 * x + hb, r_send).wait_send()

        @pl.when(goes_left)
        def _():
            left(hb, 2 * x + hb, l_send).wait_send()

        for u in range(NX - 1):

            @pl.when(u < x)
            def _():
                share(2 * u + hb).wait_send()

        @pl.when(jnp.logical_or(x == 3, jnp.logical_and(x == 0, c == 1)))
        def _():
            left(hb, 2 + hb, fl_send).wait_send()

        @pl.when(jnp.logical_and(x == 2, c == 0))
        def _():
            right(hb, 2 + hb, fr_send).wait_send()

    for d in range(1, NZ):
        to_owner(d).wait_send()
        to_block(d).wait_send()
    for d in range(1, NX):

        @pl.when(x + d < NX)
        def _():
            to_x(d).wait_send()

    to_mate_in().wait_send()
    for g in range(1, 4):
        ml_copy(g).wait_send()
    for k in range(2):
        acc_copy(k + 1).wait_send()
        acc_far(k).wait_send()
        acc_far_on(k).wait_send()
    for d in range(1, NY):
        ss_copy(d).wait_send()


def vm(*shape, dtype=F32):
    return pltpu.VMEM(shape, dtype)


def dma(*shape):
    return pltpu.SemaphoreType.DMA(shape)


SCRATCH = [
    vm(256, 256), vm(TOK, XW), vm(3, 256, 256), vm(4, 512, 384, dtype=BF16), vm(8, 512, 256),
    vm(8, 512, 384, dtype=BF16), vm(8, 512, 256, dtype=BF16),
    vm(4, 512, 128), vm(4, 512, 128), vm(4, 512, 128),
    vm(3, 8, 512), vm(3, 8, 512), vm(3, 512, 128), vm(2, 256, 128),
    vm(2, TOK, 512), vm(8, XW), vm(8, ND), vm(8, ND), vm(TOK + 8, XW), vm(TOK + 8, ND), vm(TOK + 8, ND),
    vm(TOK, XW), vm(TOK, ND), vm(TOK, ND), vm(TOK, XW), vm(TOK, XW),
    vm(16, 5, 8, ND), vm(8, 5, 8, ND), vm(8, 5, 8, ND),
    vm(8, 5, 8, ND), vm(8, 5, 8, ND), vm(5, 8, ND), vm(4, 5, 8, ND),
    vm(8, 4, 8, ND), vm(8, 4, 8, ND), vm(8, 4, 8, ND), vm(16, 4, 8, ND),
    vm(8, TOK), vm(3, 8, TOK),
    dma(5), dma(6), dma(3, 2), dma(3), dma(3), dma(2), dma(7), dma(7),
    dma(8), dma(8), dma(8), dma(2), dma(2), dma(2), dma(2),
    dma(1), dma(1), dma(7), dma(7), dma(3), dma(3), dma(7), dma(7), dma(1), dma(1),
    dma(3), dma(3), dma(2), dma(4), dma(2), dma(2), dma(2), dma(3), dma(3),
]


def on_device(
    ssm_x, ssm_z, ssm_b, ssm_c, step_sizes, a_log, conv_x, conv_b, conv_c, norm_gain,
    queries, keys, values,
):
    spec = pl.BlockSpec(memory_space=pltpu.VMEM)
    anyw = pl.BlockSpec(memory_space=pl.ANY)
    return pl.pallas_call(
        body,
        out_shape=(
            jax.ShapeDtypeStruct((TOK, XW), F32),
            jax.ShapeDtypeStruct((TOK, 256), F32),
        ),
        in_specs=[anyw] * 4 + [spec] * 6 + [anyw] * 3,
        out_specs=(spec, spec),
        scratch_shapes=SCRATCH,
        compiler_params=pltpu.CompilerParams(
            collective_id=0, has_side_effects=True, vmem_limit_bytes=60 * 1024 * 1024
        ),
        name="layer",
    )(
        ssm_x, ssm_z, ssm_b, ssm_c, step_sizes.T, a_log.reshape(1, HEADS), conv_x, conv_b, conv_c,
        norm_gain.reshape(1, XW), queries, keys, values,
    )


def solution(mesh):
    placed = (
        P("ctx", "head"),
        P("ctx", "head"),
        P("ctx", None),
        P("ctx", None),
        P("ctx", "head"),
        P("head"),
        P(None, "head"),
        P(),
        P(),
        P("head"),
        P("ctx", "head"),
        P("ctx", None),
        P("ctx", None),
    )
    return jax.shard_map(
        on_device,
        mesh=mesh,
        in_specs=placed,
        out_specs=(P("ctx", "head"), P("ctx", "head")),
        check_vma=False,
    )
```

```python
import math

import jax
import jax.numpy as jnp
from jax import lax
from jax.experimental import pallas as pl
from jax.experimental.pallas import tpu as pltpu
from jax.sharding import PartitionSpec as P

F32 = jnp.float32
BF16 = jnp.bfloat16
FLOOR = -1e30
MESH = pl.DeviceIdType.MESH
NY, NX, NZ, NC = 4, 4, 8, 2
TOK = 256
SHARD = TOK // NY
E = 128
PD = 64
ND = 256
HEADS = 8
XW = HEADS * PD


def split2(v):
    hi = v.astype(BF16)
    lo = (v - hi.astype(F32)).astype(BF16)
    return hi, lo


def bdot(a, b, ca, cb):
    return lax.dot_general(a, b, (((ca,), (cb,)), ((), ())), preferred_element_type=F32)


def dot3(a, b, ca, cb):
    ah, al = split2(a)
    bh, bl = split2(b)
    return bdot(ah, bh, ca, cb) + (bdot(ah, bl, ca, cb) + bdot(al, bh, ca, cb))


def parts3(v):
    hi = v.astype(BF16).astype(F32)
    mid = (v - hi).astype(BF16).astype(F32)
    low = (v - hi) - mid
    return hi, mid, low


def stack3(v):
    hi, mid, low = parts3(v)
    return jnp.concatenate([hi, mid, low, jnp.zeros_like(v)], axis=0).astype(BF16)


def silu(v):
    return v / (1.0 + jnp.exp(-v))


def body(
    x_ref, z_ref, b_ref, c_ref, dt_ref, alog_ref, wx_ref, wb_ref, wc_ref, gain_ref,
    q_ref, k_ref, v_ref,
    mix_ref, att_ref,
    qown, zv, qbuf, qs, kvbuf, kcat, vcat, acc, mrow, lrow, mlsend, mlrecv, crecv, crelay,
    bias_ref, halo_x, halo_b, halo_c, xp, bp, cp, xc, bc, cc, ybuf, ecum, sst, part, merged,
    rin, pre, tot, xtot, fin, iin, dsend, inc, ss_own, ss_in,
    in_sem, q_send, q_recv, halo_send, halo_recv, kv_sem, z_send, z_recv,
    part_send, part_recv, x_recv, r_send, l_send, fr_send, fl_send,
    sp_send, sp_recv, a2a_send, a2a_recv, xt_send, xt_recv, f_send, f_recv, d_send, d_recv,
    ml_send, ml_rsem, c_send, c_rsem, cr_send, cr_recv, cf_send, ss_send, ss_recv,
):
    h = lax.axis_index("head")
    i = lax.axis_index("ctx")
    c = lax.rem(i, NC)
    z = lax.rem(i // NC, NZ)
    x = i // (NC * NZ)

    def at(xx, zz, c_):
        return (xx * NZ + zz) * NC + c_

    def yid(d):
        return (lax.rem(h + d + NY, NY), i)

    def zid(d):
        return (h, at(x, lax.rem(z + d + NZ, NZ), c))

    def xid(d):
        return (h, at(lax.rem(x + d + NX, NX), z, c))

    mate = (h, i + 1 - 2 * c)

    def rcopy(src, dst, ssem, rsem, dev):
        return pltpu.make_async_remote_copy(
            src_ref=src, dst_ref=dst, send_sem=ssem, recv_sem=rsem,
            device_id=dev, device_id_type=MESH,
        )

    body_rows = pl.ds(8, TOK)

    def load(n):
        src = (q_ref, b_ref, x_ref, c_ref, z_ref)[n]
        dst = (qown, bp.at[body_rows, :], xp.at[body_rows, :], cp.at[body_rows, :], zv)[n]
        return pltpu.make_async_copy(src, dst, in_sem.at[n])

    barrier = pltpu.get_barrier_semaphore()

    def hello(dev):
        pl.semaphore_signal(barrier, inc=1, device_id=dev, device_id_type=MESH)

    for d in range(1, NY):
        hello(yid(d))
    for d in range(1, NZ):
        hello(zid(d))
    for d in range(1, NX):
        hello(xid(d))
    hello(mate)

    @pl.when(i > 0)
    def _():
        hello((h, i - 1))

    @pl.when(i < NX * NZ * NC - 1)
    def _():
        hello((h, i + 1))

    own_a = 2 * x
    mine = pl.ds(c * 256, 256)

    def slot(n):
        return kvbuf.at[2 * x + n // 4, pl.ds(c * 256 + (n % 4) * SHARD, SHARD), :]

    def local_kv():
        ours = pl.ds(h * SHARD, SHARD)
        rows = pl.ds(c * 256, SHARD)
        return (
            pltpu.make_async_copy(k_ref.at[ours, :], kvbuf.at[own_a, rows, pl.ds(0, E)], kv_sem.at[0]),
            pltpu.make_async_copy(v_ref.at[ours, :], kvbuf.at[own_a, rows, pl.ds(E, E)], kv_sem.at[1]),
        )

    for cpy in local_kv():
        cpy.start()
    for n in range(5):
        load(n).start()
    for cpy in local_kv():
        cpy.wait()

    pl.semaphore_wait(
        barrier,
        (NY - 1) + (NZ - 1) + (NX - 1) + 1
        + jnp.where(i > 0, 1, 0) + jnp.where(i < NX * NZ * NC - 1, 1, 0),
    )

    def halo(k, src, dst):
        return rcopy(
            src.at[pl.ds(TOK - 8, 8), :], dst, halo_send.at[k], halo_recv.at[k], (h, i + 1)
        )

    def halos():
        return (halo(0, x_ref, halo_x), halo(1, b_ref, halo_b), halo(2, c_ref, halo_c))

    @pl.when(i < NX * NZ * NC - 1)
    def _():
        for cpy in halos():
            cpy.start()

    far_dir = 2 - 4 * c

    def zcopy(n):
        if n <= 4:
            src, to = slot(0), (1, -1, 2, -2)[n - 1]
        elif n < 7:
            src, to = slot(n - 2), (1, -1)[n - 5]
        else:
            src, to = slot(3 + c), far_dir
        return rcopy(src, slot(n), z_send.at[n - 1], z_recv.at[n - 1], zid(to))

    for n in range(1, 5):
        zcopy(n).start()

    def qhalf(ref, k):
        return ref.at[pl.ds(k * 128, 128), :]

    def q_up(k):
        return rcopy(qhalf(q_ref, k), qbuf.at[0, pl.ds(k * 128, 128), :], q_send.at[k], q_recv.at[0, k], yid(1))

    def q_down(k):
        return rcopy(qhalf(q_ref, k), qbuf.at[1, pl.ds(k * 128, 128), :], q_send.at[2 + k], q_recv.at[1, k], yid(-1))

    def q_relay_up():
        return rcopy(qbuf.at[0, pl.ds(0, 128), :], qbuf.at[2, pl.ds(0, 128), :], q_send.at[4], q_recv.at[2, 0], yid(1))

    def q_relay_down():
        return rcopy(qbuf.at[1, pl.ds(128, 128), :], qbuf.at[2, pl.ds(128, 128), :], q_send.at[5], q_recv.at[2, 1], yid(-1))

    q_up(0).start()
    q_down(1).start()
    q_up(1).start()
    q_down(0).start()

    acc[...] = jnp.zeros_like(acc)
    lrow[...] = jnp.zeros_like(lrow)
    mrow[...] = jnp.full(mrow.shape, FLOOR, F32)

    qscale = math.log2(math.e) / math.sqrt(E)

    def load_q(g, src):
        for a in range(2):
            hi, lo = split2(src[:, a * E : (a + 1) * E] * qscale)
            qs[g, pl.ds(a * 256, 256), 0:128] = hi
            qs[g, pl.ds(a * 256, 256), 128:256] = lo
            qs[g, pl.ds(a * 256, 256), 256:384] = hi

    load(0).wait()
    load_q(0, qown[...])

    for hb in range(2):
        kidx = lax.broadcasted_iota(jnp.int32, (1, 512), 1)
        n = hb * 4 + lax.rem(kidx // SHARD, 4)
        rho = jnp.where(lax.rem(n, 2) == 1, -((n + 1) // 2), n // 2)
        kz = lax.rem(z + rho + NZ, NZ)
        kpos = at(x, kz, kidx // 256) * TOK + h * SHARD + lax.rem(kidx, SHARD)
        qpos = i * TOK + lax.broadcasted_iota(jnp.int32, (TOK, 512), 0)
        bias_ref[hb] = jnp.where(kpos <= qpos, 0.0, FLOOR)

    for n in range(1, 5):
        load(n).wait()

    @pl.when(i > 0)
    def _():
        for cpy in halos():
            cpy.wait_recv()
        xp[0:8, :] = halo_x[...]
        bp[0:8, :] = halo_b[...]
        cp[0:8, :] = halo_c[...]

    @pl.when(i == 0)
    def _():
        xp[0:8, :] = jnp.zeros((8, XW), F32)
        bp[0:8, :] = jnp.zeros((8, ND), F32)
        cp[0:8, :] = jnp.zeros((8, ND), F32)

    def conv(pad, w_ref):
        total = w_ref[0:1, :] * pad[pl.ds(5, TOK), :]
        for k in range(1, 4):
            total = total + w_ref[k : k + 1, :] * pad[pl.ds(5 + k, TOK), :]
        return silu(total)

    bc[...] = conv(bp, wb_ref)
    xc[...] = conv(xp, wx_ref)

    row_t = lax.broadcasted_iota(jnp.int32, (TOK, TOK), 0)
    col_t = lax.broadcasted_iota(jnp.int32, (TOK, TOK), 1)
    upper = jnp.where(row_t <= col_t, 1.0, 0.0).astype(BF16)
    eye = jnp.where(col_t == row_t, 1.0, 0.0).astype(BF16)
    spread_h = lax.broadcasted_iota(jnp.int32, (32, XW), 0)
    spread_c = lax.broadcasted_iota(jnp.int32, (32, XW), 1)
    expand = jnp.where(
        jnp.logical_and(spread_c // PD == spread_h % HEADS, spread_h < 3 * HEADS), 1.0, 0.0
    ).astype(BF16)

    def widen(rows):
        return bdot(stack3(rows), expand, 0, 0)

    head_r = lax.broadcasted_iota(jnp.int32, (HEADS, HEADS), 0)
    head_c = lax.broadcasted_iota(jnp.int32, (HEADS, HEADS), 1)
    rate = -jnp.exp(alog_ref[...])
    rate = jnp.sum(jnp.where(head_r == head_c, rate, 0.0), axis=1, keepdims=True)
    dt = dt_ref[...]
    c3 = bdot(stack3(dt * rate), upper, 1, 0)
    cum_t = c3[0:8] + c3[8:16] + c3[16:24]
    c3 = bdot(eye, stack3(cum_t), 1, 1)
    cum = c3[:, 0:8] + c3[:, 8:16] + c3[:, 16:24]
    towards = jnp.exp(cum_t[:, TOK - 1 : TOK] - cum_t) * dt
    own = dot3(xc[...] * widen(towards), bc[...], 0, 0)
    sst[:, 0:4, :, :] = own.reshape(16, 4, 8, ND)
    growth = jnp.broadcast_to(jnp.exp(cum_t[:, TOK - 1 : TOK]), (HEADS, ND))
    for hh in range(HEADS):
        g8 = jnp.broadcast_to(growth[hh : hh + 1, :], (8, ND))
        sst[2 * hh, 4, :, :] = g8
        sst[2 * hh + 1, 4, :, :] = g8

    def to_mate():
        return rcopy(sst.at[pl.ds(8 * (1 - c), 8)], part, sp_send.at[0], sp_recv.at[0], mate)

    to_mate().start()

    q_up(0).wait_recv()
    q_relay_up().start()
    q_down(1).wait_recv()
    q_relay_down().start()

    def kvrows(blk):
        return kvbuf.at[blk, mine, :]

    def share(blk):
        return rcopy(kvrows(blk), kvrows(blk), part_send.at[blk], part_recv.at[blk], mate)

    def right(hb, blk, sem):
        return rcopy(kvrows(blk), kvrows(blk), sem.at[hb], x_recv.at[blk], xid(1))

    def left(hb, blk, sem):
        return rcopy(kvrows(blk), kvrows(blk), sem.at[hb], x_recv.at[blk], xid(-1))

    goes_left = jnp.logical_or(x == 0, jnp.logical_and(x == 1, c == 1))

    def ready(hb):
        blk = 2 * x + hb
        share(blk).start()

        @pl.when(x < NX - 1)
        def _():
            right(hb, blk, r_send).start()

        @pl.when(goes_left)
        def _():
            left(hb, blk, l_send).start()

    for n in range(1, 4):
        zcopy(n).wait_recv()
    ready(0)
    zcopy(5).start()
    zcopy(4).wait_recv()
    zcopy(6).start()
    zcopy(7).start()

    cc[...] = conv(cp, wc_ref)
    inter = dot3(cc[...], bc[...], 1, 1)
    dt_x = widen(dt)
    ecum[...] = widen(jnp.exp(cum_t))
    causal = col_t <= row_t
    first = lax.broadcasted_iota(jnp.int32, (TOK, 128), 1) < PD
    def inside(pair):
        lanes = pl.ds(pair * 128, 128)
        xd = xc[:, pair * 128 : (pair + 1) * 128] * dt_x[:, pair * 128 : (pair + 1) * 128]
        xd = jnp.concatenate(split2(xd), axis=1)
        outs = []
        for k in range(2):
            hh = 2 * pair + k
            gap = cum[:, hh : hh + 1] - cum_t[hh : hh + 1, :]
            mixing = inter * jnp.where(causal, jnp.exp(jnp.minimum(gap, 0.0)), 0.0)
            both = bdot(jnp.concatenate(split2(mixing), axis=0), xd, 1, 0)
            both = both[0:TOK] + both[TOK : 2 * TOK]
            outs.append(both[:, 0:128] + both[:, 128:256])
        ybuf[:, lanes] = jnp.where(first, outs[0], outs[1])

    inside(0)
    inside(1)

    to_mate().wait_recv()
    whole = pl.ds(8 * c, 8)
    mine_s = sst[whole]
    theirs = part[...]
    g_mine, g_theirs = mine_s[:, 4:5], theirs[:, 4:5]
    chip = jnp.where(
        c == 0, g_theirs * mine_s[:, 0:4] + theirs[:, 0:4], g_mine * theirs[:, 0:4] + mine_s[:, 0:4]
    )
    merged[:, 0:4] = chip
    merged[:, 4:5] = g_mine * g_theirs

    def to_owner(d):
        k = lax.rem(z + d, NZ)
        return rcopy(merged.at[k], rin.at[z], a2a_send.at[d - 1], a2a_recv.at[d - 1], zid(d))

    def from_peer(d):
        return rcopy(merged.at[z], rin.at[lax.rem(z + NZ - d, NZ)], a2a_send.at[d - 1], a2a_recv.at[d - 1], zid(d))

    for d in (4, 3, 5, 2, 6, 1, 7):
        to_owner(d).start()
    rin[z] = merged[z]

    def convert(blk):
        kv = kvbuf[blk]
        hi, lo = split2(kv[:, 0:E])
        kcat[blk, :, 0:128] = hi
        kcat[blk, :, 128:256] = hi
        kcat[blk, :, 256:384] = lo
        hi, lo = split2(kv[:, E : 2 * E])
        vcat[blk, :, 0:128] = hi
        vcat[blk, :, 128:256] = lo

    def attend(g, blk, hb):
        s = bdot(qs[g], kcat[blk], 1, 1)
        if hb is not None:
            bias = bias_ref[hb]
            s = s + jnp.concatenate([bias, bias], axis=0)
        m_old = mrow[g]
        m_new = jnp.maximum(m_old, jnp.max(s, axis=1, keepdims=True))
        alpha = jnp.exp2(m_old - m_new)
        p = jnp.exp2(s - jnp.concatenate([m_new] * 4, axis=1))
        lrow[g] = lrow[g] * alpha + ((p[:, 0:128] + p[:, 128:256]) + (p[:, 256:384] + p[:, 384:512]))
        o = bdot(jnp.concatenate(split2(p), axis=0), vcat[blk], 1, 0)
        o = o[0:512] + o[512:1024]
        acc[g] = acc[g] * alpha + (o[:, 0:128] + o[:, 128:256])
        mrow[g] = m_new

    def got(blk):
        return right(0, blk, fr_send)

    def relay(hb):
        @pl.when(jnp.logical_and(x == 0, c == 1))
        def _():
            got(2 + hb).wait_recv()
            left(hb, 2 + hb, fl_send).start()

    def turn_of(k):
        u3 = jnp.where(k < 4, 2 * lax.rem(k, 2), 1)
        hb3 = jnp.where(k < 4, k // 2, k - 4)
        u = jnp.where(x == 3, u3, jnp.where(x == 2, 1 - k // 2, 0))
        return u, jnp.where(x == 3, hb3, lax.rem(k, 2))

    def block_of(k):
        u, hb = turn_of(k)
        return 2 * u + hb

    def arrive(k):
        u, hb = turn_of(k)
        blk = 2 * u + hb
        got(blk).wait_recv()
        share(blk).start()

        @pl.when(jnp.logical_and(x == 3, u == 0))
        def _():
            left(hb, blk, fl_send).start()

        @pl.when(jnp.logical_and(jnp.logical_and(x == 2, u == 1), c == 0))
        def _():
            right(hb, blk, fr_send).start()

    inside(2)
    inside(3)
    share(2 * x).wait_recv()
    convert(2 * x)
    attend(0, 2 * x, 0)
    q_up(1).wait_recv()
    load_q(1, qbuf[0])
    attend(1, 2 * x, 0)
    for n in range(5, 8):
        zcopy(n).wait_recv()
    ready(1)
    q_down(0).wait_recv()
    load_q(2, qbuf[1])
    attend(2, 2 * x, 0)

    relay(0)
    q_relay_up().wait_recv()
    q_relay_down().wait_recv()
    load_q(3, qbuf[2])
    attend(3, 2 * x, 0)

    @pl.when(x >= 1)
    def _():
        arrive(0)

    share(2 * x + 1).wait_recv()
    convert(2 * x + 1)

    def own_b(g, carry):
        attend(g, 2 * x + 1, 1)
        return carry

    lax.fori_loop(1, 4, own_b, 0)
    relay(1)

    @pl.when(x >= 1)
    def _():
        arrive(1)

    for d in range(1, NZ):
        from_peer(d).wait_recv()
    run = jnp.zeros((4, 8, ND), F32)
    gprod = jnp.ones((1, 8, ND), F32)
    for zz in range(NZ):
        pre[zz, 0:4] = run
        pre[zz, 4:5] = gprod
        gz = rin[zz, 4:5]
        run = gz * run + rin[zz, 0:4]
        gprod = gprod * gz
    tot[0:4] = run
    tot[4:5] = gprod

    def to_x(d):
        return rcopy(tot, xtot.at[x], xt_send.at[d - 1], xt_recv.at[d - 1], (h, at(x + d, z, c)))

    def from_x(d):
        return rcopy(tot, xtot.at[x - d], xt_send.at[d - 1], xt_recv.at[d - 1], (h, at(x - d, z, c)))

    for d in range(1, NX):

        @pl.when(x + d < NX)
        def _():
            to_x(d).start()

    def to_block(d):
        k = lax.rem(z + d, NZ)
        return rcopy(fin.at[k], iin.at[z], f_send.at[d - 1], f_recv.at[d - 1], zid(d))

    def from_owner(d):
        return rcopy(fin.at[z], iin.at[lax.rem(z + NZ - d, NZ)], f_send.at[d - 1], f_recv.at[d - 1], zid(d))

    def hand_back():
        for d in range(1, NX):

            @pl.when(x >= d)
            def _():
                from_x(d).wait_recv()

        before = jnp.zeros((4, 8, ND), F32)
        for xs in range(NX - 1):
            before = jnp.where(xs < x, xtot[xs, 4:5] * before + xtot[xs, 0:4], before)
        for zz in range(NZ):
            fin[zz] = pre[zz, 0:4] + pre[zz, 4:5] * before

        for d in (4, 3, 5, 2, 6, 1, 7):
            to_block(d).start()
        iin[z] = fin[z]


    def other(k, carry):
        blk = block_of(k)
        share(blk).wait_recv()
        convert(blk)

        def step(g, inner):
            attend(g, blk, None)
            return inner

        lax.fori_loop(1, 3, step, 0)
        arrive(k + 2)
        attend(3, blk, None)

        @pl.when(k == 0)
        def _():
            hand_back()

        return carry

    lax.fori_loop(0, jnp.maximum(2 * x - 2, 0), other, 0)

    @pl.when(x < 2)
    def _():
        hand_back()

    @pl.when(x >= 1)
    def _():
        for k in (2 * x - 2, 2 * x - 1):
            blk = block_of(k)
            share(blk).wait_recv()
            convert(blk)

    def last_unit(g):
        @pl.when(x >= 1)
        def _():
            def step(k, carry):
                attend(g, block_of(k), None)
                return carry

            lax.fori_loop(2 * x - 2, 2 * x, step, 0)

    pick_r = lax.broadcasted_iota(jnp.int32, (8, 128), 0)
    pick = jnp.where(pick_r == lax.broadcasted_iota(jnp.int32, (8, 128), 1), 1.0, 0.0).astype(BF16)

    def sums(g):
        return jnp.sum(lrow[g], axis=1, keepdims=True)

    def turn(cols):
        rows = cols[0].shape[0]
        lane = lax.broadcasted_iota(jnp.int32, (rows, 128), 1)
        laid = jnp.zeros((rows, 128), F32)
        for k, col in enumerate(cols):
            for n, part_ in enumerate(parts3(col)):
                laid = jnp.where(lane == 3 * k + n, part_, laid)
        return bdot(pick, laid.astype(BF16), 1, 1)

    def pack_ml(g):
        mlsend[g - 1] = turn([mrow[g], jnp.broadcast_to(sums(g), (512, 128))])

    def ml_copy(g):
        k = g - 1
        return rcopy(mlsend.at[k], mlrecv.at[k], ml_send.at[k], ml_rsem.at[k], yid((-1, 1, 2)[k]))

    def acc_copy(g):
        k = g - 1
        return rcopy(acc.at[g], crecv.at[k], c_send.at[k], c_rsem.at[k], yid((-1, 1)[k]))

    def acc_far(k):
        return rcopy(acc.at[3, pl.ds(k * 256, 256), :], crelay.at[k], cr_send.at[k], cr_recv.at[k], yid((1, -1)[k]))

    def acc_far_on(k):
        return rcopy(crelay.at[k], crecv.at[2, pl.ds(k * 256, 256), :], cf_send.at[k], c_rsem.at[2 + k], yid((1, -1)[k]))

    last_unit(3)
    pack_ml(3)
    acc_far(0).start()
    acc_far(1).start()
    ml_copy(3).start()
    last_unit(1)
    pack_ml(1)
    acc_copy(1).start()
    ml_copy(1).start()
    for d in range(1, NZ):
        from_owner(d).wait_recv()
    chip_in = iin[...]
    mine_s = sst[whole]
    theirs = part[...]
    second = jnp.where(c == 0, mine_s[:, 4:5], theirs[:, 4:5]) * chip_in + jnp.where(
        c == 0, mine_s[:, 0:4], theirs[:, 0:4]
    )
    dsend[...] = jnp.where(c == 0, second, chip_in)
    inc[whole] = jnp.where(c == 0, chip_in, second)

    def to_mate_in():
        return rcopy(dsend, inc.at[whole], d_send.at[0], d_recv.at[0], mate)

    to_mate_in().start()

    last_unit(2)
    pack_ml(2)
    acc_copy(2).start()
    ml_copy(2).start()
    def own_group(k, none):
        attend(0, block_of(k), None)
        return none

    attend(0, 2 * x + 1, 1)
    lax.fori_loop(0, x, own_group, 0)
    for k in range(2):
        acc_far(k).wait_recv()
        acc_far_on(k).start()

    to_mate_in().wait_recv()
    carried = dot3(cc[...], inc[...].reshape(XW, ND), 1, 1)
    gated = (ybuf[...] + ecum[...] * carried) * silu(zv[...])
    ybuf[...] = gated
    sq = gated * gated
    sq = (sq[:, 0:128] + sq[:, 128:256]) + (sq[:, 256:384] + sq[:, 384:512])
    ss_own[...] = turn([jnp.broadcast_to(jnp.sum(sq, axis=1, keepdims=True), (TOK, 128))])

    def ss_copy(d):
        return rcopy(ss_own, ss_in.at[d - 1], ss_send.at[d - 1], ss_recv.at[d - 1], yid(d))

    for d in range(1, NY):
        ss_copy(d).start()

    lax.fori_loop(x, 2 * x, own_group, 0)

    for k in range(3):
        ml_copy(k + 1).wait_recv()
    ms = [mrow[0]]
    ls = [jnp.broadcast_to(sums(0), (512, 128))]
    back_r = lax.broadcasted_iota(jnp.int32, (8, 256), 0)
    back_c = lax.broadcasted_iota(jnp.int32, (8, 256), 1)
    back = jnp.where(back_r // 3 == back_c // 128, 1.0, 0.0).astype(BF16)
    for k in range(3):
        col = bdot(mlrecv[k].astype(BF16), back, 0, 0)
        ms.append(col[:, 0:128])
        ls.append(col[:, 128:256])
    top = jnp.maximum(jnp.maximum(ms[0], ms[1]), jnp.maximum(ms[2], ms[3]))
    ws = [jnp.exp2(m - top) for m in ms]
    den = ws[0] * ls[0] + ws[1] * ls[1] + ws[2] * ls[2] + ws[3] * ls[3]
    inv = 1.0 / den
    acc_copy(1).wait_recv()
    acc_copy(2).wait_recv()
    for k in range(2):
        acc_far_on(k).wait_recv()
    joined = acc[0] * (ws[0] * inv)
    for k in range(3):
        joined = joined + crecv[k] * (ws[k + 1] * inv)
    att_ref[:, 0:128] = joined[0:256]
    att_ref[:, 128:256] = joined[256:512]

    for d in range(1, NY):
        ss_copy(d).wait_recv()
    ss = jnp.concatenate([ss_own[...], ss_in[0], ss_in[1], ss_in[2]], axis=0).astype(BF16)
    every = jnp.where(lax.rem(lax.broadcasted_iota(jnp.int32, (32, 128), 0), 8) < 3, 1.0, 0.0).astype(BF16)
    strength = bdot(ss, every, 0, 0) / (XW * NY)
    strength = lax.rsqrt(strength + 1e-05)
    mix_ref[...] = ybuf[...] * jnp.concatenate([strength] * 4, axis=1) * gain_ref[...]

    @pl.when(i < NX * NZ * NC - 1)
    def _():
        for cpy in halos():
            cpy.wait_send()

    for n in range(1, 8):
        zcopy(n).wait_send()
    for k in range(2):
        q_up(k).wait_send()
        q_down(k).wait_send()
    q_relay_up().wait_send()
    q_relay_down().wait_send()
    to_mate().wait_send()
    for hb in range(2):
        share(2 * x + hb).wait_send()

        @pl.when(x < NX - 1)
        def _():
            right(hb, 2 * x + hb, r_send).wait_send()

        @pl.when(goes_left)
        def _():
            left(hb, 2 * x + hb, l_send).wait_send()

        for u in range(NX - 1):

            @pl.when(u < x)
            def _():
                share(2 * u + hb).wait_send()

        @pl.when(jnp.logical_or(x == 3, jnp.logical_and(x == 0, c == 1)))
        def _():
            left(hb, 2 + hb, fl_send).wait_send()

        @pl.when(jnp.logical_and(x == 2, c == 0))
        def _():
            right(hb, 2 + hb, fr_send).wait_send()

    for d in range(1, NZ):
        to_owner(d).wait_send()
        to_block(d).wait_send()
    for d in range(1, NX):

        @pl.when(x + d < NX)
        def _():
            to_x(d).wait_send()

    to_mate_in().wait_send()
    for g in range(1, 4):
        ml_copy(g).wait_send()
    for k in range(2):
        acc_copy(k + 1).wait_send()
        acc_far(k).wait_send()
        acc_far_on(k).wait_send()
    for d in range(1, NY):
        ss_copy(d).wait_send()


def vm(*shape, dtype=F32):
    return pltpu.VMEM(shape, dtype)


def dma(*shape):
    return pltpu.SemaphoreType.DMA(shape)


SCRATCH = [
    vm(256, 256), vm(TOK, XW), vm(3, 256, 256), vm(4, 512, 384, dtype=BF16), vm(8, 512, 256),
    vm(8, 512, 384, dtype=BF16), vm(8, 512, 256, dtype=BF16),
    vm(4, 512, 128), vm(4, 512, 128), vm(4, 512, 128),
    vm(3, 8, 512), vm(3, 8, 512), vm(3, 512, 128), vm(2, 256, 128),
    vm(2, TOK, 512), vm(8, XW), vm(8, ND), vm(8, ND), vm(TOK + 8, XW), vm(TOK + 8, ND), vm(TOK + 8, ND),
    vm(TOK, XW), vm(TOK, ND), vm(TOK, ND), vm(TOK, XW), vm(TOK, XW),
    vm(16, 5, 8, ND), vm(8, 5, 8, ND), vm(8, 5, 8, ND),
    vm(8, 5, 8, ND), vm(8, 5, 8, ND), vm(5, 8, ND), vm(4, 5, 8, ND),
    vm(8, 4, 8, ND), vm(8, 4, 8, ND), vm(8, 4, 8, ND), vm(16, 4, 8, ND),
    vm(8, TOK), vm(3, 8, TOK),
    dma(5), dma(6), dma(3, 2), dma(3), dma(3), dma(2), dma(7), dma(7),
    dma(8), dma(8), dma(8), dma(2), dma(2), dma(2), dma(2),
    dma(1), dma(1), dma(7), dma(7), dma(3), dma(3), dma(7), dma(7), dma(1), dma(1),
    dma(3), dma(3), dma(2), dma(4), dma(2), dma(2), dma(2), dma(3), dma(3),
]


def on_device(
    ssm_x, ssm_z, ssm_b, ssm_c, step_sizes, a_log, conv_x, conv_b, conv_c, norm_gain,
    queries, keys, values,
):
    spec = pl.BlockSpec(memory_space=pltpu.VMEM)
    anyw = pl.BlockSpec(memory_space=pl.ANY)
    return pl.pallas_call(
        body,
        out_shape=(
            jax.ShapeDtypeStruct((TOK, XW), F32),
            jax.ShapeDtypeStruct((TOK, 256), F32),
        ),
        in_specs=[anyw] * 4 + [spec] * 6 + [anyw] * 3,
        out_specs=(spec, spec),
        scratch_shapes=SCRATCH,
        compiler_params=pltpu.CompilerParams(
            collective_id=0, has_side_effects=True, vmem_limit_bytes=60 * 1024 * 1024
        ),
        name="layer",
    )(
        ssm_x, ssm_z, ssm_b, ssm_c, step_sizes.T, a_log.reshape(1, HEADS), conv_x, conv_b, conv_c,
        norm_gain.reshape(1, XW), queries, keys, values,
    )


def solution(mesh):
    placed = (
        P("ctx", "head"),
        P("ctx", "head"),
        P("ctx", None),
        P("ctx", None),
        P("ctx", "head"),
        P("head"),
        P(None, "head"),
        P(),
        P(),
        P("head"),
        P("ctx", "head"),
        P("ctx", None),
        P("ctx", None),
    )
    return jax.shard_map(
        on_device,
        mesh=mesh,
        in_specs=placed,
        out_specs=(P("ctx", "head"), P("ctx", "head")),
        check_vma=False,
    )
```

```python
import math

import jax
import jax.numpy as jnp
from jax import lax
from jax.experimental import pallas as pl
from jax.experimental.pallas import tpu as pltpu
from jax.sharding import PartitionSpec as P

F32 = jnp.float32
BF16 = jnp.bfloat16
FLOOR = -1e30
MESH = pl.DeviceIdType.MESH
NY, NX, NZ, NC = 4, 4, 8, 2
TOK = 256
SHARD = TOK // NY
E = 128
PD = 64
ND = 256
HEADS = 8
XW = HEADS * PD


def split2(v):
    hi = v.astype(BF16)
    lo = (v - hi.astype(F32)).astype(BF16)
    return hi, lo


def bdot(a, b, ca, cb):
    return lax.dot_general(a, b, (((ca,), (cb,)), ((), ())), preferred_element_type=F32)


def dot3(a, b, ca, cb):
    ah, al = split2(a)
    bh, bl = split2(b)
    return bdot(ah, bh, ca, cb) + (bdot(ah, bl, ca, cb) + bdot(al, bh, ca, cb))


def parts3(v):
    hi = v.astype(BF16).astype(F32)
    mid = (v - hi).astype(BF16).astype(F32)
    low = (v - hi) - mid
    return hi, mid, low


def stack3(v):
    hi, mid, low = parts3(v)
    return jnp.concatenate([hi, mid, low, jnp.zeros_like(v)], axis=0).astype(BF16)


def silu(v):
    return v / (1.0 + jnp.exp(-v))


def body(
    x_ref, z_ref, b_ref, c_ref, dt_ref, alog_ref, wx_ref, wb_ref, wc_ref, gain_ref,
    q_ref, k_ref, v_ref,
    mix_ref, att_ref,
    qown, zv, qbuf, qs, kvbuf, kcat, vcat, acc, mrow, lrow, mlsend, mlrecv, crecv, crelay,
    bias_ref, halo_x, halo_b, halo_c, xp, bp, cp, xc, bc, cc, ybuf, ecum, sst, part, merged,
    rin, pre, tot, xtot, fin, iin, dsend, inc, ss_own, ss_in,
    in_sem, q_send, q_recv, halo_send, halo_recv, kv_sem, z_send, z_recv,
    part_send, part_recv, x_recv, r_send, l_send, fr_send, fl_send,
    sp_send, sp_recv, a2a_send, a2a_recv, xt_send, xt_recv, f_send, f_recv, d_send, d_recv,
    ml_send, ml_rsem, c_send, c_rsem, cr_send, cr_recv, cf_send, ss_send, ss_recv,
):
    h = lax.axis_index("head")
    i = lax.axis_index("ctx")
    c = lax.rem(i, NC)
    z = lax.rem(i // NC, NZ)
    x = i // (NC * NZ)

    def at(xx, zz, c_):
        return (xx * NZ + zz) * NC + c_

    def yid(d):
        return (lax.rem(h + d + NY, NY), i)

    def zid(d):
        return (h, at(x, lax.rem(z + d + NZ, NZ), c))

    def xid(d):
        return (h, at(lax.rem(x + d + NX, NX), z, c))

    mate = (h, i + 1 - 2 * c)

    def rcopy(src, dst, ssem, rsem, dev):
        return pltpu.make_async_remote_copy(
            src_ref=src, dst_ref=dst, send_sem=ssem, recv_sem=rsem,
            device_id=dev, device_id_type=MESH,
        )

    body_rows = pl.ds(8, TOK)

    def load(n):
        src = (q_ref, b_ref, x_ref, c_ref, z_ref)[n]
        dst = (qown, bp.at[body_rows, :], xp.at[body_rows, :], cp.at[body_rows, :], zv)[n]
        return pltpu.make_async_copy(src, dst, in_sem.at[n])

    barrier = pltpu.get_barrier_semaphore()

    def hello(dev):
        pl.semaphore_signal(barrier, inc=1, device_id=dev, device_id_type=MESH)

    for d in range(1, NY):
        hello(yid(d))
    for d in range(1, NZ):
        hello(zid(d))
    for d in range(1, NX):
        hello(xid(d))
    hello(mate)

    @pl.when(i > 0)
    def _():
        hello((h, i - 1))

    @pl.when(i < NX * NZ * NC - 1)
    def _():
        hello((h, i + 1))

    own_a = 2 * x
    mine = pl.ds(c * 256, 256)

    def slot(n):
        return kvbuf.at[2 * x + n // 4, pl.ds(c * 256 + (n % 4) * SHARD, SHARD), :]

    def local_kv():
        ours = pl.ds(h * SHARD, SHARD)
        rows = pl.ds(c * 256, SHARD)
        return (
            pltpu.make_async_copy(k_ref.at[ours, :], kvbuf.at[own_a, rows, pl.ds(0, E)], kv_sem.at[0]),
            pltpu.make_async_copy(v_ref.at[ours, :], kvbuf.at[own_a, rows, pl.ds(E, E)], kv_sem.at[1]),
        )

    for cpy in local_kv():
        cpy.start()
    for n in range(5):
        load(n).start()
    for cpy in local_kv():
        cpy.wait()

    pl.semaphore_wait(
        barrier,
        (NY - 1) + (NZ - 1) + (NX - 1) + 1
        + jnp.where(i > 0, 1, 0) + jnp.where(i < NX * NZ * NC - 1, 1, 0),
    )

    def halo(k, src, dst):
        return rcopy(
            src.at[pl.ds(TOK - 8, 8), :], dst, halo_send.at[k], halo_recv.at[k], (h, i + 1)
        )

    def halos():
        return (halo(0, x_ref, halo_x), halo(1, b_ref, halo_b), halo(2, c_ref, halo_c))

    @pl.when(i < NX * NZ * NC - 1)
    def _():
        for cpy in halos():
            cpy.start()

    far_dir = 2 - 4 * c

    def zcopy(n):
        if n <= 4:
            src, to = slot(0), (1, -1, 2, -2)[n - 1]
        elif n < 7:
            src, to = slot(n - 2), (1, -1)[n - 5]
        else:
            src, to = slot(3 + c), far_dir
        return rcopy(src, slot(n), z_send.at[n - 1], z_recv.at[n - 1], zid(to))

    for n in range(1, 5):
        zcopy(n).start()

    def qhalf(ref, k):
        return ref.at[pl.ds(k * 128, 128), :]

    def q_up(k):
        return rcopy(qhalf(q_ref, k), qbuf.at[0, pl.ds(k * 128, 128), :], q_send.at[k], q_recv.at[0, k], yid(1))

    def q_down(k):
        return rcopy(qhalf(q_ref, k), qbuf.at[1, pl.ds(k * 128, 128), :], q_send.at[2 + k], q_recv.at[1, k], yid(-1))

    def q_relay_up():
        return rcopy(qbuf.at[0, pl.ds(0, 128), :], qbuf.at[2, pl.ds(0, 128), :], q_send.at[4], q_recv.at[2, 0], yid(1))

    def q_relay_down():
        return rcopy(qbuf.at[1, pl.ds(128, 128), :], qbuf.at[2, pl.ds(128, 128), :], q_send.at[5], q_recv.at[2, 1], yid(-1))

    q_up(0).start()
    q_down(1).start()
    q_up(1).start()
    q_down(0).start()

    acc[...] = jnp.zeros_like(acc)
    lrow[...] = jnp.zeros_like(lrow)
    mrow[...] = jnp.full(mrow.shape, FLOOR, F32)

    qscale = math.log2(math.e) / math.sqrt(E)

    def load_q(g, src):
        for a in range(2):
            hi, lo = split2(src[:, a * E : (a + 1) * E] * qscale)
            qs[g, pl.ds(a * 256, 256), 0:128] = hi
            qs[g, pl.ds(a * 256, 256), 128:256] = lo
            qs[g, pl.ds(a * 256, 256), 256:384] = hi

    load(0).wait()
    load_q(0, qown[...])

    for hb in range(2):
        kidx = lax.broadcasted_iota(jnp.int32, (1, 512), 1)
        n = hb * 4 + lax.rem(kidx // SHARD, 4)
        rho = jnp.where(lax.rem(n, 2) == 1, -((n + 1) // 2), n // 2)
        kz = lax.rem(z + rho + NZ, NZ)
        kpos = at(x, kz, kidx // 256) * TOK + h * SHARD + lax.rem(kidx, SHARD)
        qpos = i * TOK + lax.broadcasted_iota(jnp.int32, (TOK, 512), 0)
        bias_ref[hb] = jnp.where(kpos <= qpos, 0.0, FLOOR)

    for n in range(1, 5):
        load(n).wait()

    @pl.when(i > 0)
    def _():
        for cpy in halos():
            cpy.wait_recv()
        xp[0:8, :] = halo_x[...]
        bp[0:8, :] = halo_b[...]
        cp[0:8, :] = halo_c[...]

    @pl.when(i == 0)
    def _():
        xp[0:8, :] = jnp.zeros((8, XW), F32)
        bp[0:8, :] = jnp.zeros((8, ND), F32)
        cp[0:8, :] = jnp.zeros((8, ND), F32)

    def conv(pad, w_ref):
        total = w_ref[0:1, :] * pad[pl.ds(5, TOK), :]
        for k in range(1, 4):
            total = total + w_ref[k : k + 1, :] * pad[pl.ds(5 + k, TOK), :]
        return silu(total)

    bc[...] = conv(bp, wb_ref)
    xc[...] = conv(xp, wx_ref)

    row_t = lax.broadcasted_iota(jnp.int32, (TOK, TOK), 0)
    col_t = lax.broadcasted_iota(jnp.int32, (TOK, TOK), 1)
    upper = jnp.where(row_t <= col_t, 1.0, 0.0).astype(BF16)
    eye = jnp.where(col_t == row_t, 1.0, 0.0).astype(BF16)
    spread_h = lax.broadcasted_iota(jnp.int32, (32, XW), 0)
    spread_c = lax.broadcasted_iota(jnp.int32, (32, XW), 1)
    expand = jnp.where(
        jnp.logical_and(spread_c // PD == spread_h % HEADS, spread_h < 3 * HEADS), 1.0, 0.0
    ).astype(BF16)

    def widen(rows):
        return bdot(stack3(rows), expand, 0, 0)

    head_r = lax.broadcasted_iota(jnp.int32, (HEADS, HEADS), 0)
    head_c = lax.broadcasted_iota(jnp.int32, (HEADS, HEADS), 1)
    rate = -jnp.exp(alog_ref[...])
    rate = jnp.sum(jnp.where(head_r == head_c, rate, 0.0), axis=1, keepdims=True)
    dt = dt_ref[...]
    c3 = bdot(stack3(dt * rate), upper, 1, 0)
    cum_t = c3[0:8] + c3[8:16] + c3[16:24]
    c3 = bdot(eye, stack3(cum_t), 1, 1)
    cum = c3[:, 0:8] + c3[:, 8:16] + c3[:, 16:24]
    towards = jnp.exp(cum_t[:, TOK - 1 : TOK] - cum_t) * dt
    own = dot3(xc[...] * widen(towards), bc[...], 0, 0)
    sst[:, 0:4, :, :] = own.reshape(16, 4, 8, ND)
    growth = jnp.broadcast_to(jnp.exp(cum_t[:, TOK - 1 : TOK]), (HEADS, ND))
    for hh in range(HEADS):
        g8 = jnp.broadcast_to(growth[hh : hh + 1, :], (8, ND))
        sst[2 * hh, 4, :, :] = g8
        sst[2 * hh + 1, 4, :, :] = g8

    def to_mate():
        return rcopy(sst.at[pl.ds(8 * (1 - c), 8)], part, sp_send.at[0], sp_recv.at[0], mate)

    to_mate().start()

    q_up(0).wait_recv()
    q_relay_up().start()
    q_down(1).wait_recv()
    q_relay_down().start()

    def kvrows(blk):
        return kvbuf.at[blk, mine, :]

    def share(blk):
        return rcopy(kvrows(blk), kvrows(blk), part_send.at[blk], part_recv.at[blk], mate)

    def right(hb, blk, sem):
        return rcopy(kvrows(blk), kvrows(blk), sem.at[hb], x_recv.at[blk], xid(1))

    def left(hb, blk, sem):
        return rcopy(kvrows(blk), kvrows(blk), sem.at[hb], x_recv.at[blk], xid(-1))

    goes_left = jnp.logical_or(x == 0, jnp.logical_and(x == 1, c == 1))

    def ready(hb):
        blk = 2 * x + hb

        @pl.when(x < NX - 1)
        def _():
            right(hb, blk, r_send).start()

        @pl.when(goes_left)
        def _():
            left(hb, blk, l_send).start()

        share(blk).start()

    for n in range(1, 4):
        zcopy(n).wait_recv()
    ready(0)
    zcopy(5).start()
    zcopy(4).wait_recv()
    zcopy(6).start()
    zcopy(7).start()

    cc[...] = conv(cp, wc_ref)
    inter = dot3(cc[...], bc[...], 1, 1)
    dt_x = widen(dt)
    ecum[...] = widen(jnp.exp(cum_t))
    causal = col_t <= row_t
    first = lax.broadcasted_iota(jnp.int32, (TOK, 128), 1) < PD
    def inside(pair):
        lanes = pl.ds(pair * 128, 128)
        xd = xc[:, pair * 128 : (pair + 1) * 128] * dt_x[:, pair * 128 : (pair + 1) * 128]
        xd = jnp.concatenate(split2(xd), axis=1)
        outs = []
        for k in range(2):
            hh = 2 * pair + k
            gap = cum[:, hh : hh + 1] - cum_t[hh : hh + 1, :]
            mixing = inter * jnp.where(causal, jnp.exp(jnp.minimum(gap, 0.0)), 0.0)
            both = bdot(jnp.concatenate(split2(mixing), axis=0), xd, 1, 0)
            both = both[0:TOK] + both[TOK : 2 * TOK]
            outs.append(both[:, 0:128] + both[:, 128:256])
        ybuf[:, lanes] = jnp.where(first, outs[0], outs[1])

    inside(0)
    inside(1)

    to_mate().wait_recv()
    whole = pl.ds(8 * c, 8)
    mine_s = sst[whole]
    theirs = part[...]
    g_mine, g_theirs = mine_s[:, 4:5], theirs[:, 4:5]
    chip = jnp.where(
        c == 0, g_theirs * mine_s[:, 0:4] + theirs[:, 0:4], g_mine * theirs[:, 0:4] + mine_s[:, 0:4]
    )
    merged[:, 0:4] = chip
    merged[:, 4:5] = g_mine * g_theirs

    def to_owner(d):
        k = lax.rem(z + d, NZ)
        return rcopy(merged.at[k], rin.at[z], a2a_send.at[d - 1], a2a_recv.at[d - 1], zid(d))

    def from_peer(d):
        return rcopy(merged.at[z], rin.at[lax.rem(z + NZ - d, NZ)], a2a_send.at[d - 1], a2a_recv.at[d - 1], zid(d))

    for d in (4, 3, 5, 2, 6, 1, 7):
        to_owner(d).start()
    rin[z] = merged[z]

    def convert(blk):
        kv = kvbuf[blk]
        hi, lo = split2(kv[:, 0:E])
        kcat[blk, :, 0:128] = hi
        kcat[blk, :, 128:256] = hi
        kcat[blk, :, 256:384] = lo
        hi, lo = split2(kv[:, E : 2 * E])
        vcat[blk, :, 0:128] = hi
        vcat[blk, :, 128:256] = lo

    def attend(g, blk, hb):
        s = bdot(qs[g], kcat[blk], 1, 1)
        if hb is not None:
            bias = bias_ref[hb]
            s = s + jnp.concatenate([bias, bias], axis=0)
        m_old = mrow[g]
        m_new = jnp.maximum(m_old, jnp.max(s, axis=1, keepdims=True))
        alpha = jnp.exp2(m_old - m_new)
        p = jnp.exp2(s - jnp.concatenate([m_new] * 4, axis=1))
        lrow[g] = lrow[g] * alpha + ((p[:, 0:128] + p[:, 128:256]) + (p[:, 256:384] + p[:, 384:512]))
        o = bdot(jnp.concatenate(split2(p), axis=0), vcat[blk], 1, 0)
        o = o[0:512] + o[512:1024]
        acc[g] = acc[g] * alpha + (o[:, 0:128] + o[:, 128:256])
        mrow[g] = m_new

    def got(blk):
        return right(0, blk, fr_send)

    def relay(hb):
        @pl.when(jnp.logical_and(x == 0, c == 1))
        def _():
            got(2 + hb).wait_recv()
            left(hb, 2 + hb, fl_send).start()

    def turn_of(k):
        u3 = jnp.where(k < 4, 2 * lax.rem(k, 2), 1)
        hb3 = jnp.where(k < 4, k // 2, k - 4)
        u = jnp.where(x == 3, u3, jnp.where(x == 2, 1 - k // 2, 0))
        return u, jnp.where(x == 3, hb3, lax.rem(k, 2))

    def block_of(k):
        u, hb = turn_of(k)
        return 2 * u + hb

    def arrive(k):
        u, hb = turn_of(k)
        blk = 2 * u + hb
        got(blk).wait_recv()

        @pl.when(jnp.logical_and(x == 3, u == 0))
        def _():
            left(hb, blk, fl_send).start()

        @pl.when(jnp.logical_and(jnp.logical_and(x == 2, u == 1), c == 0))
        def _():
            right(hb, blk, fr_send).start()

        share(blk).start()

    inside(2)
    inside(3)
    share(2 * x).wait_recv()
    convert(2 * x)
    attend(0, 2 * x, 0)
    q_up(1).wait_recv()
    load_q(1, qbuf[0])
    attend(1, 2 * x, 0)
    for n in range(5, 8):
        zcopy(n).wait_recv()
    ready(1)
    q_down(0).wait_recv()
    load_q(2, qbuf[1])
    attend(2, 2 * x, 0)

    relay(0)
    q_relay_up().wait_recv()
    q_relay_down().wait_recv()
    load_q(3, qbuf[2])
    attend(3, 2 * x, 0)

    @pl.when(x >= 1)
    def _():
        arrive(0)

    share(2 * x + 1).wait_recv()
    convert(2 * x + 1)

    def own_b(g, carry):
        attend(g, 2 * x + 1, 1)
        return carry

    lax.fori_loop(1, 3, own_b, 0)
    relay(1)

    @pl.when(x >= 1)
    def _():
        arrive(1)

    attend(3, 2 * x + 1, 1)

    for d in range(1, NZ):
        from_peer(d).wait_recv()
    run = jnp.zeros((4, 8, ND), F32)
    gprod = jnp.ones((1, 8, ND), F32)
    for zz in range(NZ):
        pre[zz, 0:4] = run
        pre[zz, 4:5] = gprod
        gz = rin[zz, 4:5]
        run = gz * run + rin[zz, 0:4]
        gprod = gprod * gz
    tot[0:4] = run
    tot[4:5] = gprod

    def to_x(d):
        return rcopy(tot, xtot.at[x], xt_send.at[d - 1], xt_recv.at[d - 1], (h, at(x + d, z, c)))

    def from_x(d):
        return rcopy(tot, xtot.at[x - d], xt_send.at[d - 1], xt_recv.at[d - 1], (h, at(x - d, z, c)))

    for d in range(1, NX):

        @pl.when(x + d < NX)
        def _():
            to_x(d).start()

    def to_block(d):
        k = lax.rem(z + d, NZ)
        return rcopy(fin.at[k], iin.at[z], f_send.at[d - 1], f_recv.at[d - 1], zid(d))

    def from_owner(d):
        return rcopy(fin.at[z], iin.at[lax.rem(z + NZ - d, NZ)], f_send.at[d - 1], f_recv.at[d - 1], zid(d))

    def hand_back():
        for d in range(1, NX):

            @pl.when(x >= d)
            def _():
                from_x(d).wait_recv()

        before = jnp.zeros((4, 8, ND), F32)
        for xs in range(NX - 1):
            before = jnp.where(xs < x, xtot[xs, 4:5] * before + xtot[xs, 0:4], before)
        for zz in range(NZ):
            fin[zz] = pre[zz, 0:4] + pre[zz, 4:5] * before

        for d in (4, 3, 5, 2, 6, 1, 7):
            to_block(d).start()
        iin[z] = fin[z]


    def other(k, carry):
        blk = block_of(k)
        share(blk).wait_recv()
        convert(blk)

        def step(g, inner):
            attend(g, blk, None)
            return inner

        lax.fori_loop(1, 3, step, 0)
        arrive(k + 2)
        attend(3, blk, None)

        @pl.when(k == 0)
        def _():
            hand_back()

        return carry

    lax.fori_loop(0, jnp.maximum(2 * x - 2, 0), other, 0)

    @pl.when(x < 2)
    def _():
        hand_back()

    @pl.when(x >= 1)
    def _():
        for k in (2 * x - 2, 2 * x - 1):
            blk = block_of(k)
            share(blk).wait_recv()
            convert(blk)

    def last_unit(g):
        @pl.when(x >= 1)
        def _():
            def step(k, carry):
                attend(g, block_of(k), None)
                return carry

            lax.fori_loop(2 * x - 2, 2 * x, step, 0)

    pick_r = lax.broadcasted_iota(jnp.int32, (8, 128), 0)
    pick = jnp.where(pick_r == lax.broadcasted_iota(jnp.int32, (8, 128), 1), 1.0, 0.0).astype(BF16)

    def sums(g):
        return jnp.sum(lrow[g], axis=1, keepdims=True)

    def turn(cols):
        rows = cols[0].shape[0]
        lane = lax.broadcasted_iota(jnp.int32, (rows, 128), 1)
        laid = jnp.zeros((rows, 128), F32)
        for k, col in enumerate(cols):
            for n, part_ in enumerate(parts3(col)):
                laid = jnp.where(lane == 3 * k + n, part_, laid)
        return bdot(pick, laid.astype(BF16), 1, 1)

    def pack_ml(g):
        mlsend[g - 1] = turn([mrow[g], jnp.broadcast_to(sums(g), (512, 128))])

    def ml_copy(g):
        k = g - 1
        return rcopy(mlsend.at[k], mlrecv.at[k], ml_send.at[k], ml_rsem.at[k], yid((-1, 1, 2)[k]))

    def acc_copy(g):
        k = g - 1
        return rcopy(acc.at[g], crecv.at[k], c_send.at[k], c_rsem.at[k], yid((-1, 1)[k]))

    def acc_far(k):
        return rcopy(acc.at[3, pl.ds(k * 256, 256), :], crelay.at[k], cr_send.at[k], cr_recv.at[k], yid((1, -1)[k]))

    def acc_far_on(k):
        return rcopy(crelay.at[k], crecv.at[2, pl.ds(k * 256, 256), :], cf_send.at[k], c_rsem.at[2 + k], yid((1, -1)[k]))

    last_unit(3)
    pack_ml(3)
    acc_far(0).start()
    acc_far(1).start()
    ml_copy(3).start()
    last_unit(1)
    pack_ml(1)
    acc_copy(1).start()
    ml_copy(1).start()
    for d in range(1, NZ):
        from_owner(d).wait_recv()
    chip_in = iin[...]
    mine_s = sst[whole]
    theirs = part[...]
    second = jnp.where(c == 0, mine_s[:, 4:5], theirs[:, 4:5]) * chip_in + jnp.where(
        c == 0, mine_s[:, 0:4], theirs[:, 0:4]
    )
    dsend[...] = jnp.where(c == 0, second, chip_in)
    inc[whole] = jnp.where(c == 0, chip_in, second)

    def to_mate_in():
        return rcopy(dsend, inc.at[whole], d_send.at[0], d_recv.at[0], mate)

    to_mate_in().start()

    last_unit(2)
    pack_ml(2)
    acc_copy(2).start()
    ml_copy(2).start()
    def own_group(k, none):
        attend(0, block_of(k), None)
        return none

    attend(0, 2 * x + 1, 1)
    lax.fori_loop(0, x, own_group, 0)
    for k in range(2):
        acc_far(k).wait_recv()
        acc_far_on(k).start()

    to_mate_in().wait_recv()
    carried = dot3(cc[...], inc[...].reshape(XW, ND), 1, 1)
    gated = (ybuf[...] + ecum[...] * carried) * silu(zv[...])
    ybuf[...] = gated
    sq = gated * gated
    sq = (sq[:, 0:128] + sq[:, 128:256]) + (sq[:, 256:384] + sq[:, 384:512])
    ss_own[...] = turn([jnp.broadcast_to(jnp.sum(sq, axis=1, keepdims=True), (TOK, 128))])

    def ss_copy(d):
        return rcopy(ss_own, ss_in.at[d - 1], ss_send.at[d - 1], ss_recv.at[d - 1], yid(d))

    for d in range(1, NY):
        ss_copy(d).start()

    lax.fori_loop(x, 2 * x, own_group, 0)

    for k in range(3):
        ml_copy(k + 1).wait_recv()
    ms = [mrow[0]]
    ls = [jnp.broadcast_to(sums(0), (512, 128))]
    back_r = lax.broadcasted_iota(jnp.int32, (8, 256), 0)
    back_c = lax.broadcasted_iota(jnp.int32, (8, 256), 1)
    back = jnp.where(back_r // 3 == back_c // 128, 1.0, 0.0).astype(BF16)
    for k in range(3):
        col = bdot(mlrecv[k].astype(BF16), back, 0, 0)
        ms.append(col[:, 0:128])
        ls.append(col[:, 128:256])
    top = jnp.maximum(jnp.maximum(ms[0], ms[1]), jnp.maximum(ms[2], ms[3]))
    ws = [jnp.exp2(m - top) for m in ms]
    den = ws[0] * ls[0] + ws[1] * ls[1] + ws[2] * ls[2] + ws[3] * ls[3]
    inv = 1.0 / den
    acc_copy(1).wait_recv()
    acc_copy(2).wait_recv()
    for k in range(2):
        acc_far_on(k).wait_recv()
    joined = acc[0] * (ws[0] * inv)
    for k in range(3):
        joined = joined + crecv[k] * (ws[k + 1] * inv)
    att_ref[:, 0:128] = joined[0:256]
    att_ref[:, 128:256] = joined[256:512]

    for d in range(1, NY):
        ss_copy(d).wait_recv()
    ss = jnp.concatenate([ss_own[...], ss_in[0], ss_in[1], ss_in[2]], axis=0).astype(BF16)
    every = jnp.where(lax.rem(lax.broadcasted_iota(jnp.int32, (32, 128), 0), 8) < 3, 1.0, 0.0).astype(BF16)
    strength = bdot(ss, every, 0, 0) / (XW * NY)
    strength = lax.rsqrt(strength + 1e-05)
    mix_ref[...] = ybuf[...] * jnp.concatenate([strength] * 4, axis=1) * gain_ref[...]

    @pl.when(i < NX * NZ * NC - 1)
    def _():
        for cpy in halos():
            cpy.wait_send()

    for n in range(1, 8):
        zcopy(n).wait_send()
    for k in range(2):
        q_up(k).wait_send()
        q_down(k).wait_send()
    q_relay_up().wait_send()
    q_relay_down().wait_send()
    to_mate().wait_send()
    for hb in range(2):
        share(2 * x + hb).wait_send()

        @pl.when(x < NX - 1)
        def _():
            right(hb, 2 * x + hb, r_send).wait_send()

        @pl.when(goes_left)
        def _():
            left(hb, 2 * x + hb, l_send).wait_send()

        for u in range(NX - 1):

            @pl.when(u < x)
            def _():
                share(2 * u + hb).wait_send()

        @pl.when(jnp.logical_or(x == 3, jnp.logical_and(x == 0, c == 1)))
        def _():
            left(hb, 2 + hb, fl_send).wait_send()

        @pl.when(jnp.logical_and(x == 2, c == 0))
        def _():
            right(hb, 2 + hb, fr_send).wait_send()

    for d in range(1, NZ):
        to_owner(d).wait_send()
        to_block(d).wait_send()
    for d in range(1, NX):

        @pl.when(x + d < NX)
        def _():
            to_x(d).wait_send()

    to_mate_in().wait_send()
    for g in range(1, 4):
        ml_copy(g).wait_send()
    for k in range(2):
        acc_copy(k + 1).wait_send()
        acc_far(k).wait_send()
        acc_far_on(k).wait_send()
    for d in range(1, NY):
        ss_copy(d).wait_send()


def vm(*shape, dtype=F32):
    return pltpu.VMEM(shape, dtype)


def dma(*shape):
    return pltpu.SemaphoreType.DMA(shape)


SCRATCH = [
    vm(256, 256), vm(TOK, XW), vm(3, 256, 256), vm(4, 512, 384, dtype=BF16), vm(8, 512, 256),
    vm(8, 512, 384, dtype=BF16), vm(8, 512, 256, dtype=BF16),
    vm(4, 512, 128), vm(4, 512, 128), vm(4, 512, 128),
    vm(3, 8, 512), vm(3, 8, 512), vm(3, 512, 128), vm(2, 256, 128),
    vm(2, TOK, 512), vm(8, XW), vm(8, ND), vm(8, ND), vm(TOK + 8, XW), vm(TOK + 8, ND), vm(TOK + 8, ND),
    vm(TOK, XW), vm(TOK, ND), vm(TOK, ND), vm(TOK, XW), vm(TOK, XW),
    vm(16, 5, 8, ND), vm(8, 5, 8, ND), vm(8, 5, 8, ND),
    vm(8, 5, 8, ND), vm(8, 5, 8, ND), vm(5, 8, ND), vm(4, 5, 8, ND),
    vm(8, 4, 8, ND), vm(8, 4, 8, ND), vm(8, 4, 8, ND), vm(16, 4, 8, ND),
    vm(8, TOK), vm(3, 8, TOK),
    dma(5), dma(6), dma(3, 2), dma(3), dma(3), dma(2), dma(7), dma(7),
    dma(8), dma(8), dma(8), dma(2), dma(2), dma(2), dma(2),
    dma(1), dma(1), dma(7), dma(7), dma(3), dma(3), dma(7), dma(7), dma(1), dma(1),
    dma(3), dma(3), dma(2), dma(4), dma(2), dma(2), dma(2), dma(3), dma(3),
]


def on_device(
    ssm_x, ssm_z, ssm_b, ssm_c, step_sizes, a_log, conv_x, conv_b, conv_c, norm_gain,
    queries, keys, values,
):
    spec = pl.BlockSpec(memory_space=pltpu.VMEM)
    anyw = pl.BlockSpec(memory_space=pl.ANY)
    return pl.pallas_call(
        body,
        out_shape=(
            jax.ShapeDtypeStruct((TOK, XW), F32),
            jax.ShapeDtypeStruct((TOK, 256), F32),
        ),
        in_specs=[anyw] * 4 + [spec] * 6 + [anyw] * 3,
        out_specs=(spec, spec),
        scratch_shapes=SCRATCH,
        compiler_params=pltpu.CompilerParams(
            collective_id=0, has_side_effects=True, vmem_limit_bytes=60 * 1024 * 1024
        ),
        name="layer",
    )(
        ssm_x, ssm_z, ssm_b, ssm_c, step_sizes.T, a_log.reshape(1, HEADS), conv_x, conv_b, conv_c,
        norm_gain.reshape(1, XW), queries, keys, values,
    )


def solution(mesh):
    placed = (
        P("ctx", "head"),
        P("ctx", "head"),
        P("ctx", None),
        P("ctx", None),
        P("ctx", "head"),
        P("head"),
        P(None, "head"),
        P(),
        P(),
        P("head"),
        P("ctx", "head"),
        P("ctx", None),
        P("ctx", None),
    )
    return jax.shard_map(
        on_device,
        mesh=mesh,
        in_specs=placed,
        out_specs=(P("ctx", "head"), P("ctx", "head")),
        check_vma=False,
    )
```
